256 devices in a mesh: row: 16 (over x_lo, y, core), col: 16 (over z, x_hi).
Axes of the slice: x: 4 (x_hi: 2, x_lo: 2; x = x_hi * 2 + x_lo), y: 4, z: 8, core: 2. Of those that a mesh axis runs over, the one named last changes fastest.
Arguments:
- green: bfloat16 [32768, 32768], P('row', 'col'), may hold values from -0.046875 to 0.046875
- mask: int32 [128, 128], P('row', 'col'), may hold values from 0 to 1, as said below
- probes: bfloat16 [32768, 256], P('col', 'row'), may hold values from -6 to 6
Outputs:
- sketch: float32 [32768, 256], P('row', 'col')
- adjoint: float32 [32768, 256], P('col', 'row')
The draws below stay inside these ranges and needn't reach their ends.
Inputs may be any that keep to these rules, and one draw needn't show every extreme that they name: `mask`: block row i belongs to gauge i % 6 and time block i // 6; block column j to window j // 8. A block is 1 when its time block is no earlier than the window's onset plus a travel delay of its gauge and subfault block.
All inputs are finite; a program needn't handle non-finite values.
Results may differ from the reference program's by a relative error of at most 0.0022.
Values may be sent and summed in bfloat16 or wider, within the bound.
A program may use at most 128 MiB of HBM per device.

```python
import jax
import jax.numpy as jnp
from jax import lax

K = 256
SUBFAULTS = 2048
GAUGES = 6
BLK = 256
ROWS = 32768
WINDOWS = 16
COLS = 32768
RBLOCKS = 128
CBLOCKS = 128
TBLOCKS = 21


def draw_mask(key, part):
    per_window = SUBFAULTS // BLK
    travel = jax.random.randint(key, (GAUGES, per_window), 0, max(2, TBLOCKS // 4 + 1))
    travel = travel.at[0, 0].set(1)
    rows_idx = jnp.arange(RBLOCKS)
    gauge = rows_idx % GAUGES
    tblock = rows_idx // GAUGES
    cols_idx = jnp.arange(CBLOCKS)
    window = cols_idx // per_window
    subblock = cols_idx % per_window
    onset = window * TBLOCKS // (2 * WINDOWS)
    delay = travel[gauge][:, subblock]
    return (tblock[:, None] >= onset[None, :] + delay).astype(jnp.int32)


def shard_levels(own_key, shape, shards, least, top_value):
    factor_of, own = 1.0, jax.random.fold_in(own_key, 6)
    for position, blocks in shards:
        draws = jnp.exp(jax.random.uniform(jax.random.fold_in(own, position), (blocks,), jnp.float32, least / len(shards), top_value / len(shards)))
        factor_of = factor_of * jnp.repeat(draws, shape[position] // blocks).reshape([-1 if axis == position else 1 for axis in range(len(shape))])
    return factor_of


def normal_values(own_key, extent, width, most, pieces=(), kind=jnp.bfloat16):
    loudness = shard_levels(own_key, extent, pieces, -0.22, 0.18) if pieces else 1.0
    result = jax.random.normal(own_key, extent, jnp.float32) * width * loudness
    return jnp.minimum(jnp.maximum(result, -most), most).astype(kind)


def setup_inputs(seed: int = 0) -> dict:
    keys = jax.random.split(jax.random.key(seed), 4)
    return {
        "green": normal_values(keys[0], (ROWS, COLS), (COLS // 2) ** -0.5, 0.046875, ((0, 16), (1, 16))),
        "mask": draw_mask(jax.random.fold_in(keys[3], 71), 0),
        "probes": normal_values(keys[2], (COLS, K), 1.0, 6.0, ((0, 16), (1, 16))),
    }


def reference(green, mask, probes):
    shaped = green.reshape(RBLOCKS, BLK, CBLOCKS, BLK)
    tiles = (shaped * mask.astype(jnp.bfloat16)[:, None, :, None]).reshape(ROWS, COLS)
    sketch = jnp.dot(tiles, probes, preferred_element_type=jnp.float32)
    lowered = sketch.astype(jnp.bfloat16)
    adjoint = lax.dot_general(tiles, lowered, (((0,), (0,)), ((), ())), preferred_element_type=jnp.float32)
    return sketch, adjoint
```

```python
import jax
import jax.numpy as jnp
from jax import lax
from jax.sharding import PartitionSpec as P


def local(green, mask, probes):
    row_blocks, col_blocks = mask.shape
    block_size = green.shape[0] // row_blocks
    shaped = green.reshape(row_blocks, block_size, col_blocks, block_size)
    tiles = (shaped * mask.astype(jnp.bfloat16)[:, None, :, None]).reshape(green.shape)
    all_probes = lax.all_gather(probes, "row", axis=1, tiled=True)
    partial_sketch = jnp.dot(tiles, all_probes, preferred_element_type=jnp.float32)
    own_sketch = lax.psum_scatter(partial_sketch, "col", scatter_dimension=1, tiled=True)
    lowered = lax.all_gather(own_sketch.astype(jnp.bfloat16), "col", axis=1, tiled=True)
    term_t = lax.dot_general(
        lowered,
        tiles,
        (((0,), (0,)), ((), ())),
        preferred_element_type=jnp.float32,
    )
    adjoint_t = lax.psum_scatter(term_t, "row", scatter_dimension=0, tiled=True)
    return (own_sketch, adjoint_t.T)


def solution(mesh):
    in_specs = (P("row", "col"), P("row", "col"), P("col", "row"))
    out_specs = (P("row", "col"), P("col", "row"))
    return jax.shard_map(local, mesh=mesh, in_specs=in_specs, out_specs=out_specs, check_vma=False)
```

```python
import functools

import jax
import jax.numpy as jnp
from jax import lax
from jax.experimental import pallas as pl
from jax.experimental.pallas import tpu as pltpu
from jax.sharding import PartitionSpec as P

MESH = pl.DeviceIdType.MESH


def _peer(axis, other, p):
    return (other, p) if axis == "col" else (p, other)


def _greet(axis, other, me, n):
    barrier = pltpu.get_barrier_semaphore()
    for d in range(1, n):
        peer = _peer(axis, other, lax.rem(me + d, n))
        pl.semaphore_signal(barrier, 1, device_id=peer, device_id_type=MESH)
    pl.semaphore_wait(barrier, n - 1)


def _rs_kernel(axis, other_axis, n, x_ref, o_ref, recv, send_sem, recv_sem):
    me = lax.axis_index(axis)
    other = lax.axis_index(other_axis)
    _greet(axis, other, me, n)
    copies = []
    for d in range(1, n):
        peer = lax.rem(me + d, n)
        copy = pltpu.make_async_remote_copy(
            src_ref=x_ref.at[peer],
            dst_ref=recv.at[d - 1],
            send_sem=send_sem.at[d - 1],
            recv_sem=recv_sem.at[d - 1],
            device_id=_peer(axis, other, peer),
            device_id_type=MESH,
        )
        copy.start()
        copies.append(copy)
    acc = x_ref[me]
    for d, copy in enumerate(copies):
        copy.wait_recv()
        acc = acc + recv[d]
    for copy in copies:
        copy.wait_send()
    o_ref[...] = acc


def _ag_kernel(axis, other_axis, n, x_ref, o_ref, recv, send_sem, recv_sem):
    me = lax.axis_index(axis)
    other = lax.axis_index(other_axis)
    _greet(axis, other, me, n)
    copies = []
    for d in range(1, n):
        peer = lax.rem(me + d, n)
        copy = pltpu.make_async_remote_copy(
            src_ref=x_ref,
            dst_ref=recv.at[d - 1],
            send_sem=send_sem.at[d - 1],
            recv_sem=recv_sem.at[d - 1],
            device_id=_peer(axis, other, peer),
            device_id_type=MESH,
        )
        copy.start()
        copies.append(copy)
    o_ref[me] = x_ref[...]
    for d, copy in enumerate(copies):
        copy.wait_recv()
        o_ref[lax.rem(me + n - 1 - d, n)] = recv[d]
    for copy in copies:
        copy.wait_send()


def _reduce_scatter(x, axis, other_axis, collective_id):
    n, rows, width = x.shape
    return pl.pallas_call(
        functools.partial(_rs_kernel, axis, other_axis, n),
        out_shape=jax.ShapeDtypeStruct((rows, width), x.dtype),
        in_specs=[pl.BlockSpec(memory_space=pltpu.VMEM)],
        out_specs=pl.BlockSpec(memory_space=pltpu.VMEM),
        scratch_shapes=[
            pltpu.VMEM((n - 1, rows, width), x.dtype),
            pltpu.SemaphoreType.DMA((n - 1,)),
            pltpu.SemaphoreType.DMA((n - 1,)),
        ],
        compiler_params=pltpu.CompilerParams(collective_id=collective_id, has_side_effects=True),
    )(x)


def _all_gather(x, axis, other_axis, n, collective_id):
    rows, width = x.shape
    return pl.pallas_call(
        functools.partial(_ag_kernel, axis, other_axis, n),
        out_shape=jax.ShapeDtypeStruct((n, rows, width), x.dtype),
        in_specs=[pl.BlockSpec(memory_space=pltpu.VMEM)],
        out_specs=pl.BlockSpec(memory_space=pltpu.VMEM),
        scratch_shapes=[
            pltpu.VMEM((n - 1, rows, width), x.dtype),
            pltpu.SemaphoreType.DMA((n - 1,)),
            pltpu.SemaphoreType.DMA((n - 1,)),
        ],
        compiler_params=pltpu.CompilerParams(collective_id=collective_id, has_side_effects=True),
    )(x)


def local(green, mask, probes):
    n_row = lax.axis_size("row")
    n_col = lax.axis_size("col")
    row_blocks, col_blocks = mask.shape
    block_size = green.shape[0] // row_blocks
    shaped = green.reshape(row_blocks, block_size, col_blocks, block_size)
    tiles = (shaped * mask.astype(jnp.bfloat16)[:, None, :, None]).reshape(green.shape)
    all_probes = lax.all_gather(probes, "row", axis=1, tiled=True)
    k = all_probes.shape[1]
    partial_t = jnp.dot(tiles, all_probes, preferred_element_type=jnp.float32).T
    sketch_t = _reduce_scatter(partial_t.reshape(n_col, k // n_col, -1), "col", "row", 0)
    lowered_t = _all_gather(sketch_t.astype(jnp.bfloat16), "col", "row", n_col, 1).reshape(k, -1)
    term_t = jnp.dot(lowered_t, tiles, preferred_element_type=jnp.float32)
    adjoint_t = _reduce_scatter(term_t.reshape(n_row, k // n_row, -1), "row", "col", 2)
    return (sketch_t.T, adjoint_t.T)


def solution(mesh):
    in_specs = (P("row", "col"), P("row", "col"), P("col", "row"))
    out_specs = (P("row", "col"), P("col", "row"))
    return jax.shard_map(local, mesh=mesh, in_specs=in_specs, out_specs=out_specs, check_vma=False)
```

```python
import functools

import jax
import jax.numpy as jnp
from jax import lax
from jax.experimental import pallas as pl
from jax.experimental.pallas import tpu as pltpu
from jax.sharding import PartitionSpec as P

MESH = pl.DeviceIdType.MESH


def _peer(axis, other, p):
    return (other, p) if axis == "col" else (p, other)


def _greet(axis, other, me, n):
    barrier = pltpu.get_barrier_semaphore()
    for d in range(1, n):
        peer = _peer(axis, other, lax.rem(me + d, n))
        pl.semaphore_signal(barrier, 1, device_id=peer, device_id_type=MESH)
    pl.semaphore_wait(barrier, n - 1)


def _rs_kernel(axis, other_axis, n, x_ref, o_ref, recv, send_sem, recv_sem):
    me = lax.axis_index(axis)
    other = lax.axis_index(other_axis)
    _greet(axis, other, me, n)
    copies = []
    for d in range(1, n):
        peer = lax.rem(me + d, n)
        copy = pltpu.make_async_remote_copy(
            src_ref=x_ref.at[peer],
            dst_ref=recv.at[d - 1],
            send_sem=send_sem.at[d - 1],
            recv_sem=recv_sem.at[d - 1],
            device_id=_peer(axis, other, peer),
            device_id_type=MESH,
        )
        copy.start()
        copies.append(copy)
    acc = x_ref[me]
    for d, copy in enumerate(copies):
        copy.wait_recv()
        acc = acc + recv[d]
    for copy in copies:
        copy.wait_send()
    o_ref[...] = acc


def _ag_kernel(axis, other_axis, n, x_ref, o_ref, recv, send_sem, recv_sem):
    me = lax.axis_index(axis)
    other = lax.axis_index(other_axis)
    _greet(axis, other, me, n)
    copies = []
    for d in range(1, n):
        peer = lax.rem(me + d, n)
        copy = pltpu.make_async_remote_copy(
            src_ref=x_ref,
            dst_ref=recv.at[d - 1],
            send_sem=send_sem.at[d - 1],
            recv_sem=recv_sem.at[d - 1],
            device_id=_peer(axis, other, peer),
            device_id_type=MESH,
        )
        copy.start()
        copies.append(copy)
    o_ref[me] = x_ref[...]
    for d, copy in enumerate(copies):
        copy.wait_recv()
        o_ref[lax.rem(me + n - 1 - d, n)] = recv[d]
    for copy in copies:
        copy.wait_send()


def _reduce_scatter(x, axis, other_axis, collective_id):
    n, rows, width = x.shape
    return pl.pallas_call(
        functools.partial(_rs_kernel, axis, other_axis, n),
        out_shape=jax.ShapeDtypeStruct((rows, width), x.dtype),
        in_specs=[pl.BlockSpec(memory_space=pltpu.VMEM)],
        out_specs=pl.BlockSpec(memory_space=pltpu.VMEM),
        scratch_shapes=[
            pltpu.VMEM((n - 1, rows, width), x.dtype),
            pltpu.SemaphoreType.DMA((n - 1,)),
            pltpu.SemaphoreType.DMA((n - 1,)),
        ],
        compiler_params=pltpu.CompilerParams(collective_id=collective_id, has_side_effects=True),
    )(x)


def _all_gather(x, axis, other_axis, n, collective_id):
    rows, width = x.shape
    return pl.pallas_call(
        functools.partial(_ag_kernel, axis, other_axis, n),
        out_shape=jax.ShapeDtypeStruct((n, rows, width), x.dtype),
        in_specs=[pl.BlockSpec(memory_space=pltpu.VMEM)],
        out_specs=pl.BlockSpec(memory_space=pltpu.VMEM),
        scratch_shapes=[
            pltpu.VMEM((n - 1, rows, width), x.dtype),
            pltpu.SemaphoreType.DMA((n - 1,)),
            pltpu.SemaphoreType.DMA((n - 1,)),
        ],
        compiler_params=pltpu.CompilerParams(collective_id=collective_id, has_side_effects=True),
    )(x)


def _sketch_kernel(nb, bs, mask_ref, g_ref, p_ref, o_ref):
    i = pl.program_id(0)
    o_ref[...] = jnp.zeros_like(o_ref)
    for j in range(nb):
        @pl.when(mask_ref[i, j] != 0)
        def _():
            o_ref[...] += lax.dot_general(
                p_ref[:, j * bs:(j + 1) * bs],
                g_ref[:, j * bs:(j + 1) * bs],
                (((1,), (1,)), ((), ())),
                preferred_element_type=jnp.float32,
            )


def _adjoint_kernel(nb, bs, mask_ref, l_ref, g_ref, o_ref):
    j = pl.program_id(0)
    o_ref[...] = jnp.zeros_like(o_ref)
    for i in range(nb):
        @pl.when(mask_ref[i, j] != 0)
        def _():
            o_ref[...] += jnp.dot(
                l_ref[:, i * bs:(i + 1) * bs],
                g_ref[i * bs:(i + 1) * bs, :],
                preferred_element_type=jnp.float32,
            )


def _sketch_partial(mask, green, probes_t):
    rb, cb = mask.shape
    bs = green.shape[0] // rb
    k = probes_t.shape[0]
    return pl.pallas_call(
        functools.partial(_sketch_kernel, cb, bs),
        out_shape=jax.ShapeDtypeStruct((k, green.shape[0]), jnp.float32),
        grid_spec=pltpu.PrefetchScalarGridSpec(
            num_scalar_prefetch=1,
            grid=(rb,),
            in_specs=[
                pl.BlockSpec((bs, green.shape[1]), lambda i, m: (i, 0)),
                pl.BlockSpec((k, green.shape[1]), lambda i, m: (0, 0)),
            ],
            out_specs=pl.BlockSpec((k, bs), lambda i, m: (0, i)),
        ),
    )(mask, green, probes_t)


def _adjoint_partial(mask, lowered_t, green):
    rb, cb = mask.shape
    bs = green.shape[0] // rb
    k = lowered_t.shape[0]
    return pl.pallas_call(
        functools.partial(_adjoint_kernel, rb, bs),
        out_shape=jax.ShapeDtypeStruct((k, green.shape[1]), jnp.float32),
        grid_spec=pltpu.PrefetchScalarGridSpec(
            num_scalar_prefetch=1,
            grid=(cb,),
            in_specs=[
                pl.BlockSpec((k, green.shape[0]), lambda j, m: (0, 0)),
                pl.BlockSpec((green.shape[0], bs), lambda j, m: (0, j)),
            ],
            out_specs=pl.BlockSpec((k, bs), lambda j, m: (0, j)),
        ),
    )(mask, lowered_t, green)


def local(green, mask, probes):
    n_row = lax.axis_size("row")
    n_col = lax.axis_size("col")
    probes_t = _all_gather(probes.T, "row", "col", n_row, 3)
    k = probes_t.shape[0] * probes_t.shape[1]
    probes_t = probes_t.reshape(k, -1)
    partial_t = _sketch_partial(mask, green, probes_t)
    sketch_t = _reduce_scatter(partial_t.reshape(n_col, k // n_col, -1), "col", "row", 0)
    lowered_t = _all_gather(sketch_t.astype(jnp.bfloat16), "col", "row", n_col, 1).reshape(k, -1)
    term_t = _adjoint_partial(mask, lowered_t, green)
    adjoint_t = _reduce_scatter(term_t.reshape(n_row, k // n_row, -1), "row", "col", 2)
    return (sketch_t.T, adjoint_t.T)


def solution(mesh):
    in_specs = (P("row", "col"), P("row", "col"), P("col", "row"))
    out_specs = (P("row", "col"), P("col", "row"))
    return jax.shard_map(local, mesh=mesh, in_specs=in_specs, out_specs=out_specs, check_vma=False)
```

```python
import functools

import jax
import jax.numpy as jnp
from jax import lax
from jax.experimental import pallas as pl
from jax.experimental.pallas import tpu as pltpu
from jax.sharding import PartitionSpec as P

MESH = pl.DeviceIdType.MESH


def _peer(axis, other, p):
    return (other, p) if axis == "col" else (p, other)


def _greet(axis, other, me, n):
    barrier = pltpu.get_barrier_semaphore()
    for d in range(1, n):
        peer = _peer(axis, other, lax.rem(me + d, n))
        pl.semaphore_signal(barrier, 1, device_id=peer, device_id_type=MESH)
    pl.semaphore_wait(barrier, n - 1)


def _rs_kernel(axis, other_axis, n, x_ref, o_ref, recv, send_sem, recv_sem):
    me = lax.axis_index(axis)
    other = lax.axis_index(other_axis)
    _greet(axis, other, me, n)
    copies = []
    for d in range(1, n):
        peer = lax.rem(me + d, n)
        copy = pltpu.make_async_remote_copy(
            src_ref=x_ref.at[peer],
            dst_ref=recv.at[d - 1],
            send_sem=send_sem.at[d - 1],
            recv_sem=recv_sem.at[d - 1],
            device_id=_peer(axis, other, peer),
            device_id_type=MESH,
        )
        copy.start()
        copies.append(copy)
    acc = x_ref[me]
    for d, copy in enumerate(copies):
        copy.wait_recv()
        acc = acc + recv[d]
    for copy in copies:
        copy.wait_send()
    o_ref[...] = acc


def _ag_kernel(axis, other_axis, n, x_ref, o_ref, recv, send_sem, recv_sem):
    me = lax.axis_index(axis)
    other = lax.axis_index(other_axis)
    _greet(axis, other, me, n)
    copies = []
    for d in range(1, n):
        peer = lax.rem(me + d, n)
        copy = pltpu.make_async_remote_copy(
            src_ref=x_ref,
            dst_ref=recv.at[d - 1],
            send_sem=send_sem.at[d - 1],
            recv_sem=recv_sem.at[d - 1],
            device_id=_peer(axis, other, peer),
            device_id_type=MESH,
        )
        copy.start()
        copies.append(copy)
    o_ref[me] = x_ref[...]
    for d, copy in enumerate(copies):
        copy.wait_recv()
        o_ref[lax.rem(me + n - 1 - d, n)] = recv[d]
    for copy in copies:
        copy.wait_send()


def _reduce_scatter(x, axis, other_axis, collective_id):
    n, rows, width = x.shape
    return pl.pallas_call(
        functools.partial(_rs_kernel, axis, other_axis, n),
        out_shape=jax.ShapeDtypeStruct((rows, width), x.dtype),
        in_specs=[pl.BlockSpec(memory_space=pltpu.VMEM)],
        out_specs=pl.BlockSpec(memory_space=pltpu.VMEM),
        scratch_shapes=[
            pltpu.VMEM((n - 1, rows, width), x.dtype),
            pltpu.SemaphoreType.DMA((n - 1,)),
            pltpu.SemaphoreType.DMA((n - 1,)),
        ],
        compiler_params=pltpu.CompilerParams(collective_id=collective_id, has_side_effects=True),
    )(x)


def _all_gather(x, axis, other_axis, n, collective_id):
    rows, width = x.shape
    return pl.pallas_call(
        functools.partial(_ag_kernel, axis, other_axis, n),
        out_shape=jax.ShapeDtypeStruct((n, rows, width), x.dtype),
        in_specs=[pl.BlockSpec(memory_space=pltpu.VMEM)],
        out_specs=pl.BlockSpec(memory_space=pltpu.VMEM),
        scratch_shapes=[
            pltpu.VMEM((n - 1, rows, width), x.dtype),
            pltpu.SemaphoreType.DMA((n - 1,)),
            pltpu.SemaphoreType.DMA((n - 1,)),
        ],
        compiler_params=pltpu.CompilerParams(collective_id=collective_id, has_side_effects=True),
    )(x)


def _mask_lanes(mask_ref, nb, bs, width, row=None, col=None):
    blk = lax.broadcasted_iota(jnp.int32, (1, width), 1) // bs
    keep = jnp.zeros((1, width), jnp.int32)
    for b in range(nb):
        value = mask_ref[row, b] if col is None else mask_ref[b, col]
        keep = jnp.where(blk == b, value, keep)
    return keep != 0


def _sketch_kernel(nb, bs, mask_ref, g_ref, p_ref, o_ref):
    i = pl.program_id(0)
    keep = _mask_lanes(mask_ref, nb, bs, p_ref.shape[1], row=i)
    p = jnp.where(keep, p_ref[...], jnp.zeros_like(p_ref))
    o_ref[...] = lax.dot_general(
        p, g_ref[...], (((1,), (1,)), ((), ())), preferred_element_type=jnp.float32
    )


def _adjoint_kernel(nb, bs, mask_ref, l_ref, g_ref, o_ref):
    j = pl.program_id(0)
    keep = _mask_lanes(mask_ref, nb, bs, l_ref.shape[1], col=j)
    lowered = jnp.where(keep, l_ref[...], jnp.zeros_like(l_ref))
    o_ref[...] = jnp.dot(lowered, g_ref[...], preferred_element_type=jnp.float32)


def _sketch_partial(mask, green, probes_t):
    rb, cb = mask.shape
    bs = green.shape[0] // rb
    k = probes_t.shape[0]
    return pl.pallas_call(
        functools.partial(_sketch_kernel, cb, bs),
        out_shape=jax.ShapeDtypeStruct((k, green.shape[0]), jnp.float32),
        grid_spec=pltpu.PrefetchScalarGridSpec(
            num_scalar_prefetch=1,
            grid=(rb,),
            in_specs=[
                pl.BlockSpec((bs, green.shape[1]), lambda i, m: (i, 0)),
                pl.BlockSpec((k, green.shape[1]), lambda i, m: (0, 0)),
            ],
            out_specs=pl.BlockSpec((k, bs), lambda i, m: (0, i)),
        ),
    )(mask, green, probes_t)


def _adjoint_partial(mask, lowered_t, green):
    rb, cb = mask.shape
    bs = green.shape[0] // rb
    k = lowered_t.shape[0]
    return pl.pallas_call(
        functools.partial(_adjoint_kernel, rb, bs),
        out_shape=jax.ShapeDtypeStruct((k, green.shape[1]), jnp.float32),
        grid_spec=pltpu.PrefetchScalarGridSpec(
            num_scalar_prefetch=1,
            grid=(cb,),
            in_specs=[
                pl.BlockSpec((k, green.shape[0]), lambda j, m: (0, 0)),
                pl.BlockSpec((green.shape[0], bs), lambda j, m: (0, j)),
            ],
            out_specs=pl.BlockSpec((k, bs), lambda j, m: (0, j)),
        ),
    )(mask, lowered_t, green)


def local(green, mask, probes):
    n_row = lax.axis_size("row")
    n_col = lax.axis_size("col")
    probes_t = _all_gather(probes.T, "row", "col", n_row, 3)
    k = probes_t.shape[0] * probes_t.shape[1]
    probes_t = probes_t.reshape(k, -1)
    partial_t = _sketch_partial(mask, green, probes_t)
    sketch_t = _reduce_scatter(partial_t.reshape(n_col, k // n_col, -1), "col", "row", 0)
    lowered_t = _all_gather(sketch_t.astype(jnp.bfloat16), "col", "row", n_col, 1).reshape(k, -1)
    term_t = _adjoint_partial(mask, lowered_t, green)
    adjoint_t = _reduce_scatter(term_t.reshape(n_row, k // n_row, -1), "row", "col", 2)
    return (sketch_t.T, adjoint_t.T)


def solution(mesh):
    in_specs = (P("row", "col"), P("row", "col"), P("col", "row"))
    out_specs = (P("row", "col"), P("col", "row"))
    return jax.shard_map(local, mesh=mesh, in_specs=in_specs, out_specs=out_specs, check_vma=False)
```

```python
import functools

import jax
import jax.numpy as jnp
from jax import lax
from jax.experimental import pallas as pl
from jax.experimental.pallas import tpu as pltpu
from jax.sharding import PartitionSpec as P

MESH = pl.DeviceIdType.MESH


def _peer(axis, other, p):
    return (other, p) if axis == "col" else (p, other)


def _greet(axis, other, me, n):
    barrier = pltpu.get_barrier_semaphore()
    for d in range(1, n):
        peer = _peer(axis, other, lax.rem(me + d, n))
        pl.semaphore_signal(barrier, 1, device_id=peer, device_id_type=MESH)
    pl.semaphore_wait(barrier, n - 1)


def _rs_kernel(axis, other_axis, n, x_ref, o_ref, recv, send_sem, recv_sem):
    me = lax.axis_index(axis)
    other = lax.axis_index(other_axis)
    _greet(axis, other, me, n)
    copies = []
    for d in range(1, n):
        peer = lax.rem(me + d, n)
        copy = pltpu.make_async_remote_copy(
            src_ref=x_ref.at[peer],
            dst_ref=recv.at[d - 1],
            send_sem=send_sem.at[d - 1],
            recv_sem=recv_sem.at[d - 1],
            device_id=_peer(axis, other, peer),
            device_id_type=MESH,
        )
        copy.start()
        copies.append(copy)
    acc = x_ref[me]
    for d, copy in enumerate(copies):
        copy.wait_recv()
        acc = acc + recv[d]
    for copy in copies:
        copy.wait_send()
    o_ref[...] = acc


def _ag_kernel(axis, other_axis, n, x_ref, o_ref, recv, send_sem, recv_sem):
    me = lax.axis_index(axis)
    other = lax.axis_index(other_axis)
    _greet(axis, other, me, n)
    copies = []
    for d in range(1, n):
        peer = lax.rem(me + d, n)
        copy = pltpu.make_async_remote_copy(
            src_ref=x_ref,
            dst_ref=recv.at[d - 1],
            send_sem=send_sem.at[d - 1],
            recv_sem=recv_sem.at[d - 1],
            device_id=_peer(axis, other, peer),
            device_id_type=MESH,
        )
        copy.start()
        copies.append(copy)
    o_ref[me] = x_ref[...]
    for d, copy in enumerate(copies):
        copy.wait_recv()
        o_ref[lax.rem(me + n - 1 - d, n)] = recv[d]
    for copy in copies:
        copy.wait_send()


def _row_greet(me, other, chips):
    chip, core = me // 2, lax.rem(me, 2)
    barrier = pltpu.get_barrier_semaphore()
    pl.semaphore_signal(barrier, 1, device_id=(chip * 2 + 1 - core, other), device_id_type=MESH)
    for d in range(1, chips):
        peer = lax.rem(chip + d, chips) * 2 + core
        pl.semaphore_signal(barrier, 1, device_id=(peer, other), device_id_type=MESH)
    pl.semaphore_wait(barrier, chips)
    return chip, core


def _row_rs_kernel(chips, x_ref, o_ref, recv1, mid, recv2, s1, r1, s2, r2):
    me = lax.axis_index("row")
    other = lax.axis_index("col")
    chip, core = _row_greet(me, other, chips)
    sib = (chip * 2 + 1 - core, other)
    first = []
    for q in range(chips):
        copy = pltpu.make_async_remote_copy(
            src_ref=x_ref.at[q, 1 - core],
            dst_ref=recv1.at[q],
            send_sem=s1.at[q],
            recv_sem=r1.at[q],
            device_id=sib,
            device_id_type=MESH,
        )
        copy.start()
        first.append(copy)
    for q in range(chips):
        first[q].wait_recv()
    for d in range(1, chips):
        target = lax.rem(chip + d, chips)
        mid[d - 1] = x_ref[target, core] + recv1[target]
    sends = []
    for d in range(1, chips):
        target = lax.rem(chip + d, chips)
        copy = pltpu.make_async_remote_copy(
            src_ref=mid.at[d - 1],
            dst_ref=recv2.at[d - 1],
            send_sem=s2.at[d - 1],
            recv_sem=r2.at[d - 1],
            device_id=(target * 2 + core, other),
            device_id_type=MESH,
        )
        copy.start()
        sends.append(copy)
    acc = x_ref[chip, core] + recv1[chip]
    for d, copy in enumerate(sends):
        copy.wait_recv()
        acc = acc + recv2[d]
    for copy in first + sends:
        copy.wait_send()
    o_ref[...] = acc


def _row_ag_kernel(chips, x_ref, o_ref, recv_s, recv_a, recv_f, s1, r1, s2, r2):
    me = lax.axis_index("row")
    other = lax.axis_index("col")
    chip, core = _row_greet(me, other, chips)
    sib = (chip * 2 + 1 - core, other)
    to_sib = pltpu.make_async_remote_copy(
        src_ref=x_ref, dst_ref=recv_s, send_sem=s1.at[0], recv_sem=r1.at[0],
        device_id=sib, device_id_type=MESH,
    )
    to_sib.start()
    first = [to_sib]
    for d in range(1, chips):
        peer = lax.rem(chip + d, chips) * 2 + core
        copy = pltpu.make_async_remote_copy(
            src_ref=x_ref, dst_ref=recv_a.at[d - 1], send_sem=s1.at[d], recv_sem=r1.at[d],
            device_id=(peer, other), device_id_type=MESH,
        )
        copy.start()
        first.append(copy)
    o_ref[chip, core] = x_ref[...]
    forwards = []
    for d in range(1, chips):
        first[d].wait_recv()
        copy = pltpu.make_async_remote_copy(
            src_ref=recv_a.at[d - 1], dst_ref=recv_f.at[d - 1], send_sem=s2.at[d - 1],
            recv_sem=r2.at[d - 1], device_id=sib, device_id_type=MESH,
        )
        copy.start()
        forwards.append(copy)
        o_ref[lax.rem(chip + chips - d, chips), core] = recv_a[d - 1]
    to_sib.wait_recv()
    o_ref[chip, 1 - core] = recv_s[...]
    for d, copy in enumerate(forwards):
        copy.wait_recv()
        o_ref[lax.rem(chip + chips - 1 - d, chips), 1 - core] = recv_f[d]
    for copy in first + forwards:
        copy.wait_send()


def _row_reduce_scatter(x, collective_id):
    chips, _, rows, width = x.shape
    return pl.pallas_call(
        functools.partial(_row_rs_kernel, chips),
        out_shape=jax.ShapeDtypeStruct((rows, width), x.dtype),
        in_specs=[pl.BlockSpec(memory_space=pltpu.VMEM)],
        out_specs=pl.BlockSpec(memory_space=pltpu.VMEM),
        scratch_shapes=[
            pltpu.VMEM((chips, rows, width), x.dtype),
            pltpu.VMEM((chips - 1, rows, width), x.dtype),
            pltpu.VMEM((chips - 1, rows, width), x.dtype),
            pltpu.SemaphoreType.DMA((chips,)),
            pltpu.SemaphoreType.DMA((chips,)),
            pltpu.SemaphoreType.DMA((chips - 1,)),
            pltpu.SemaphoreType.DMA((chips - 1,)),
        ],
        compiler_params=pltpu.CompilerParams(collective_id=collective_id, has_side_effects=True),
    )(x)


def _row_all_gather(x, chips, collective_id):
    rows, width = x.shape
    return pl.pallas_call(
        functools.partial(_row_ag_kernel, chips),
        out_shape=jax.ShapeDtypeStruct((chips, 2, rows, width), x.dtype),
        in_specs=[pl.BlockSpec(memory_space=pltpu.VMEM)],
        out_specs=pl.BlockSpec(memory_space=pltpu.VMEM),
        scratch_shapes=[
            pltpu.VMEM((rows, width), x.dtype),
            pltpu.VMEM((chips - 1, rows, width), x.dtype),
            pltpu.VMEM((chips - 1, rows, width), x.dtype),
            pltpu.SemaphoreType.DMA((chips,)),
            pltpu.SemaphoreType.DMA((chips,)),
            pltpu.SemaphoreType.DMA((chips - 1,)),
            pltpu.SemaphoreType.DMA((chips - 1,)),
        ],
        compiler_params=pltpu.CompilerParams(collective_id=collective_id, has_side_effects=True),
    )(x)


def _reduce_scatter(x, axis, other_axis, collective_id):
    n, rows, width = x.shape
    return pl.pallas_call(
        functools.partial(_rs_kernel, axis, other_axis, n),
        out_shape=jax.ShapeDtypeStruct((rows, width), x.dtype),
        in_specs=[pl.BlockSpec(memory_space=pltpu.VMEM)],
        out_specs=pl.BlockSpec(memory_space=pltpu.VMEM),
        scratch_shapes=[
            pltpu.VMEM((n - 1, rows, width), x.dtype),
            pltpu.SemaphoreType.DMA((n - 1,)),
            pltpu.SemaphoreType.DMA((n - 1,)),
        ],
        compiler_params=pltpu.CompilerParams(collective_id=collective_id, has_side_effects=True),
    )(x)


def _all_gather(x, axis, other_axis, n, collective_id):
    rows, width = x.shape
    return pl.pallas_call(
        functools.partial(_ag_kernel, axis, other_axis, n),
        out_shape=jax.ShapeDtypeStruct((n, rows, width), x.dtype),
        in_specs=[pl.BlockSpec(memory_space=pltpu.VMEM)],
        out_specs=pl.BlockSpec(memory_space=pltpu.VMEM),
        scratch_shapes=[
            pltpu.VMEM((n - 1, rows, width), x.dtype),
            pltpu.SemaphoreType.DMA((n - 1,)),
            pltpu.SemaphoreType.DMA((n - 1,)),
        ],
        compiler_params=pltpu.CompilerParams(collective_id=collective_id, has_side_effects=True),
    )(x)


def _mask_lanes(mask_ref, nb, bs, width, row=None, col=None):
    blk = lax.broadcasted_iota(jnp.int32, (1, width), 1) // bs
    keep = jnp.zeros((1, width), jnp.int32)
    for b in range(nb):
        value = mask_ref[row, b] if col is None else mask_ref[b, col]
        keep = jnp.where(blk == b, value, keep)
    return keep != 0


def _sketch_kernel(nb, bs, mask_ref, g_ref, p_ref, o_ref):
    i = pl.program_id(0)
    keep = _mask_lanes(mask_ref, nb, bs, p_ref.shape[1], row=i)
    p = jnp.where(keep, p_ref[...], jnp.zeros_like(p_ref))
    o_ref[...] = lax.dot_general(
        p, g_ref[...], (((1,), (1,)), ((), ())), preferred_element_type=jnp.float32
    )


def _adjoint_kernel(nb, bs, mask_ref, l_ref, g_ref, o_ref):
    j = pl.program_id(0)
    keep = _mask_lanes(mask_ref, nb, bs, l_ref.shape[1], col=j)
    lowered = jnp.where(keep, l_ref[...], jnp.zeros_like(l_ref))
    o_ref[...] = jnp.dot(lowered, g_ref[...], preferred_element_type=jnp.float32)


def _sketch_partial(mask, green, probes_t):
    rb, cb = mask.shape
    bs = green.shape[0] // rb
    k = probes_t.shape[0]
    return pl.pallas_call(
        functools.partial(_sketch_kernel, cb, bs),
        out_shape=jax.ShapeDtypeStruct((k, green.shape[0]), jnp.float32),
        grid_spec=pltpu.PrefetchScalarGridSpec(
            num_scalar_prefetch=1,
            grid=(rb,),
            in_specs=[
                pl.BlockSpec((bs, green.shape[1]), lambda i, m: (i, 0)),
                pl.BlockSpec((k, green.shape[1]), lambda i, m: (0, 0)),
            ],
            out_specs=pl.BlockSpec((k, bs), lambda i, m: (0, i)),
        ),
    )(mask, green, probes_t)


def _adjoint_partial(mask, lowered_t, green):
    rb, cb = mask.shape
    bs = green.shape[0] // rb
    k = lowered_t.shape[0]
    return pl.pallas_call(
        functools.partial(_adjoint_kernel, rb, bs),
        out_shape=jax.ShapeDtypeStruct((k, green.shape[1]), jnp.float32),
        grid_spec=pltpu.PrefetchScalarGridSpec(
            num_scalar_prefetch=1,
            grid=(cb,),
            in_specs=[
                pl.BlockSpec((k, green.shape[0]), lambda j, m: (0, 0)),
                pl.BlockSpec((green.shape[0], bs), lambda j, m: (0, j)),
            ],
            out_specs=pl.BlockSpec((k, bs), lambda j, m: (0, j)),
        ),
    )(mask, lowered_t, green)


def local(green, mask, probes):
    n_row = lax.axis_size("row")
    n_col = lax.axis_size("col")
    probes_t = _row_all_gather(probes.T, n_row // 2, 3)
    k = n_row * probes_t.shape[2]
    probes_t = probes_t.reshape(k, -1)
    partial_t = _sketch_partial(mask, green, probes_t)
    sketch_t = _reduce_scatter(partial_t.reshape(n_col, k // n_col, -1), "col", "row", 0)
    lowered_t = _all_gather(sketch_t.astype(jnp.bfloat16), "col", "row", n_col, 1).reshape(k, -1)
    term_t = _adjoint_partial(mask, lowered_t, green)
    adjoint_t = _row_reduce_scatter(term_t.reshape(n_row // 2, 2, k // n_row, -1), 2)
    return (sketch_t.T, adjoint_t.T)


def solution(mesh):
    in_specs = (P("row", "col"), P("row", "col"), P("col", "row"))
    out_specs = (P("row", "col"), P("col", "row"))
    return jax.shard_map(local, mesh=mesh, in_specs=in_specs, out_specs=out_specs, check_vma=False)
```

```python
import functools

import jax
import jax.numpy as jnp
from jax import lax
from jax.experimental import pallas as pl
from jax.experimental.pallas import tpu as pltpu
from jax.sharding import PartitionSpec as P

MESH = pl.DeviceIdType.MESH


def _peer(axis, other, p):
    return (other, p) if axis == "col" else (p, other)


def _greet(axis, other, me, n):
    barrier = pltpu.get_barrier_semaphore()
    for d in range(1, n):
        peer = _peer(axis, other, lax.rem(me + d, n))
        pl.semaphore_signal(barrier, 1, device_id=peer, device_id_type=MESH)
    pl.semaphore_wait(barrier, n - 1)


def _rs_kernel(axis, other_axis, n, x_ref, o_ref, recv, send_sem, recv_sem):
    me = lax.axis_index(axis)
    other = lax.axis_index(other_axis)
    _greet(axis, other, me, n)
    copies = []
    for d in range(1, n):
        peer = lax.rem(me + d, n)
        copy = pltpu.make_async_remote_copy(
            src_ref=x_ref.at[peer],
            dst_ref=recv.at[d - 1],
            send_sem=send_sem.at[d - 1],
            recv_sem=recv_sem.at[d - 1],
            device_id=_peer(axis, other, peer),
            device_id_type=MESH,
        )
        copy.start()
        copies.append(copy)
    acc = x_ref[me]
    for d, copy in enumerate(copies):
        copy.wait_recv()
        acc = acc + recv[d]
    for copy in copies:
        copy.wait_send()
    o_ref[...] = acc


def _ag_kernel(axis, other_axis, n, x_ref, o_ref, recv, send_sem, recv_sem):
    me = lax.axis_index(axis)
    other = lax.axis_index(other_axis)
    _greet(axis, other, me, n)
    copies = []
    for d in range(1, n):
        peer = lax.rem(me + d, n)
        copy = pltpu.make_async_remote_copy(
            src_ref=x_ref,
            dst_ref=recv.at[d - 1],
            send_sem=send_sem.at[d - 1],
            recv_sem=recv_sem.at[d - 1],
            device_id=_peer(axis, other, peer),
            device_id_type=MESH,
        )
        copy.start()
        copies.append(copy)
    o_ref[me] = x_ref[...]
    for d, copy in enumerate(copies):
        copy.wait_recv()
        o_ref[lax.rem(me + n - 1 - d, n)] = recv[d]
    for copy in copies:
        copy.wait_send()


def _row_greet(axis, me, other, chips):
    chip, core = me // 2, lax.rem(me, 2)
    barrier = pltpu.get_barrier_semaphore()
    pl.semaphore_signal(barrier, 1, device_id=_peer(axis, other, chip * 2 + 1 - core), device_id_type=MESH)
    for d in range(1, chips):
        peer = lax.rem(chip + d, chips) * 2 + core
        pl.semaphore_signal(barrier, 1, device_id=_peer(axis, other, peer), device_id_type=MESH)
    pl.semaphore_wait(barrier, chips)
    return chip, core


def _row_rs_kernel(axis, other_axis, chips, x_ref, o_ref, recv1, mid, recv2, s1, r1, s2, r2):
    me = lax.axis_index(axis)
    other = lax.axis_index(other_axis)
    chip, core = _row_greet(axis, me, other, chips)
    sib = _peer(axis, other, chip * 2 + 1 - core)
    first = []
    for q in range(chips):
        copy = pltpu.make_async_remote_copy(
            src_ref=x_ref.at[q, 1 - core],
            dst_ref=recv1.at[q],
            send_sem=s1.at[q],
            recv_sem=r1.at[q],
            device_id=sib,
            device_id_type=MESH,
        )
        copy.start()
        first.append(copy)
    for q in range(chips):
        first[q].wait_recv()
    for d in range(1, chips):
        target = lax.rem(chip + d, chips)
        mid[d - 1] = x_ref[target, core] + recv1[target]
    sends = []
    for d in range(1, chips):
        target = lax.rem(chip + d, chips)
        copy = pltpu.make_async_remote_copy(
            src_ref=mid.at[d - 1],
            dst_ref=recv2.at[d - 1],
            send_sem=s2.at[d - 1],
            recv_sem=r2.at[d - 1],
            device_id=_peer(axis, other, target * 2 + core),
            device_id_type=MESH,
        )
        copy.start()
        sends.append(copy)
    acc = x_ref[chip, core] + recv1[chip]
    for d, copy in enumerate(sends):
        copy.wait_recv()
        acc = acc + recv2[d]
    for copy in first + sends:
        copy.wait_send()
    o_ref[...] = acc


def _row_ag_kernel(axis, other_axis, chips, x_ref, o_ref, recv_s, recv_a, recv_f, s1, r1, s2, r2):
    me = lax.axis_index(axis)
    other = lax.axis_index(other_axis)
    chip, core = _row_greet(axis, me, other, chips)
    sib = _peer(axis, other, chip * 2 + 1 - core)
    to_sib = pltpu.make_async_remote_copy(
        src_ref=x_ref, dst_ref=recv_s, send_sem=s1.at[0], recv_sem=r1.at[0],
        device_id=sib, device_id_type=MESH,
    )
    to_sib.start()
    first = [to_sib]
    for d in range(1, chips):
        peer = lax.rem(chip + d, chips) * 2 + core
        copy = pltpu.make_async_remote_copy(
            src_ref=x_ref, dst_ref=recv_a.at[d - 1], send_sem=s1.at[d], recv_sem=r1.at[d],
            device_id=_peer(axis, other, peer), device_id_type=MESH,
        )
        copy.start()
        first.append(copy)
    o_ref[chip, core] = x_ref[...]
    forwards = []
    for d in range(1, chips):
        first[d].wait_recv()
        copy = pltpu.make_async_remote_copy(
            src_ref=recv_a.at[d - 1], dst_ref=recv_f.at[d - 1], send_sem=s2.at[d - 1],
            recv_sem=r2.at[d - 1], device_id=sib, device_id_type=MESH,
        )
        copy.start()
        forwards.append(copy)
        o_ref[lax.rem(chip + chips - d, chips), core] = recv_a[d - 1]
    to_sib.wait_recv()
    o_ref[chip, 1 - core] = recv_s[...]
    for d, copy in enumerate(forwards):
        copy.wait_recv()
        o_ref[lax.rem(chip + chips - 1 - d, chips), 1 - core] = recv_f[d]
    for copy in first + forwards:
        copy.wait_send()


def _row_reduce_scatter(x, axis, other_axis, collective_id):
    chips, _, rows, width = x.shape
    return pl.pallas_call(
        functools.partial(_row_rs_kernel, axis, other_axis, chips),
        out_shape=jax.ShapeDtypeStruct((rows, width), x.dtype),
        in_specs=[pl.BlockSpec(memory_space=pltpu.VMEM)],
        out_specs=pl.BlockSpec(memory_space=pltpu.VMEM),
        scratch_shapes=[
            pltpu.VMEM((chips, rows, width), x.dtype),
            pltpu.VMEM((chips - 1, rows, width), x.dtype),
            pltpu.VMEM((chips - 1, rows, width), x.dtype),
            pltpu.SemaphoreType.DMA((chips,)),
            pltpu.SemaphoreType.DMA((chips,)),
            pltpu.SemaphoreType.DMA((chips - 1,)),
            pltpu.SemaphoreType.DMA((chips - 1,)),
        ],
        compiler_params=pltpu.CompilerParams(collective_id=collective_id, has_side_effects=True),
    )(x)


def _row_all_gather(x, axis, other_axis, chips, collective_id):
    rows, width = x.shape
    return pl.pallas_call(
        functools.partial(_row_ag_kernel, axis, other_axis, chips),
        out_shape=jax.ShapeDtypeStruct((chips, 2, rows, width), x.dtype),
        in_specs=[pl.BlockSpec(memory_space=pltpu.VMEM)],
        out_specs=pl.BlockSpec(memory_space=pltpu.VMEM),
        scratch_shapes=[
            pltpu.VMEM((rows, width), x.dtype),
            pltpu.VMEM((chips - 1, rows, width), x.dtype),
            pltpu.VMEM((chips - 1, rows, width), x.dtype),
            pltpu.SemaphoreType.DMA((chips,)),
            pltpu.SemaphoreType.DMA((chips,)),
            pltpu.SemaphoreType.DMA((chips - 1,)),
            pltpu.SemaphoreType.DMA((chips - 1,)),
        ],
        compiler_params=pltpu.CompilerParams(collective_id=collective_id, has_side_effects=True),
    )(x)


def _reduce_scatter(x, axis, other_axis, collective_id):
    n, rows, width = x.shape
    return pl.pallas_call(
        functools.partial(_rs_kernel, axis, other_axis, n),
        out_shape=jax.ShapeDtypeStruct((rows, width), x.dtype),
        in_specs=[pl.BlockSpec(memory_space=pltpu.VMEM)],
        out_specs=pl.BlockSpec(memory_space=pltpu.VMEM),
        scratch_shapes=[
            pltpu.VMEM((n - 1, rows, width), x.dtype),
            pltpu.SemaphoreType.DMA((n - 1,)),
            pltpu.SemaphoreType.DMA((n - 1,)),
        ],
        compiler_params=pltpu.CompilerParams(collective_id=collective_id, has_side_effects=True),
    )(x)


def _all_gather(x, axis, other_axis, n, collective_id):
    rows, width = x.shape
    return pl.pallas_call(
        functools.partial(_ag_kernel, axis, other_axis, n),
        out_shape=jax.ShapeDtypeStruct((n, rows, width), x.dtype),
        in_specs=[pl.BlockSpec(memory_space=pltpu.VMEM)],
        out_specs=pl.BlockSpec(memory_space=pltpu.VMEM),
        scratch_shapes=[
            pltpu.VMEM((n - 1, rows, width), x.dtype),
            pltpu.SemaphoreType.DMA((n - 1,)),
            pltpu.SemaphoreType.DMA((n - 1,)),
        ],
        compiler_params=pltpu.CompilerParams(collective_id=collective_id, has_side_effects=True),
    )(x)


def _mask_lanes(mask_ref, nb, bs, width, row=None, col=None):
    blk = lax.broadcasted_iota(jnp.int32, (1, width), 1) // bs
    keep = jnp.zeros((1, width), jnp.int32)
    for b in range(nb):
        value = mask_ref[row, b] if col is None else mask_ref[b, col]
        keep = jnp.where(blk == b, value, keep)
    return keep != 0


def _sketch_kernel(nb, bs, mask_ref, g_ref, p_ref, o_ref):
    i = pl.program_id(0)
    keep = _mask_lanes(mask_ref, nb, bs, p_ref.shape[1], row=i)
    p = jnp.where(keep, p_ref[...], jnp.zeros_like(p_ref))
    o_ref[...] = lax.dot_general(
        p, g_ref[...], (((1,), (1,)), ((), ())), preferred_element_type=jnp.float32
    )


def _adjoint_kernel(nb, bs, mask_ref, l_ref, g_ref, o_ref):
    j = pl.program_id(0)
    keep = _mask_lanes(mask_ref, nb, bs, l_ref.shape[1], col=j)
    lowered = jnp.where(keep, l_ref[...], jnp.zeros_like(l_ref))
    o_ref[...] = jnp.dot(lowered, g_ref[...], preferred_element_type=jnp.float32)


def _sketch_partial(mask, green, probes_t):
    rb, cb = mask.shape
    bs = green.shape[0] // rb
    k = probes_t.shape[0]
    return pl.pallas_call(
        functools.partial(_sketch_kernel, cb, bs),
        out_shape=jax.ShapeDtypeStruct((k, green.shape[0]), jnp.float32),
        grid_spec=pltpu.PrefetchScalarGridSpec(
            num_scalar_prefetch=1,
            grid=(rb,),
            in_specs=[
                pl.BlockSpec((bs, green.shape[1]), lambda i, m: (i, 0)),
                pl.BlockSpec((k, green.shape[1]), lambda i, m: (0, 0)),
            ],
            out_specs=pl.BlockSpec((k, bs), lambda i, m: (0, i)),
        ),
    )(mask, green, probes_t)


def _adjoint_partial(mask, lowered_t, green):
    rb, cb = mask.shape
    bs = green.shape[0] // rb
    k = lowered_t.shape[0]
    return pl.pallas_call(
        functools.partial(_adjoint_kernel, rb, bs),
        out_shape=jax.ShapeDtypeStruct((k, green.shape[1]), jnp.float32),
        grid_spec=pltpu.PrefetchScalarGridSpec(
            num_scalar_prefetch=1,
            grid=(cb,),
            in_specs=[
                pl.BlockSpec((k, green.shape[0]), lambda j, m: (0, 0)),
                pl.BlockSpec((green.shape[0], bs), lambda j, m: (0, j)),
            ],
            out_specs=pl.BlockSpec((k, bs), lambda j, m: (0, j)),
        ),
    )(mask, lowered_t, green)


def local(green, mask, probes):
    n_row = lax.axis_size("row")
    n_col = lax.axis_size("col")
    probes_t = _row_all_gather(probes.T, "row", "col", n_row // 2, 3)
    k = n_row * probes_t.shape[2]
    probes_t = probes_t.reshape(k, -1)
    partial_t = _sketch_partial(mask, green, probes_t)
    sketch_t = _row_reduce_scatter(partial_t.reshape(n_col // 2, 2, k // n_col, -1), "col", "row", 0)
    lowered_t = _row_all_gather(sketch_t.astype(jnp.bfloat16), "col", "row", n_col // 2, 1).reshape(k, -1)
    term_t = _adjoint_partial(mask, lowered_t, green)
    adjoint_t = _row_reduce_scatter(term_t.reshape(n_row // 2, 2, k // n_row, -1), "row", "col", 2)
    return (sketch_t.T, adjoint_t.T)


def solution(mesh):
    in_specs = (P("row", "col"), P("row", "col"), P("col", "row"))
    out_specs = (P("row", "col"), P("col", "row"))
    return jax.shard_map(local, mesh=mesh, in_specs=in_specs, out_specs=out_specs, check_vma=False)
```

```python
import functools

import jax
import jax.numpy as jnp
from jax import lax
from jax.experimental import pallas as pl
from jax.experimental.pallas import tpu as pltpu
from jax.sharding import PartitionSpec as P

MESH = pl.DeviceIdType.MESH


def _peer(axis, other, p):
    return (other, p) if axis == "col" else (p, other)


def _greet(axis, other, me, n):
    barrier = pltpu.get_barrier_semaphore()
    for d in range(1, n):
        peer = _peer(axis, other, lax.rem(me + d, n))
        pl.semaphore_signal(barrier, 1, device_id=peer, device_id_type=MESH)
    pl.semaphore_wait(barrier, n - 1)


def _rs_kernel(axis, other_axis, n, x_ref, o_ref, recv, send_sem, recv_sem):
    me = lax.axis_index(axis)
    other = lax.axis_index(other_axis)
    _greet(axis, other, me, n)
    copies = []
    for d in range(1, n):
        peer = lax.rem(me + d, n)
        copy = pltpu.make_async_remote_copy(
            src_ref=x_ref.at[peer],
            dst_ref=recv.at[d - 1],
            send_sem=send_sem.at[d - 1],
            recv_sem=recv_sem.at[d - 1],
            device_id=_peer(axis, other, peer),
            device_id_type=MESH,
        )
        copy.start()
        copies.append(copy)
    acc = x_ref[me]
    for d, copy in enumerate(copies):
        copy.wait_recv()
        acc = acc + recv[d]
    for copy in copies:
        copy.wait_send()
    o_ref[...] = acc


def _ag_kernel(axis, other_axis, n, x_ref, o_ref, recv, send_sem, recv_sem):
    me = lax.axis_index(axis)
    other = lax.axis_index(other_axis)
    _greet(axis, other, me, n)
    copies = []
    for d in range(1, n):
        peer = lax.rem(me + d, n)
        copy = pltpu.make_async_remote_copy(
            src_ref=x_ref,
            dst_ref=recv.at[d - 1],
            send_sem=send_sem.at[d - 1],
            recv_sem=recv_sem.at[d - 1],
            device_id=_peer(axis, other, peer),
            device_id_type=MESH,
        )
        copy.start()
        copies.append(copy)
    o_ref[me] = x_ref[...]
    for d, copy in enumerate(copies):
        copy.wait_recv()
        o_ref[lax.rem(me + n - 1 - d, n)] = recv[d]
    for copy in copies:
        copy.wait_send()


def _row_greet(axis, me, other, chips):
    chip, core = me // 2, lax.rem(me, 2)
    barrier = pltpu.get_barrier_semaphore()
    pl.semaphore_signal(barrier, 1, device_id=_peer(axis, other, chip * 2 + 1 - core), device_id_type=MESH)
    for d in range(1, chips):
        peer = lax.rem(chip + d, chips) * 2 + core
        pl.semaphore_signal(barrier, 1, device_id=_peer(axis, other, peer), device_id_type=MESH)
    pl.semaphore_wait(barrier, chips)
    return chip, core


def _row_rs_kernel(axis, other_axis, chips, x_ref, o_ref, recv1, mid, recv2, s1, r1, s2, r2):
    me = lax.axis_index(axis)
    other = lax.axis_index(other_axis)
    chip, core = _row_greet(axis, me, other, chips)
    _rs_body(axis, other, chips, chip, core, x_ref, o_ref, recv1, mid, recv2, s1, r1, s2, r2)


def _rs_body(axis, other, chips, chip, core, x_ref, o_ref, recv1, mid, recv2, s1, r1, s2, r2):
    sib = _peer(axis, other, chip * 2 + 1 - core)
    first = []
    for q in range(chips):
        copy = pltpu.make_async_remote_copy(
            src_ref=x_ref.at[q, 1 - core],
            dst_ref=recv1.at[q],
            send_sem=s1.at[q],
            recv_sem=r1.at[q],
            device_id=sib,
            device_id_type=MESH,
        )
        copy.start()
        first.append(copy)
    for q in range(chips):
        first[q].wait_recv()
    for d in range(1, chips):
        target = lax.rem(chip + d, chips)
        mid[d - 1] = x_ref[target, core] + recv1[target]
    sends = []
    for d in range(1, chips):
        target = lax.rem(chip + d, chips)
        copy = pltpu.make_async_remote_copy(
            src_ref=mid.at[d - 1],
            dst_ref=recv2.at[d - 1],
            send_sem=s2.at[d - 1],
            recv_sem=r2.at[d - 1],
            device_id=_peer(axis, other, target * 2 + core),
            device_id_type=MESH,
        )
        copy.start()
        sends.append(copy)
    acc = x_ref[chip, core] + recv1[chip]
    for d, copy in enumerate(sends):
        copy.wait_recv()
        acc = acc + recv2[d]
    for copy in first + sends:
        copy.wait_send()
    o_ref[...] = acc


def _row_ag_kernel(axis, other_axis, chips, x_ref, o_ref, recv_s, recv_a, recv_f, s1, r1, s2, r2):
    me = lax.axis_index(axis)
    other = lax.axis_index(other_axis)
    chip, core = _row_greet(axis, me, other, chips)
    _ag_body(axis, other, chips, chip, core, x_ref, o_ref, recv_s, recv_a, recv_f, s1, r1, s2, r2)


def _ag_body(axis, other, chips, chip, core, x_ref, o_ref, recv_s, recv_a, recv_f, s1, r1, s2, r2):
    sib = _peer(axis, other, chip * 2 + 1 - core)
    to_sib = pltpu.make_async_remote_copy(
        src_ref=x_ref, dst_ref=recv_s, send_sem=s1.at[0], recv_sem=r1.at[0],
        device_id=sib, device_id_type=MESH,
    )
    to_sib.start()
    first = [to_sib]
    for d in range(1, chips):
        peer = lax.rem(chip + d, chips) * 2 + core
        copy = pltpu.make_async_remote_copy(
            src_ref=x_ref, dst_ref=recv_a.at[d - 1], send_sem=s1.at[d], recv_sem=r1.at[d],
            device_id=_peer(axis, other, peer), device_id_type=MESH,
        )
        copy.start()
        first.append(copy)
    o_ref[chip, core] = x_ref[...]
    forwards = []
    for d in range(1, chips):
        first[d].wait_recv()
        copy = pltpu.make_async_remote_copy(
            src_ref=recv_a.at[d - 1], dst_ref=recv_f.at[d - 1], send_sem=s2.at[d - 1],
            recv_sem=r2.at[d - 1], device_id=sib, device_id_type=MESH,
        )
        copy.start()
        forwards.append(copy)
        o_ref[lax.rem(chip + chips - d, chips), core] = recv_a[d - 1]
    to_sib.wait_recv()
    o_ref[chip, 1 - core] = recv_s[...]
    for d, copy in enumerate(forwards):
        copy.wait_recv()
        o_ref[lax.rem(chip + chips - 1 - d, chips), 1 - core] = recv_f[d]
    for copy in first + forwards:
        copy.wait_send()


def _ar_kernel(axis, other_axis, chips, x_ref, o_ref, g_ref, low, *scratch):
    me = lax.axis_index(axis)
    other = lax.axis_index(other_axis)
    chip, core = _row_greet(axis, me, other, chips)
    _rs_body(axis, other, chips, chip, core, x_ref, o_ref, *scratch[:7])
    low[...] = o_ref[...].astype(low.dtype)
    _ag_body(axis, other, chips, chip, core, low, g_ref, *scratch[7:])


def _all_reduce(x, axis, other_axis, collective_id):
    chips, _, rows, width = x.shape
    low = jnp.bfloat16
    return pl.pallas_call(
        functools.partial(_ar_kernel, axis, other_axis, chips),
        out_shape=(
            jax.ShapeDtypeStruct((rows, width), x.dtype),
            jax.ShapeDtypeStruct((chips, 2, rows, width), low),
        ),
        in_specs=[pl.BlockSpec(memory_space=pltpu.VMEM)],
        out_specs=(pl.BlockSpec(memory_space=pltpu.VMEM), pl.BlockSpec(memory_space=pltpu.VMEM)),
        scratch_shapes=[
            pltpu.VMEM((rows, width), low),
            pltpu.VMEM((chips, rows, width), x.dtype),
            pltpu.VMEM((chips - 1, rows, width), x.dtype),
            pltpu.VMEM((chips - 1, rows, width), x.dtype),
            pltpu.SemaphoreType.DMA((chips,)),
            pltpu.SemaphoreType.DMA((chips,)),
            pltpu.SemaphoreType.DMA((chips - 1,)),
            pltpu.SemaphoreType.DMA((chips - 1,)),
            pltpu.VMEM((rows, width), low),
            pltpu.VMEM((chips - 1, rows, width), low),
            pltpu.VMEM((chips - 1, rows, width), low),
            pltpu.SemaphoreType.DMA((chips,)),
            pltpu.SemaphoreType.DMA((chips,)),
            pltpu.SemaphoreType.DMA((chips - 1,)),
            pltpu.SemaphoreType.DMA((chips - 1,)),
        ],
        compiler_params=pltpu.CompilerParams(collective_id=collective_id, has_side_effects=True),
    )(x)


def _row_reduce_scatter(x, axis, other_axis, collective_id):
    chips, _, rows, width = x.shape
    return pl.pallas_call(
        functools.partial(_row_rs_kernel, axis, other_axis, chips),
        out_shape=jax.ShapeDtypeStruct((rows, width), x.dtype),
        in_specs=[pl.BlockSpec(memory_space=pltpu.VMEM)],
        out_specs=pl.BlockSpec(memory_space=pltpu.VMEM),
        scratch_shapes=[
            pltpu.VMEM((chips, rows, width), x.dtype),
            pltpu.VMEM((chips - 1, rows, width), x.dtype),
            pltpu.VMEM((chips - 1, rows, width), x.dtype),
            pltpu.SemaphoreType.DMA((chips,)),
            pltpu.SemaphoreType.DMA((chips,)),
            pltpu.SemaphoreType.DMA((chips - 1,)),
            pltpu.SemaphoreType.DMA((chips - 1,)),
        ],
        compiler_params=pltpu.CompilerParams(collective_id=collective_id, has_side_effects=True),
    )(x)


def _row_all_gather(x, axis, other_axis, chips, collective_id):
    rows, width = x.shape
    return pl.pallas_call(
        functools.partial(_row_ag_kernel, axis, other_axis, chips),
        out_shape=jax.ShapeDtypeStruct((chips, 2, rows, width), x.dtype),
        in_specs=[pl.BlockSpec(memory_space=pltpu.VMEM)],
        out_specs=pl.BlockSpec(memory_space=pltpu.VMEM),
        scratch_shapes=[
            pltpu.VMEM((rows, width), x.dtype),
            pltpu.VMEM((chips - 1, rows, width), x.dtype),
            pltpu.VMEM((chips - 1, rows, width), x.dtype),
            pltpu.SemaphoreType.DMA((chips,)),
            pltpu.SemaphoreType.DMA((chips,)),
            pltpu.SemaphoreType.DMA((chips - 1,)),
            pltpu.SemaphoreType.DMA((chips - 1,)),
        ],
        compiler_params=pltpu.CompilerParams(collective_id=collective_id, has_side_effects=True),
    )(x)


def _reduce_scatter(x, axis, other_axis, collective_id):
    n, rows, width = x.shape
    return pl.pallas_call(
        functools.partial(_rs_kernel, axis, other_axis, n),
        out_shape=jax.ShapeDtypeStruct((rows, width), x.dtype),
        in_specs=[pl.BlockSpec(memory_space=pltpu.VMEM)],
        out_specs=pl.BlockSpec(memory_space=pltpu.VMEM),
        scratch_shapes=[
            pltpu.VMEM((n - 1, rows, width), x.dtype),
            pltpu.SemaphoreType.DMA((n - 1,)),
            pltpu.SemaphoreType.DMA((n - 1,)),
        ],
        compiler_params=pltpu.CompilerParams(collective_id=collective_id, has_side_effects=True),
    )(x)


def _all_gather(x, axis, other_axis, n, collective_id):
    rows, width = x.shape
    return pl.pallas_call(
        functools.partial(_ag_kernel, axis, other_axis, n),
        out_shape=jax.ShapeDtypeStruct((n, rows, width), x.dtype),
        in_specs=[pl.BlockSpec(memory_space=pltpu.VMEM)],
        out_specs=pl.BlockSpec(memory_space=pltpu.VMEM),
        scratch_shapes=[
            pltpu.VMEM((n - 1, rows, width), x.dtype),
            pltpu.SemaphoreType.DMA((n - 1,)),
            pltpu.SemaphoreType.DMA((n - 1,)),
        ],
        compiler_params=pltpu.CompilerParams(collective_id=collective_id, has_side_effects=True),
    )(x)


def _mask_lanes(mask_ref, nb, bs, width, row=None, col=None):
    blk = lax.broadcasted_iota(jnp.int32, (1, width), 1) // bs
    keep = jnp.zeros((1, width), jnp.int32)
    for b in range(nb):
        value = mask_ref[row, b] if col is None else mask_ref[b, col]
        keep = jnp.where(blk == b, value, keep)
    return keep != 0


def _sketch_kernel(nb, bs, mask_ref, g_ref, p_ref, o_ref):
    i = pl.program_id(0)
    keep = _mask_lanes(mask_ref, nb, bs, p_ref.shape[1], row=i)
    p = jnp.where(keep, p_ref[...], jnp.zeros_like(p_ref))
    o_ref[...] = lax.dot_general(
        p, g_ref[...], (((1,), (1,)), ((), ())), preferred_element_type=jnp.float32
    )


def _adjoint_kernel(nb, bs, mask_ref, l_ref, g_ref, o_ref):
    j = pl.program_id(0)
    keep = _mask_lanes(mask_ref, nb, bs, l_ref.shape[1], col=j)
    lowered = jnp.where(keep, l_ref[...], jnp.zeros_like(l_ref))
    o_ref[...] = jnp.dot(lowered, g_ref[...], preferred_element_type=jnp.float32)


def _sketch_partial(mask, green, probes_t):
    rb, cb = mask.shape
    bs = green.shape[0] // rb
    k = probes_t.shape[0]
    return pl.pallas_call(
        functools.partial(_sketch_kernel, cb, bs),
        out_shape=jax.ShapeDtypeStruct((k, green.shape[0]), jnp.float32),
        grid_spec=pltpu.PrefetchScalarGridSpec(
            num_scalar_prefetch=1,
            grid=(rb,),
            in_specs=[
                pl.BlockSpec((bs, green.shape[1]), lambda i, m: (i, 0)),
                pl.BlockSpec((k, green.shape[1]), lambda i, m: (0, 0)),
            ],
            out_specs=pl.BlockSpec((k, bs), lambda i, m: (0, i)),
        ),
    )(mask, green, probes_t)


def _adjoint_partial(mask, lowered_t, green):
    rb, cb = mask.shape
    bs = green.shape[0] // rb
    k = lowered_t.shape[0]
    return pl.pallas_call(
        functools.partial(_adjoint_kernel, rb, bs),
        out_shape=jax.ShapeDtypeStruct((k, green.shape[1]), jnp.float32),
        grid_spec=pltpu.PrefetchScalarGridSpec(
            num_scalar_prefetch=1,
            grid=(cb,),
            in_specs=[
                pl.BlockSpec((k, green.shape[0]), lambda j, m: (0, 0)),
                pl.BlockSpec((green.shape[0], bs), lambda j, m: (0, j)),
            ],
            out_specs=pl.BlockSpec((k, bs), lambda j, m: (0, j)),
        ),
    )(mask, lowered_t, green)


def local(green, mask, probes):
    n_row = lax.axis_size("row")
    n_col = lax.axis_size("col")
    probes_t = _row_all_gather(probes.T, "row", "col", n_row // 2, 3)
    k = n_row * probes_t.shape[2]
    probes_t = probes_t.reshape(k, -1)
    partial_t = _sketch_partial(mask, green, probes_t)
    sketch_t, lowered_t = _all_reduce(partial_t.reshape(n_col // 2, 2, k // n_col, -1), "col", "row", 0)
    lowered_t = lowered_t.reshape(k, -1)
    term_t = _adjoint_partial(mask, lowered_t, green)
    adjoint_t = _row_reduce_scatter(term_t.reshape(n_row // 2, 2, k // n_row, -1), "row", "col", 2)
    return (sketch_t.T, adjoint_t.T)


def solution(mesh):
    in_specs = (P("row", "col"), P("row", "col"), P("col", "row"))
    out_specs = (P("row", "col"), P("col", "row"))
    return jax.shard_map(local, mesh=mesh, in_specs=in_specs, out_specs=out_specs, check_vma=False)
```

```python
import functools

import jax
import jax.numpy as jnp
from jax import lax
from jax.experimental import pallas as pl
from jax.experimental.pallas import tpu as pltpu
from jax.sharding import PartitionSpec as P

MESH = pl.DeviceIdType.MESH


def _peer(axis, other, p):
    return (other, p) if axis == "col" else (p, other)


def _greet(axis, other, me, n):
    barrier = pltpu.get_barrier_semaphore()
    for d in range(1, n):
        peer = _peer(axis, other, lax.rem(me + d, n))
        pl.semaphore_signal(barrier, 1, device_id=peer, device_id_type=MESH)
    pl.semaphore_wait(barrier, n - 1)


def _rs_kernel(axis, other_axis, n, x_ref, o_ref, recv, send_sem, recv_sem):
    me = lax.axis_index(axis)
    other = lax.axis_index(other_axis)
    _greet(axis, other, me, n)
    copies = []
    for d in range(1, n):
        peer = lax.rem(me + d, n)
        copy = pltpu.make_async_remote_copy(
            src_ref=x_ref.at[peer],
            dst_ref=recv.at[d - 1],
            send_sem=send_sem.at[d - 1],
            recv_sem=recv_sem.at[d - 1],
            device_id=_peer(axis, other, peer),
            device_id_type=MESH,
        )
        copy.start()
        copies.append(copy)
    acc = x_ref[me]
    for d, copy in enumerate(copies):
        copy.wait_recv()
        acc = acc + recv[d]
    for copy in copies:
        copy.wait_send()
    o_ref[...] = acc


def _ag_kernel(axis, other_axis, n, x_ref, o_ref, recv, send_sem, recv_sem):
    me = lax.axis_index(axis)
    other = lax.axis_index(other_axis)
    _greet(axis, other, me, n)
    copies = []
    for d in range(1, n):
        peer = lax.rem(me + d, n)
        copy = pltpu.make_async_remote_copy(
            src_ref=x_ref,
            dst_ref=recv.at[d - 1],
            send_sem=send_sem.at[d - 1],
            recv_sem=recv_sem.at[d - 1],
            device_id=_peer(axis, other, peer),
            device_id_type=MESH,
        )
        copy.start()
        copies.append(copy)
    o_ref[me] = x_ref[...]
    for d, copy in enumerate(copies):
        copy.wait_recv()
        o_ref[lax.rem(me + n - 1 - d, n)] = recv[d]
    for copy in copies:
        copy.wait_send()


def _split(axis, me):
    if axis == "col":
        return (me // 4) * 2 + lax.rem(me, 2), lax.rem(me // 2, 2)
    return me // 2, lax.rem(me, 2)


def _index(axis, group, bit):
    if axis == "col":
        return (group // 2) * 4 + bit * 2 + lax.rem(group, 2)
    return group * 2 + bit


def _row_greet(axis, me, other, chips):
    chip, core = _split(axis, me)
    barrier = pltpu.get_barrier_semaphore()
    pl.semaphore_signal(barrier, 1, device_id=_peer(axis, other, _index(axis, chip, 1 - core)), device_id_type=MESH)
    for d in range(1, chips):
        peer = _index(axis, lax.rem(chip + d, chips), core)
        pl.semaphore_signal(barrier, 1, device_id=_peer(axis, other, peer), device_id_type=MESH)
    pl.semaphore_wait(barrier, chips)
    return chip, core


def _row_rs_kernel(axis, other_axis, chips, x_ref, o_ref, recv1, mid, recv2, s1, r1, s2, r2):
    me = lax.axis_index(axis)
    other = lax.axis_index(other_axis)
    chip, core = _row_greet(axis, me, other, chips)
    _rs_body(axis, other, chips, chip, core, x_ref, o_ref, recv1, mid, recv2, s1, r1, s2, r2)


def _rs_body(axis, other, chips, chip, core, x_ref, o_ref, recv1, mid, recv2, s1, r1, s2, r2):
    sib = _peer(axis, other, _index(axis, chip, 1 - core))
    first = []
    for q in range(chips):
        copy = pltpu.make_async_remote_copy(
            src_ref=x_ref.at[_index(axis, q, 1 - core)],
            dst_ref=recv1.at[q],
            send_sem=s1.at[q],
            recv_sem=r1.at[q],
            device_id=sib,
            device_id_type=MESH,
        )
        copy.start()
        first.append(copy)
    for q in range(chips):
        first[q].wait_recv()
    for d in range(1, chips):
        target = lax.rem(chip + d, chips)
        mid[d - 1] = x_ref[_index(axis, target, core)] + recv1[target]
    sends = []
    for d in range(1, chips):
        target = lax.rem(chip + d, chips)
        copy = pltpu.make_async_remote_copy(
            src_ref=mid.at[d - 1],
            dst_ref=recv2.at[d - 1],
            send_sem=s2.at[d - 1],
            recv_sem=r2.at[d - 1],
            device_id=_peer(axis, other, _index(axis, target, core)),
            device_id_type=MESH,
        )
        copy.start()
        sends.append(copy)
    acc = x_ref[_index(axis, chip, core)] + recv1[chip]
    for d, copy in enumerate(sends):
        copy.wait_recv()
        acc = acc + recv2[d]
    for copy in first + sends:
        copy.wait_send()
    o_ref[...] = acc


def _row_ag_kernel(axis, other_axis, chips, x_ref, o_ref, recv_s, recv_a, recv_f, s1, r1, s2, r2):
    me = lax.axis_index(axis)
    other = lax.axis_index(other_axis)
    chip, core = _row_greet(axis, me, other, chips)
    _ag_body(axis, other, chips, chip, core, x_ref, o_ref, recv_s, recv_a, recv_f, s1, r1, s2, r2)


def _ag_body(axis, other, chips, chip, core, x_ref, o_ref, recv_s, recv_a, recv_f, s1, r1, s2, r2):
    sib = _peer(axis, other, _index(axis, chip, 1 - core))
    to_sib = pltpu.make_async_remote_copy(
        src_ref=x_ref, dst_ref=recv_s, send_sem=s1.at[0], recv_sem=r1.at[0],
        device_id=sib, device_id_type=MESH,
    )
    to_sib.start()
    first = [to_sib]
    for d in range(1, chips):
        peer = _index(axis, lax.rem(chip + d, chips), core)
        copy = pltpu.make_async_remote_copy(
            src_ref=x_ref, dst_ref=recv_a.at[d - 1], send_sem=s1.at[d], recv_sem=r1.at[d],
            device_id=_peer(axis, other, peer), device_id_type=MESH,
        )
        copy.start()
        first.append(copy)
    o_ref[_index(axis, chip, core)] = x_ref[...]
    forwards = []
    for d in range(1, chips):
        first[d].wait_recv()
        copy = pltpu.make_async_remote_copy(
            src_ref=recv_a.at[d - 1], dst_ref=recv_f.at[d - 1], send_sem=s2.at[d - 1],
            recv_sem=r2.at[d - 1], device_id=sib, device_id_type=MESH,
        )
        copy.start()
        forwards.append(copy)
        o_ref[_index(axis, lax.rem(chip + chips - d, chips), core)] = recv_a[d - 1]
    to_sib.wait_recv()
    o_ref[_index(axis, chip, 1 - core)] = recv_s[...]
    for d, copy in enumerate(forwards):
        copy.wait_recv()
        o_ref[_index(axis, lax.rem(chip + chips - 1 - d, chips), 1 - core)] = recv_f[d]
    for copy in first + forwards:
        copy.wait_send()


def _ar_kernel(axis, other_axis, chips, x_ref, o_ref, g_ref, low, *scratch):
    me = lax.axis_index(axis)
    other = lax.axis_index(other_axis)
    chip, core = _row_greet(axis, me, other, chips)
    _rs_body(axis, other, chips, chip, core, x_ref, o_ref, *scratch[:7])
    low[...] = o_ref[...].astype(low.dtype)
    _ag_body(axis, other, chips, chip, core, low, g_ref, *scratch[7:])


def _all_reduce(x, axis, other_axis, collective_id):
    n, rows, width = x.shape
    chips = n // 2
    low = jnp.bfloat16
    return pl.pallas_call(
        functools.partial(_ar_kernel, axis, other_axis, chips),
        out_shape=(
            jax.ShapeDtypeStruct((rows, width), x.dtype),
            jax.ShapeDtypeStruct((n, rows, width), low),
        ),
        in_specs=[pl.BlockSpec(memory_space=pltpu.VMEM)],
        out_specs=(pl.BlockSpec(memory_space=pltpu.VMEM), pl.BlockSpec(memory_space=pltpu.VMEM)),
        scratch_shapes=[
            pltpu.VMEM((rows, width), low),
            pltpu.VMEM((chips, rows, width), x.dtype),
            pltpu.VMEM((chips - 1, rows, width), x.dtype),
            pltpu.VMEM((chips - 1, rows, width), x.dtype),
            pltpu.SemaphoreType.DMA((chips,)),
            pltpu.SemaphoreType.DMA((chips,)),
            pltpu.SemaphoreType.DMA((chips - 1,)),
            pltpu.SemaphoreType.DMA((chips - 1,)),
            pltpu.VMEM((rows, width), low),
            pltpu.VMEM((chips - 1, rows, width), low),
            pltpu.VMEM((chips - 1, rows, width), low),
            pltpu.SemaphoreType.DMA((chips,)),
            pltpu.SemaphoreType.DMA((chips,)),
            pltpu.SemaphoreType.DMA((chips - 1,)),
            pltpu.SemaphoreType.DMA((chips - 1,)),
        ],
        compiler_params=pltpu.CompilerParams(collective_id=collective_id, has_side_effects=True),
    )(x)


def _row_reduce_scatter(x, axis, other_axis, collective_id):
    n, rows, width = x.shape
    chips = n // 2
    return pl.pallas_call(
        functools.partial(_row_rs_kernel, axis, other_axis, chips),
        out_shape=jax.ShapeDtypeStruct((rows, width), x.dtype),
        in_specs=[pl.BlockSpec(memory_space=pltpu.VMEM)],
        out_specs=pl.BlockSpec(memory_space=pltpu.VMEM),
        scratch_shapes=[
            pltpu.VMEM((chips, rows, width), x.dtype),
            pltpu.VMEM((chips - 1, rows, width), x.dtype),
            pltpu.VMEM((chips - 1, rows, width), x.dtype),
            pltpu.SemaphoreType.DMA((chips,)),
            pltpu.SemaphoreType.DMA((chips,)),
            pltpu.SemaphoreType.DMA((chips - 1,)),
            pltpu.SemaphoreType.DMA((chips - 1,)),
        ],
        compiler_params=pltpu.CompilerParams(collective_id=collective_id, has_side_effects=True),
    )(x)


def _row_all_gather(x, axis, other_axis, chips, collective_id):
    rows, width = x.shape
    return pl.pallas_call(
        functools.partial(_row_ag_kernel, axis, other_axis, chips),
        out_shape=jax.ShapeDtypeStruct((2 * chips, rows, width), x.dtype),
        in_specs=[pl.BlockSpec(memory_space=pltpu.VMEM)],
        out_specs=pl.BlockSpec(memory_space=pltpu.VMEM),
        scratch_shapes=[
            pltpu.VMEM((rows, width), x.dtype),
            pltpu.VMEM((chips - 1, rows, width), x.dtype),
            pltpu.VMEM((chips - 1, rows, width), x.dtype),
            pltpu.SemaphoreType.DMA((chips,)),
            pltpu.SemaphoreType.DMA((chips,)),
            pltpu.SemaphoreType.DMA((chips - 1,)),
            pltpu.SemaphoreType.DMA((chips - 1,)),
        ],
        compiler_params=pltpu.CompilerParams(collective_id=collective_id, has_side_effects=True),
    )(x)


def _reduce_scatter(x, axis, other_axis, collective_id):
    n, rows, width = x.shape
    return pl.pallas_call(
        functools.partial(_rs_kernel, axis, other_axis, n),
        out_shape=jax.ShapeDtypeStruct((rows, width), x.dtype),
        in_specs=[pl.BlockSpec(memory_space=pltpu.VMEM)],
        out_specs=pl.BlockSpec(memory_space=pltpu.VMEM),
        scratch_shapes=[
            pltpu.VMEM((n - 1, rows, width), x.dtype),
            pltpu.SemaphoreType.DMA((n - 1,)),
            pltpu.SemaphoreType.DMA((n - 1,)),
        ],
        compiler_params=pltpu.CompilerParams(collective_id=collective_id, has_side_effects=True),
    )(x)


def _all_gather(x, axis, other_axis, n, collective_id):
    rows, width = x.shape
    return pl.pallas_call(
        functools.partial(_ag_kernel, axis, other_axis, n),
        out_shape=jax.ShapeDtypeStruct((n, rows, width), x.dtype),
        in_specs=[pl.BlockSpec(memory_space=pltpu.VMEM)],
        out_specs=pl.BlockSpec(memory_space=pltpu.VMEM),
        scratch_shapes=[
            pltpu.VMEM((n - 1, rows, width), x.dtype),
            pltpu.SemaphoreType.DMA((n - 1,)),
            pltpu.SemaphoreType.DMA((n - 1,)),
        ],
        compiler_params=pltpu.CompilerParams(collective_id=collective_id, has_side_effects=True),
    )(x)


def _mask_lanes(mask_ref, nb, bs, width, row=None, col=None):
    blk = lax.broadcasted_iota(jnp.int32, (1, width), 1) // bs
    keep = jnp.zeros((1, width), jnp.int32)
    for b in range(nb):
        value = mask_ref[row, b] if col is None else mask_ref[b, col]
        keep = jnp.where(blk == b, value, keep)
    return keep != 0


def _sketch_kernel(nb, bs, mask_ref, g_ref, p_ref, o_ref):
    i = pl.program_id(0)
    keep = _mask_lanes(mask_ref, nb, bs, p_ref.shape[1], row=i)
    p = jnp.where(keep, p_ref[...], jnp.zeros_like(p_ref))
    o_ref[...] = lax.dot_general(
        p, g_ref[...], (((1,), (1,)), ((), ())), preferred_element_type=jnp.float32
    )


def _adjoint_kernel(nb, bs, mask_ref, l_ref, g_ref, o_ref):
    j = pl.program_id(0)
    keep = _mask_lanes(mask_ref, nb, bs, l_ref.shape[1], col=j)
    lowered = jnp.where(keep, l_ref[...], jnp.zeros_like(l_ref))
    o_ref[...] = jnp.dot(lowered, g_ref[...], preferred_element_type=jnp.float32)


def _sketch_partial(mask, green, probes_t):
    rb, cb = mask.shape
    bs = green.shape[0] // rb
    k = probes_t.shape[0]
    return pl.pallas_call(
        functools.partial(_sketch_kernel, cb, bs),
        out_shape=jax.ShapeDtypeStruct((k, green.shape[0]), jnp.float32),
        grid_spec=pltpu.PrefetchScalarGridSpec(
            num_scalar_prefetch=1,
            grid=(rb,),
            in_specs=[
                pl.BlockSpec((bs, green.shape[1]), lambda i, m: (i, 0)),
                pl.BlockSpec((k, green.shape[1]), lambda i, m: (0, 0)),
            ],
            out_specs=pl.BlockSpec((k, bs), lambda i, m: (0, i)),
        ),
    )(mask, green, probes_t)


def _adjoint_partial(mask, lowered_t, green):
    rb, cb = mask.shape
    bs = green.shape[0] // rb
    k = lowered_t.shape[0]
    return pl.pallas_call(
        functools.partial(_adjoint_kernel, rb, bs),
        out_shape=jax.ShapeDtypeStruct((k, green.shape[1]), jnp.float32),
        grid_spec=pltpu.PrefetchScalarGridSpec(
            num_scalar_prefetch=1,
            grid=(cb,),
            in_specs=[
                pl.BlockSpec((k, green.shape[0]), lambda j, m: (0, 0)),
                pl.BlockSpec((green.shape[0], bs), lambda j, m: (0, j)),
            ],
            out_specs=pl.BlockSpec((k, bs), lambda j, m: (0, j)),
        ),
    )(mask, lowered_t, green)


def local(green, mask, probes):
    n_row = lax.axis_size("row")
    n_col = lax.axis_size("col")
    probes_t = _row_all_gather(probes.T, "row", "col", n_row // 2, 3)
    k = n_row * probes_t.shape[1]
    probes_t = probes_t.reshape(k, -1)
    partial_t = _sketch_partial(mask, green, probes_t)
    sketch_t, lowered_t = _all_reduce(partial_t.reshape(n_col, k // n_col, -1), "col", "row", 0)
    lowered_t = lowered_t.reshape(k, -1)
    term_t = _adjoint_partial(mask, lowered_t, green)
    adjoint_t = _row_reduce_scatter(term_t.reshape(n_row, k // n_row, -1), "row", "col", 2)
    return (sketch_t.T, adjoint_t.T)


def solution(mesh):
    in_specs = (P("row", "col"), P("row", "col"), P("col", "row"))
    out_specs = (P("row", "col"), P("col", "row"))
    return jax.shard_map(local, mesh=mesh, in_specs=in_specs, out_specs=out_specs, check_vma=False)
```

```python
import functools

import jax
import jax.numpy as jnp
from jax import lax
from jax.experimental import pallas as pl
from jax.experimental.pallas import tpu as pltpu
from jax.sharding import PartitionSpec as P

MESH = pl.DeviceIdType.MESH


def _peer(axis, other, p):
    return (other, p) if axis == "col" else (p, other)


def _greet(axis, other, me, n):
    barrier = pltpu.get_barrier_semaphore()
    for d in range(1, n):
        peer = _peer(axis, other, lax.rem(me + d, n))
        pl.semaphore_signal(barrier, 1, device_id=peer, device_id_type=MESH)
    pl.semaphore_wait(barrier, n - 1)


def _rs_kernel(axis, other_axis, n, x_ref, o_ref, recv, send_sem, recv_sem):
    me = lax.axis_index(axis)
    other = lax.axis_index(other_axis)
    _greet(axis, other, me, n)
    copies = []
    for d in range(1, n):
        peer = lax.rem(me + d, n)
        copy = pltpu.make_async_remote_copy(
            src_ref=x_ref.at[peer],
            dst_ref=recv.at[d - 1],
            send_sem=send_sem.at[d - 1],
            recv_sem=recv_sem.at[d - 1],
            device_id=_peer(axis, other, peer),
            device_id_type=MESH,
        )
        copy.start()
        copies.append(copy)
    acc = x_ref[me]
    for d, copy in enumerate(copies):
        copy.wait_recv()
        acc = acc + recv[d]
    for copy in copies:
        copy.wait_send()
    o_ref[...] = acc


def _ag_kernel(axis, other_axis, n, x_ref, o_ref, recv, send_sem, recv_sem):
    me = lax.axis_index(axis)
    other = lax.axis_index(other_axis)
    _greet(axis, other, me, n)
    copies = []
    for d in range(1, n):
        peer = lax.rem(me + d, n)
        copy = pltpu.make_async_remote_copy(
            src_ref=x_ref,
            dst_ref=recv.at[d - 1],
            send_sem=send_sem.at[d - 1],
            recv_sem=recv_sem.at[d - 1],
            device_id=_peer(axis, other, peer),
            device_id_type=MESH,
        )
        copy.start()
        copies.append(copy)
    o_ref[me] = x_ref[...]
    for d, copy in enumerate(copies):
        copy.wait_recv()
        o_ref[lax.rem(me + n - 1 - d, n)] = recv[d]
    for copy in copies:
        copy.wait_send()


def _row_greet(axis, me, other, chips):
    chip, core = me // 2, lax.rem(me, 2)
    barrier = pltpu.get_barrier_semaphore()
    pl.semaphore_signal(barrier, 1, device_id=_peer(axis, other, chip * 2 + 1 - core), device_id_type=MESH)
    for d in range(1, chips):
        peer = lax.rem(chip + d, chips) * 2 + core
        pl.semaphore_signal(barrier, 1, device_id=_peer(axis, other, peer), device_id_type=MESH)
    pl.semaphore_wait(barrier, chips)
    return chip, core


def _row_rs_kernel(axis, other_axis, chips, x_ref, o_ref, recv1, mid, recv2, s1, r1, s2, r2):
    me = lax.axis_index(axis)
    other = lax.axis_index(other_axis)
    chip, core = _row_greet(axis, me, other, chips)
    _rs_body(axis, other, chips, chip, core, x_ref, o_ref, recv1, mid, recv2, s1, r1, s2, r2)


def _rs_body(axis, other, chips, chip, core, x_ref, o_ref, recv1, mid, recv2, s1, r1, s2, r2):
    sib = _peer(axis, other, chip * 2 + 1 - core)
    first = []
    for q in range(chips):
        copy = pltpu.make_async_remote_copy(
            src_ref=x_ref.at[q, 1 - core],
            dst_ref=recv1.at[q],
            send_sem=s1.at[q],
            recv_sem=r1.at[q],
            device_id=sib,
            device_id_type=MESH,
        )
        copy.start()
        first.append(copy)
    for q in range(chips):
        first[q].wait_recv()
    for d in range(1, chips):
        target = lax.rem(chip + d, chips)
        mid[d - 1] = x_ref[target, core] + recv1[target]
    sends = []
    for d in range(1, chips):
        target = lax.rem(chip + d, chips)
        copy = pltpu.make_async_remote_copy(
            src_ref=mid.at[d - 1],
            dst_ref=recv2.at[d - 1],
            send_sem=s2.at[d - 1],
            recv_sem=r2.at[d - 1],
            device_id=_peer(axis, other, target * 2 + core),
            device_id_type=MESH,
        )
        copy.start()
        sends.append(copy)
    acc = x_ref[chip, core] + recv1[chip]
    for d, copy in enumerate(sends):
        copy.wait_recv()
        acc = acc + recv2[d]
    for copy in first + sends:
        copy.wait_send()
    o_ref[...] = acc


def _row_ag_kernel(axis, other_axis, chips, x_ref, o_ref, recv_s, recv_a, recv_f, s1, r1, s2, r2):
    me = lax.axis_index(axis)
    other = lax.axis_index(other_axis)
    chip, core = _row_greet(axis, me, other, chips)
    _ag_body(axis, other, chips, chip, core, x_ref, o_ref, recv_s, recv_a, recv_f, s1, r1, s2, r2)


def _ag_body(axis, other, chips, chip, core, x_ref, o_ref, recv_s, recv_a, recv_f, s1, r1, s2, r2):
    sib = _peer(axis, other, chip * 2 + 1 - core)
    to_sib = pltpu.make_async_remote_copy(
        src_ref=x_ref, dst_ref=recv_s, send_sem=s1.at[0], recv_sem=r1.at[0],
        device_id=sib, device_id_type=MESH,
    )
    to_sib.start()
    first = [to_sib]
    for d in range(1, chips):
        peer = lax.rem(chip + d, chips) * 2 + core
        copy = pltpu.make_async_remote_copy(
            src_ref=x_ref, dst_ref=recv_a.at[d - 1], send_sem=s1.at[d], recv_sem=r1.at[d],
            device_id=_peer(axis, other, peer), device_id_type=MESH,
        )
        copy.start()
        first.append(copy)
    o_ref[chip, core] = x_ref[...]
    forwards = []
    for d in range(1, chips):
        first[d].wait_recv()
        copy = pltpu.make_async_remote_copy(
            src_ref=recv_a.at[d - 1], dst_ref=recv_f.at[d - 1], send_sem=s2.at[d - 1],
            recv_sem=r2.at[d - 1], device_id=sib, device_id_type=MESH,
        )
        copy.start()
        forwards.append(copy)
        o_ref[lax.rem(chip + chips - d, chips), core] = recv_a[d - 1]
    to_sib.wait_recv()
    o_ref[chip, 1 - core] = recv_s[...]
    for d, copy in enumerate(forwards):
        copy.wait_recv()
        o_ref[lax.rem(chip + chips - 1 - d, chips), 1 - core] = recv_f[d]
    for copy in first + forwards:
        copy.wait_send()


def _ar_kernel(axis, other_axis, chips, x_ref, o_ref, g_ref, low, *scratch):
    me = lax.axis_index(axis)
    other = lax.axis_index(other_axis)
    chip, core = _row_greet(axis, me, other, chips)
    _rs_body(axis, other, chips, chip, core, x_ref, o_ref, *scratch[:7])
    low[...] = o_ref[...].astype(low.dtype)
    _ag_body(axis, other, chips, chip, core, low, g_ref, *scratch[7:])


def _all_reduce(x, axis, other_axis, collective_id):
    chips, _, rows, width = x.shape
    low = jnp.bfloat16
    return pl.pallas_call(
        functools.partial(_ar_kernel, axis, other_axis, chips),
        out_shape=(
            jax.ShapeDtypeStruct((rows, width), x.dtype),
            jax.ShapeDtypeStruct((chips, 2, rows, width), low),
        ),
        in_specs=[pl.BlockSpec(memory_space=pltpu.VMEM)],
        out_specs=(pl.BlockSpec(memory_space=pltpu.VMEM), pl.BlockSpec(memory_space=pltpu.VMEM)),
        scratch_shapes=[
            pltpu.VMEM((rows, width), low),
            pltpu.VMEM((chips, rows, width), x.dtype),
            pltpu.VMEM((chips - 1, rows, width), x.dtype),
            pltpu.VMEM((chips - 1, rows, width), x.dtype),
            pltpu.SemaphoreType.DMA((chips,)),
            pltpu.SemaphoreType.DMA((chips,)),
            pltpu.SemaphoreType.DMA((chips - 1,)),
            pltpu.SemaphoreType.DMA((chips - 1,)),
            pltpu.VMEM((rows, width), low),
            pltpu.VMEM((chips - 1, rows, width), low),
            pltpu.VMEM((chips - 1, rows, width), low),
            pltpu.SemaphoreType.DMA((chips,)),
            pltpu.SemaphoreType.DMA((chips,)),
            pltpu.SemaphoreType.DMA((chips - 1,)),
            pltpu.SemaphoreType.DMA((chips - 1,)),
        ],
        compiler_params=pltpu.CompilerParams(collective_id=collective_id, has_side_effects=True),
    )(x)


def _row_reduce_scatter(x, axis, other_axis, collective_id):
    chips, _, rows, width = x.shape
    return pl.pallas_call(
        functools.partial(_row_rs_kernel, axis, other_axis, chips),
        out_shape=jax.ShapeDtypeStruct((rows, width), x.dtype),
        in_specs=[pl.BlockSpec(memory_space=pltpu.VMEM)],
        out_specs=pl.BlockSpec(memory_space=pltpu.VMEM),
        scratch_shapes=[
            pltpu.VMEM((chips, rows, width), x.dtype),
            pltpu.VMEM((chips - 1, rows, width), x.dtype),
            pltpu.VMEM((chips - 1, rows, width), x.dtype),
            pltpu.SemaphoreType.DMA((chips,)),
            pltpu.SemaphoreType.DMA((chips,)),
            pltpu.SemaphoreType.DMA((chips - 1,)),
            pltpu.SemaphoreType.DMA((chips - 1,)),
        ],
        compiler_params=pltpu.CompilerParams(collective_id=collective_id, has_side_effects=True),
    )(x)


def _row_all_gather(x, axis, other_axis, chips, collective_id):
    rows, width = x.shape
    return pl.pallas_call(
        functools.partial(_row_ag_kernel, axis, other_axis, chips),
        out_shape=jax.ShapeDtypeStruct((chips, 2, rows, width), x.dtype),
        in_specs=[pl.BlockSpec(memory_space=pltpu.VMEM)],
        out_specs=pl.BlockSpec(memory_space=pltpu.VMEM),
        scratch_shapes=[
            pltpu.VMEM((rows, width), x.dtype),
            pltpu.VMEM((chips - 1, rows, width), x.dtype),
            pltpu.VMEM((chips - 1, rows, width), x.dtype),
            pltpu.SemaphoreType.DMA((chips,)),
            pltpu.SemaphoreType.DMA((chips,)),
            pltpu.SemaphoreType.DMA((chips - 1,)),
            pltpu.SemaphoreType.DMA((chips - 1,)),
        ],
        compiler_params=pltpu.CompilerParams(collective_id=collective_id, has_side_effects=True),
    )(x)


def _reduce_scatter(x, axis, other_axis, collective_id):
    n, rows, width = x.shape
    return pl.pallas_call(
        functools.partial(_rs_kernel, axis, other_axis, n),
        out_shape=jax.ShapeDtypeStruct((rows, width), x.dtype),
        in_specs=[pl.BlockSpec(memory_space=pltpu.VMEM)],
        out_specs=pl.BlockSpec(memory_space=pltpu.VMEM),
        scratch_shapes=[
            pltpu.VMEM((n - 1, rows, width), x.dtype),
            pltpu.SemaphoreType.DMA((n - 1,)),
            pltpu.SemaphoreType.DMA((n - 1,)),
        ],
        compiler_params=pltpu.CompilerParams(collective_id=collective_id, has_side_effects=True),
    )(x)


def _all_gather(x, axis, other_axis, n, collective_id):
    rows, width = x.shape
    return pl.pallas_call(
        functools.partial(_ag_kernel, axis, other_axis, n),
        out_shape=jax.ShapeDtypeStruct((n, rows, width), x.dtype),
        in_specs=[pl.BlockSpec(memory_space=pltpu.VMEM)],
        out_specs=pl.BlockSpec(memory_space=pltpu.VMEM),
        scratch_shapes=[
            pltpu.VMEM((n - 1, rows, width), x.dtype),
            pltpu.SemaphoreType.DMA((n - 1,)),
            pltpu.SemaphoreType.DMA((n - 1,)),
        ],
        compiler_params=pltpu.CompilerParams(collective_id=collective_id, has_side_effects=True),
    )(x)


def _mask_lanes(mask_ref, nb, bs, width, row=None, col=None):
    blk = lax.broadcasted_iota(jnp.int32, (1, width), 1) // bs
    keep = jnp.zeros((1, width), jnp.int32)
    for b in range(nb):
        value = mask_ref[row, b] if col is None else mask_ref[b, col]
        keep = jnp.where(blk == b, value, keep)
    return keep != 0


def _sub_blocks(nb):
    return 4 if nb % 4 == 0 else (2 if nb % 2 == 0 else 1)


def _sketch_kernel(nb, bs, sub, mask_ref, g_ref, p_ref, o_ref):
    i = pl.program_id(0)
    for h in range(sub):
        keep = _mask_lanes(mask_ref, nb, bs, p_ref.shape[1], row=i * sub + h)
        p = jnp.where(keep, p_ref[...], jnp.zeros_like(p_ref))
        o_ref[:, h * bs:(h + 1) * bs] = lax.dot_general(
            p, g_ref[h * bs:(h + 1) * bs, :], (((1,), (1,)), ((), ())), preferred_element_type=jnp.float32
        )


def _adjoint_kernel(nb, bs, sub, mask_ref, l_ref, g_ref, o_ref):
    j = pl.program_id(0)
    for h in range(sub):
        keep = _mask_lanes(mask_ref, nb, bs, l_ref.shape[1], col=j * sub + h)
        lowered = jnp.where(keep, l_ref[...], jnp.zeros_like(l_ref))
        o_ref[:, h * bs:(h + 1) * bs] = jnp.dot(
            lowered, g_ref[:, h * bs:(h + 1) * bs], preferred_element_type=jnp.float32
        )


def _sketch_partial(mask, green, probes_t):
    rb, cb = mask.shape
    bs = green.shape[0] // rb
    sub = _sub_blocks(rb)
    k = probes_t.shape[0]
    return pl.pallas_call(
        functools.partial(_sketch_kernel, cb, bs, sub),
        out_shape=jax.ShapeDtypeStruct((k, green.shape[0]), jnp.float32),
        grid_spec=pltpu.PrefetchScalarGridSpec(
            num_scalar_prefetch=1,
            grid=(rb // sub,),
            in_specs=[
                pl.BlockSpec((bs * sub, green.shape[1]), lambda i, m: (i, 0)),
                pl.BlockSpec((k, green.shape[1]), lambda i, m: (0, 0)),
            ],
            out_specs=pl.BlockSpec((k, bs * sub), lambda i, m: (0, i)),
        ),
    )(mask, green, probes_t)


def _adjoint_partial(mask, lowered_t, green):
    rb, cb = mask.shape
    bs = green.shape[0] // rb
    sub = _sub_blocks(cb)
    k = lowered_t.shape[0]
    return pl.pallas_call(
        functools.partial(_adjoint_kernel, rb, bs, sub),
        out_shape=jax.ShapeDtypeStruct((k, green.shape[1]), jnp.float32),
        grid_spec=pltpu.PrefetchScalarGridSpec(
            num_scalar_prefetch=1,
            grid=(cb // sub,),
            in_specs=[
                pl.BlockSpec((k, green.shape[0]), lambda j, m: (0, 0)),
                pl.BlockSpec((green.shape[0], bs * sub), lambda j, m: (0, j)),
            ],
            out_specs=pl.BlockSpec((k, bs * sub), lambda j, m: (0, j)),
        ),
    )(mask, lowered_t, green)


def local(green, mask, probes):
    n_row = lax.axis_size("row")
    n_col = lax.axis_size("col")
    probes_t = _row_all_gather(probes.T, "row", "col", n_row // 2, 3)
    k = n_row * probes_t.shape[2]
    probes_t = probes_t.reshape(k, -1)
    partial_t = _sketch_partial(mask, green, probes_t)
    sketch_t, lowered_t = _all_reduce(partial_t.reshape(n_col // 2, 2, k // n_col, -1), "col", "row", 0)
    lowered_t = lowered_t.reshape(k, -1)
    term_t = _adjoint_partial(mask, lowered_t, green)
    adjoint_t = _row_reduce_scatter(term_t.reshape(n_row // 2, 2, k // n_row, -1), "row", "col", 2)
    return (sketch_t.T, adjoint_t.T)


def solution(mesh):
    in_specs = (P("row", "col"), P("row", "col"), P("col", "row"))
    out_specs = (P("row", "col"), P("col", "row"))
    return jax.shard_map(local, mesh=mesh, in_specs=in_specs, out_specs=out_specs, check_vma=False)
```

```python
import functools

import jax
import jax.numpy as jnp
from jax import lax
from jax.experimental import pallas as pl
from jax.experimental.pallas import tpu as pltpu
from jax.sharding import PartitionSpec as P

MESH = pl.DeviceIdType.MESH


def _peer(axis, other, p):
    return (other, p) if axis == "col" else (p, other)


def _greet(axis, other, me, n):
    barrier = pltpu.get_barrier_semaphore()
    for d in range(1, n):
        peer = _peer(axis, other, lax.rem(me + d, n))
        pl.semaphore_signal(barrier, 1, device_id=peer, device_id_type=MESH)
    pl.semaphore_wait(barrier, n - 1)


def _rs_kernel(axis, other_axis, n, x_ref, o_ref, recv, send_sem, recv_sem):
    me = lax.axis_index(axis)
    other = lax.axis_index(other_axis)
    _greet(axis, other, me, n)
    copies = []
    for d in range(1, n):
        peer = lax.rem(me + d, n)
        copy = pltpu.make_async_remote_copy(
            src_ref=x_ref.at[peer],
            dst_ref=recv.at[d - 1],
            send_sem=send_sem.at[d - 1],
            recv_sem=recv_sem.at[d - 1],
            device_id=_peer(axis, other, peer),
            device_id_type=MESH,
        )
        copy.start()
        copies.append(copy)
    acc = x_ref[me]
    for d, copy in enumerate(copies):
        copy.wait_recv()
        acc = acc + recv[d]
    for copy in copies:
        copy.wait_send()
    o_ref[...] = acc


def _ag_kernel(axis, other_axis, n, x_ref, o_ref, recv, send_sem, recv_sem):
    me = lax.axis_index(axis)
    other = lax.axis_index(other_axis)
    _greet(axis, other, me, n)
    copies = []
    for d in range(1, n):
        peer = lax.rem(me + d, n)
        copy = pltpu.make_async_remote_copy(
            src_ref=x_ref,
            dst_ref=recv.at[d - 1],
            send_sem=send_sem.at[d - 1],
            recv_sem=recv_sem.at[d - 1],
            device_id=_peer(axis, other, peer),
            device_id_type=MESH,
        )
        copy.start()
        copies.append(copy)
    o_ref[me] = x_ref[...]
    for d, copy in enumerate(copies):
        copy.wait_recv()
        o_ref[lax.rem(me + n - 1 - d, n)] = recv[d]
    for copy in copies:
        copy.wait_send()


def _index(axis, group, bit):
    return group * 2 + bit


def _row_greet(axis, me, other, chips):
    chip, core = me // 2, lax.rem(me, 2)
    barrier = pltpu.get_barrier_semaphore()
    pl.semaphore_signal(barrier, 1, device_id=_peer(axis, other, chip * 2 + 1 - core), device_id_type=MESH)
    for d in range(1, chips):
        peer = lax.rem(chip + d, chips) * 2 + core
        pl.semaphore_signal(barrier, 1, device_id=_peer(axis, other, peer), device_id_type=MESH)
    pl.semaphore_wait(barrier, chips)
    return chip, core


def _row_rs_kernel(axis, other_axis, chips, x_ref, o_ref, recv1, mid, recv2, s1, r1, s2, r2):
    me = lax.axis_index(axis)
    other = lax.axis_index(other_axis)
    chip, core = _row_greet(axis, me, other, chips)
    _rs_body(axis, other, chips, chip, core, x_ref, o_ref, recv1, mid, recv2, s1, r1, s2, r2)


def _rs_body(axis, other, chips, chip, core, x_ref, o_ref, recv1, mid, recv2, s1, r1, s2, r2):
    sib = _peer(axis, other, chip * 2 + 1 - core)
    first = []
    for q in range(chips):
        copy = pltpu.make_async_remote_copy(
            src_ref=x_ref.at[q, 1 - core],
            dst_ref=recv1.at[q],
            send_sem=s1.at[q],
            recv_sem=r1.at[q],
            device_id=sib,
            device_id_type=MESH,
        )
        copy.start()
        first.append(copy)
    for q in range(chips):
        first[q].wait_recv()
    for d in range(1, chips):
        target = lax.rem(chip + d, chips)
        mid[d - 1] = x_ref[target, core] + recv1[target]
    sends = []
    for d in range(1, chips):
        target = lax.rem(chip + d, chips)
        copy = pltpu.make_async_remote_copy(
            src_ref=mid.at[d - 1],
            dst_ref=recv2.at[d - 1],
            send_sem=s2.at[d - 1],
            recv_sem=r2.at[d - 1],
            device_id=_peer(axis, other, target * 2 + core),
            device_id_type=MESH,
        )
        copy.start()
        sends.append(copy)
    acc = x_ref[chip, core] + recv1[chip]
    for d, copy in enumerate(sends):
        copy.wait_recv()
        acc = acc + recv2[d]
    for copy in first + sends:
        copy.wait_send()
    o_ref[...] = acc


def _row_ag_kernel(axis, other_axis, chips, x_ref, o_ref, recv_s, recv_a, recv_f, s1, r1, s2, r2):
    me = lax.axis_index(axis)
    other = lax.axis_index(other_axis)
    chip, core = _row_greet(axis, me, other, chips)
    _ag_body(axis, other, chips, chip, core, x_ref, o_ref, recv_s, recv_a, recv_f, s1, r1, s2, r2)


def _ag_body(axis, other, chips, chip, core, x_ref, o_ref, recv_s, recv_a, recv_f, s1, r1, s2, r2):
    sib = _peer(axis, other, chip * 2 + 1 - core)
    to_sib = pltpu.make_async_remote_copy(
        src_ref=x_ref, dst_ref=recv_s, send_sem=s1.at[0], recv_sem=r1.at[0],
        device_id=sib, device_id_type=MESH,
    )
    to_sib.start()
    first = [to_sib]
    for d in range(1, chips):
        peer = lax.rem(chip + d, chips) * 2 + core
        copy = pltpu.make_async_remote_copy(
            src_ref=x_ref, dst_ref=recv_a.at[d - 1], send_sem=s1.at[d], recv_sem=r1.at[d],
            device_id=_peer(axis, other, peer), device_id_type=MESH,
        )
        copy.start()
        first.append(copy)
    o_ref[chip, core] = x_ref[...]
    forwards = []
    for d in range(1, chips):
        first[d].wait_recv()
        copy = pltpu.make_async_remote_copy(
            src_ref=recv_a.at[d - 1], dst_ref=recv_f.at[d - 1], send_sem=s2.at[d - 1],
            recv_sem=r2.at[d - 1], device_id=sib, device_id_type=MESH,
        )
        copy.start()
        forwards.append(copy)
        o_ref[lax.rem(chip + chips - d, chips), core] = recv_a[d - 1]
    to_sib.wait_recv()
    o_ref[chip, 1 - core] = recv_s[...]
    for d, copy in enumerate(forwards):
        copy.wait_recv()
        o_ref[lax.rem(chip + chips - 1 - d, chips), 1 - core] = recv_f[d]
    for copy in first + forwards:
        copy.wait_send()


def _col_rs_body(axis, other, chips, chip, core, x_ref, o_ref, recv1, mid, recv2, s1, r1, s2, r2):
    sib = _peer(axis, other, _index(axis, chip, 1 - core))
    first = []
    for d in range(1, chips):
        target = lax.rem(chip + d, chips)
        for half, bit in enumerate((core, 1 - core)):
            copy = pltpu.make_async_remote_copy(
                src_ref=x_ref.at[_index(axis, target, bit)],
                dst_ref=recv1.at[d - 1, half],
                send_sem=s1.at[d - 1, half],
                recv_sem=r1.at[d - 1, half],
                device_id=_peer(axis, other, _index(axis, target, core)),
                device_id_type=MESH,
            )
            copy.start()
            first.append(copy)
    for copy in first:
        copy.wait_recv()
    part = x_ref[_index(axis, chip, 1 - core)]
    for d in range(chips - 1):
        part = part + recv1[d, 1]
    mid[...] = part
    last = pltpu.make_async_remote_copy(
        src_ref=mid, dst_ref=recv2, send_sem=s2.at[0], recv_sem=r2.at[0],
        device_id=sib, device_id_type=MESH,
    )
    last.start()
    acc = x_ref[_index(axis, chip, core)]
    for d in range(chips - 1):
        acc = acc + recv1[d, 0]
    last.wait_recv()
    o_ref[...] = acc + recv2[...]
    for copy in first + [last]:
        copy.wait_send()


def _col_ag_body(axis, other, chips, chip, core, x_ref, o_ref, recv_s, recv_a, s1, r1, s2, r2):
    sib = _peer(axis, other, _index(axis, chip, 1 - core))
    to_sib = pltpu.make_async_remote_copy(
        src_ref=x_ref, dst_ref=recv_s, send_sem=s1.at[0], recv_sem=r1.at[0],
        device_id=sib, device_id_type=MESH,
    )
    to_sib.start()
    sends = []
    for d in range(1, chips):
        peer = _peer(axis, other, _index(axis, lax.rem(chip + d, chips), core))
        copy = pltpu.make_async_remote_copy(
            src_ref=x_ref, dst_ref=recv_a.at[d - 1, 0], send_sem=s2.at[d - 1, 0],
            recv_sem=r2.at[d - 1, 0], device_id=peer, device_id_type=MESH,
        )
        copy.start()
        sends.append(copy)
    o_ref[_index(axis, chip, core)] = x_ref[...]
    to_sib.wait_recv()
    for d in range(1, chips):
        peer = _peer(axis, other, _index(axis, lax.rem(chip + d, chips), core))
        copy = pltpu.make_async_remote_copy(
            src_ref=recv_s, dst_ref=recv_a.at[d - 1, 1], send_sem=s2.at[d - 1, 1],
            recv_sem=r2.at[d - 1, 1], device_id=peer, device_id_type=MESH,
        )
        copy.start()
        sends.append(copy)
    o_ref[_index(axis, chip, 1 - core)] = recv_s[...]
    for copy in sends:
        copy.wait_recv()
    for d in range(1, chips):
        source = lax.rem(chip + chips - d, chips)
        o_ref[_index(axis, source, core)] = recv_a[d - 1, 0]
        o_ref[_index(axis, source, 1 - core)] = recv_a[d - 1, 1]
    for copy in [to_sib] + sends:
        copy.wait_send()


def _ar_kernel(axis, other_axis, chips, x_ref, o_ref, g_ref, low, *scratch):
    me = lax.axis_index(axis)
    other = lax.axis_index(other_axis)
    chip, core = _row_greet(axis, me, other, chips)
    _col_rs_body(axis, other, chips, chip, core, x_ref, o_ref, *scratch[:7])
    low[...] = o_ref[...].astype(low.dtype)
    _col_ag_body(axis, other, chips, chip, core, low, g_ref, *scratch[7:])


def _all_reduce(x, axis, other_axis, collective_id):
    n, rows, width = x.shape
    chips = n // 2
    low = jnp.bfloat16
    return pl.pallas_call(
        functools.partial(_ar_kernel, axis, other_axis, chips),
        out_shape=(
            jax.ShapeDtypeStruct((rows, width), x.dtype),
            jax.ShapeDtypeStruct((n, rows, width), low),
        ),
        in_specs=[pl.BlockSpec(memory_space=pltpu.VMEM)],
        out_specs=(pl.BlockSpec(memory_space=pltpu.VMEM), pl.BlockSpec(memory_space=pltpu.VMEM)),
        scratch_shapes=[
            pltpu.VMEM((rows, width), low),
            pltpu.VMEM((chips - 1, 2, rows, width), x.dtype),
            pltpu.VMEM((rows, width), x.dtype),
            pltpu.VMEM((rows, width), x.dtype),
            pltpu.SemaphoreType.DMA((chips - 1, 2)),
            pltpu.SemaphoreType.DMA((chips - 1, 2)),
            pltpu.SemaphoreType.DMA((1,)),
            pltpu.SemaphoreType.DMA((1,)),
            pltpu.VMEM((rows, width), low),
            pltpu.VMEM((chips - 1, 2, rows, width), low),
            pltpu.SemaphoreType.DMA((1,)),
            pltpu.SemaphoreType.DMA((1,)),
            pltpu.SemaphoreType.DMA((chips - 1, 2)),
            pltpu.SemaphoreType.DMA((chips - 1, 2)),
        ],
        compiler_params=pltpu.CompilerParams(collective_id=collective_id, has_side_effects=True),
    )(x)


def _row_reduce_scatter(x, axis, other_axis, collective_id):
    chips, _, rows, width = x.shape
    return pl.pallas_call(
        functools.partial(_row_rs_kernel, axis, other_axis, chips),
        out_shape=jax.ShapeDtypeStruct((rows, width), x.dtype),
        in_specs=[pl.BlockSpec(memory_space=pltpu.VMEM)],
        out_specs=pl.BlockSpec(memory_space=pltpu.VMEM),
        scratch_shapes=[
            pltpu.VMEM((chips, rows, width), x.dtype),
            pltpu.VMEM((chips - 1, rows, width), x.dtype),
            pltpu.VMEM((chips - 1, rows, width), x.dtype),
            pltpu.SemaphoreType.DMA((chips,)),
            pltpu.SemaphoreType.DMA((chips,)),
            pltpu.SemaphoreType.DMA((chips - 1,)),
            pltpu.SemaphoreType.DMA((chips - 1,)),
        ],
        compiler_params=pltpu.CompilerParams(collective_id=collective_id, has_side_effects=True),
    )(x)


def _row_all_gather(x, axis, other_axis, chips, collective_id):
    rows, width = x.shape
    return pl.pallas_call(
        functools.partial(_row_ag_kernel, axis, other_axis, chips),
        out_shape=jax.ShapeDtypeStruct((chips, 2, rows, width), x.dtype),
        in_specs=[pl.BlockSpec(memory_space=pltpu.VMEM)],
        out_specs=pl.BlockSpec(memory_space=pltpu.VMEM),
        scratch_shapes=[
            pltpu.VMEM((rows, width), x.dtype),
            pltpu.VMEM((chips - 1, rows, width), x.dtype),
            pltpu.VMEM((chips - 1, rows, width), x.dtype),
            pltpu.SemaphoreType.DMA((chips,)),
            pltpu.SemaphoreType.DMA((chips,)),
            pltpu.SemaphoreType.DMA((chips - 1,)),
            pltpu.SemaphoreType.DMA((chips - 1,)),
        ],
        compiler_params=pltpu.CompilerParams(collective_id=collective_id, has_side_effects=True),
    )(x)


def _reduce_scatter(x, axis, other_axis, collective_id):
    n, rows, width = x.shape
    return pl.pallas_call(
        functools.partial(_rs_kernel, axis, other_axis, n),
        out_shape=jax.ShapeDtypeStruct((rows, width), x.dtype),
        in_specs=[pl.BlockSpec(memory_space=pltpu.VMEM)],
        out_specs=pl.BlockSpec(memory_space=pltpu.VMEM),
        scratch_shapes=[
            pltpu.VMEM((n - 1, rows, width), x.dtype),
            pltpu.SemaphoreType.DMA((n - 1,)),
            pltpu.SemaphoreType.DMA((n - 1,)),
        ],
        compiler_params=pltpu.CompilerParams(collective_id=collective_id, has_side_effects=True),
    )(x)


def _all_gather(x, axis, other_axis, n, collective_id):
    rows, width = x.shape
    return pl.pallas_call(
        functools.partial(_ag_kernel, axis, other_axis, n),
        out_shape=jax.ShapeDtypeStruct((n, rows, width), x.dtype),
        in_specs=[pl.BlockSpec(memory_space=pltpu.VMEM)],
        out_specs=pl.BlockSpec(memory_space=pltpu.VMEM),
        scratch_shapes=[
            pltpu.VMEM((n - 1, rows, width), x.dtype),
            pltpu.SemaphoreType.DMA((n - 1,)),
            pltpu.SemaphoreType.DMA((n - 1,)),
        ],
        compiler_params=pltpu.CompilerParams(collective_id=collective_id, has_side_effects=True),
    )(x)


def _mask_lanes(mask_ref, nb, bs, width, row=None, col=None):
    blk = lax.broadcasted_iota(jnp.int32, (1, width), 1) // bs
    keep = jnp.zeros((1, width), jnp.int32)
    for b in range(nb):
        value = mask_ref[row, b] if col is None else mask_ref[b, col]
        keep = jnp.where(blk == b, value, keep)
    return keep != 0


def _sub_blocks(nb):
    return 4 if nb % 4 == 0 else (2 if nb % 2 == 0 else 1)


def _sketch_kernel(nb, bs, sub, mask_ref, g_ref, p_ref, o_ref):
    i = pl.program_id(0)
    for h in range(sub):
        keep = _mask_lanes(mask_ref, nb, bs, p_ref.shape[1], row=i * sub + h)
        p = jnp.where(keep, p_ref[...], jnp.zeros_like(p_ref))
        o_ref[:, h * bs:(h + 1) * bs] = lax.dot_general(
            p, g_ref[h * bs:(h + 1) * bs, :], (((1,), (1,)), ((), ())), preferred_element_type=jnp.float32
        )


def _adjoint_kernel(nb, bs, sub, mask_ref, l_ref, g_ref, o_ref):
    j = pl.program_id(0)
    for h in range(sub):
        keep = _mask_lanes(mask_ref, nb, bs, l_ref.shape[1], col=j * sub + h)
        lowered = jnp.where(keep, l_ref[...], jnp.zeros_like(l_ref))
        o_ref[:, h * bs:(h + 1) * bs] = jnp.dot(
            lowered, g_ref[:, h * bs:(h + 1) * bs], preferred_element_type=jnp.float32
        )


def _sketch_partial(mask, green, probes_t):
    rb, cb = mask.shape
    bs = green.shape[0] // rb
    sub = _sub_blocks(rb)
    k = probes_t.shape[0]
    return pl.pallas_call(
        functools.partial(_sketch_kernel, cb, bs, sub),
        out_shape=jax.ShapeDtypeStruct((k, green.shape[0]), jnp.float32),
        grid_spec=pltpu.PrefetchScalarGridSpec(
            num_scalar_prefetch=1,
            grid=(rb // sub,),
            in_specs=[
                pl.BlockSpec((bs * sub, green.shape[1]), lambda i, m: (i, 0)),
                pl.BlockSpec((k, green.shape[1]), lambda i, m: (0, 0)),
            ],
            out_specs=pl.BlockSpec((k, bs * sub), lambda i, m: (0, i)),
        ),
    )(mask, green, probes_t)


def _adjoint_partial(mask, lowered_t, green):
    rb, cb = mask.shape
    bs = green.shape[0] // rb
    sub = _sub_blocks(cb)
    k = lowered_t.shape[0]
    return pl.pallas_call(
        functools.partial(_adjoint_kernel, rb, bs, sub),
        out_shape=jax.ShapeDtypeStruct((k, green.shape[1]), jnp.float32),
        grid_spec=pltpu.PrefetchScalarGridSpec(
            num_scalar_prefetch=1,
            grid=(cb // sub,),
            in_specs=[
                pl.BlockSpec((k, green.shape[0]), lambda j, m: (0, 0)),
                pl.BlockSpec((green.shape[0], bs * sub), lambda j, m: (0, j)),
            ],
            out_specs=pl.BlockSpec((k, bs * sub), lambda j, m: (0, j)),
        ),
    )(mask, lowered_t, green)


def local(green, mask, probes):
    n_row = lax.axis_size("row")
    n_col = lax.axis_size("col")
    probes_t = _row_all_gather(probes.T, "row", "col", n_row // 2, 3)
    k = n_row * probes_t.shape[2]
    probes_t = probes_t.reshape(k, -1)
    partial_t = _sketch_partial(mask, green, probes_t)
    sketch_t, lowered_t = _all_reduce(partial_t.reshape(n_col, k // n_col, -1), "col", "row", 0)
    lowered_t = lowered_t.reshape(k, -1)
    term_t = _adjoint_partial(mask, lowered_t, green)
    adjoint_t = _row_reduce_scatter(term_t.reshape(n_row // 2, 2, k // n_row, -1), "row", "col", 2)
    return (sketch_t.T, adjoint_t.T)


def solution(mesh):
    in_specs = (P("row", "col"), P("row", "col"), P("col", "row"))
    out_specs = (P("row", "col"), P("col", "row"))
    return jax.shard_map(local, mesh=mesh, in_specs=in_specs, out_specs=out_specs, check_vma=False)
```

```python
import functools

import jax
import jax.numpy as jnp
from jax import lax
from jax.experimental import pallas as pl
from jax.experimental.pallas import tpu as pltpu
from jax.sharding import PartitionSpec as P

MESH = pl.DeviceIdType.MESH


def _peer(axis, other, p):
    return (other, p) if axis == "col" else (p, other)


def _greet(axis, other, me, n):
    barrier = pltpu.get_barrier_semaphore()
    for d in range(1, n):
        peer = _peer(axis, other, lax.rem(me + d, n))
        pl.semaphore_signal(barrier, 1, device_id=peer, device_id_type=MESH)
    pl.semaphore_wait(barrier, n - 1)


def _rs_kernel(axis, other_axis, n, x_ref, o_ref, recv, send_sem, recv_sem):
    me = lax.axis_index(axis)
    other = lax.axis_index(other_axis)
    _greet(axis, other, me, n)
    copies = []
    for d in range(1, n):
        peer = lax.rem(me + d, n)
        copy = pltpu.make_async_remote_copy(
            src_ref=x_ref.at[peer],
            dst_ref=recv.at[d - 1],
            send_sem=send_sem.at[d - 1],
            recv_sem=recv_sem.at[d - 1],
            device_id=_peer(axis, other, peer),
            device_id_type=MESH,
        )
        copy.start()
        copies.append(copy)
    acc = x_ref[me]
    for d, copy in enumerate(copies):
        copy.wait_recv()
        acc = acc + recv[d]
    for copy in copies:
        copy.wait_send()
    o_ref[...] = acc


def _ag_kernel(axis, other_axis, n, x_ref, o_ref, recv, send_sem, recv_sem):
    me = lax.axis_index(axis)
    other = lax.axis_index(other_axis)
    _greet(axis, other, me, n)
    copies = []
    for d in range(1, n):
        peer = lax.rem(me + d, n)
        copy = pltpu.make_async_remote_copy(
            src_ref=x_ref,
            dst_ref=recv.at[d - 1],
            send_sem=send_sem.at[d - 1],
            recv_sem=recv_sem.at[d - 1],
            device_id=_peer(axis, other, peer),
            device_id_type=MESH,
        )
        copy.start()
        copies.append(copy)
    o_ref[me] = x_ref[...]
    for d, copy in enumerate(copies):
        copy.wait_recv()
        o_ref[lax.rem(me + n - 1 - d, n)] = recv[d]
    for copy in copies:
        copy.wait_send()


def _row_greet(axis, me, other, chips):
    chip, core = me // 2, lax.rem(me, 2)
    barrier = pltpu.get_barrier_semaphore()
    pl.semaphore_signal(barrier, 1, device_id=_peer(axis, other, chip * 2 + 1 - core), device_id_type=MESH)
    for d in range(1, chips):
        peer = lax.rem(chip + d, chips) * 2 + core
        pl.semaphore_signal(barrier, 1, device_id=_peer(axis, other, peer), device_id_type=MESH)
    pl.semaphore_wait(barrier, chips)
    return chip, core


def _row_rs_kernel(axis, other_axis, chips, x_ref, o_ref, recv1, mid, recv2, s1, r1, s2, r2):
    me = lax.axis_index(axis)
    other = lax.axis_index(other_axis)
    chip, core = _row_greet(axis, me, other, chips)
    _rs_body(axis, other, chips, chip, core, x_ref, o_ref, recv1, mid, recv2, s1, r1, s2, r2)


def _rs_body(axis, other, chips, chip, core, x_ref, o_ref, recv1, mid, recv2, s1, r1, s2, r2):
    sib = _peer(axis, other, chip * 2 + 1 - core)
    first = []
    for q in range(chips):
        copy = pltpu.make_async_remote_copy(
            src_ref=x_ref.at[q, 1 - core],
            dst_ref=recv1.at[q],
            send_sem=s1.at[q],
            recv_sem=r1.at[q],
            device_id=sib,
            device_id_type=MESH,
        )
        copy.start()
        first.append(copy)
    for q in range(chips):
        first[q].wait_recv()
    for d in range(1, chips):
        target = lax.rem(chip + d, chips)
        mid[d - 1] = x_ref[target, core] + recv1[target]
    sends = []
    for d in range(1, chips):
        target = lax.rem(chip + d, chips)
        copy = pltpu.make_async_remote_copy(
            src_ref=mid.at[d - 1],
            dst_ref=recv2.at[d - 1],
            send_sem=s2.at[d - 1],
            recv_sem=r2.at[d - 1],
            device_id=_peer(axis, other, target * 2 + core),
            device_id_type=MESH,
        )
        copy.start()
        sends.append(copy)
    acc = x_ref[chip, core] + recv1[chip]
    for d, copy in enumerate(sends):
        copy.wait_recv()
        acc = acc + recv2[d]
    for copy in first + sends:
        copy.wait_send()
    o_ref[...] = acc


def _row_ag_kernel(axis, other_axis, chips, x_ref, o_ref, recv_s, recv_a, recv_f, s1, r1, s2, r2):
    me = lax.axis_index(axis)
    other = lax.axis_index(other_axis)
    chip, core = _row_greet(axis, me, other, chips)
    _ag_body(axis, other, chips, chip, core, x_ref, o_ref, recv_s, recv_a, recv_f, s1, r1, s2, r2)


def _ag_body(axis, other, chips, chip, core, x_ref, o_ref, recv_s, recv_a, recv_f, s1, r1, s2, r2):
    sib = _peer(axis, other, chip * 2 + 1 - core)
    to_sib = pltpu.make_async_remote_copy(
        src_ref=x_ref, dst_ref=recv_s, send_sem=s1.at[0], recv_sem=r1.at[0],
        device_id=sib, device_id_type=MESH,
    )
    to_sib.start()
    first = [to_sib]
    for d in range(1, chips):
        peer = lax.rem(chip + d, chips) * 2 + core
        copy = pltpu.make_async_remote_copy(
            src_ref=x_ref, dst_ref=recv_a.at[d - 1], send_sem=s1.at[d], recv_sem=r1.at[d],
            device_id=_peer(axis, other, peer), device_id_type=MESH,
        )
        copy.start()
        first.append(copy)
    o_ref[chip, core] = x_ref[...]
    forwards = []
    for d in range(1, chips):
        first[d].wait_recv()
        copy = pltpu.make_async_remote_copy(
            src_ref=recv_a.at[d - 1], dst_ref=recv_f.at[d - 1], send_sem=s2.at[d - 1],
            recv_sem=r2.at[d - 1], device_id=sib, device_id_type=MESH,
        )
        copy.start()
        forwards.append(copy)
        o_ref[lax.rem(chip + chips - d, chips), core] = recv_a[d - 1]
    to_sib.wait_recv()
    o_ref[chip, 1 - core] = recv_s[...]
    for d, copy in enumerate(forwards):
        copy.wait_recv()
        o_ref[lax.rem(chip + chips - 1 - d, chips), 1 - core] = recv_f[d]
    for copy in first + forwards:
        copy.wait_send()


def _mixed_rs_body(axis, other, chips, chip, core, x_ref, o_ref, ra1, ma, ra2, rb1, mb, rb2,
                   sa1, qa1, sa2, qa2, sb1, qb1, sb2, qb2):
    sib = _peer(axis, other, chip * 2 + 1 - core)
    width = x_ref.shape[-1]
    a1 = []
    for q in range(chips):
        copy = pltpu.make_async_remote_copy(
            src_ref=x_ref.at[0, q * 2 + 1 - core], dst_ref=ra1.at[q], send_sem=sa1.at[q],
            recv_sem=qa1.at[q], device_id=sib, device_id_type=MESH,
        )
        copy.start()
        a1.append(copy)
    b1 = []
    for d in range(1, chips):
        target = lax.rem(chip + d, chips)
        for half, bit in enumerate((core, 1 - core)):
            copy = pltpu.make_async_remote_copy(
                src_ref=x_ref.at[1, target * 2 + bit], dst_ref=rb1.at[d - 1, half],
                send_sem=sb1.at[d - 1, half], recv_sem=qb1.at[d - 1, half],
                device_id=_peer(axis, other, target * 2 + core), device_id_type=MESH,
            )
            copy.start()
            b1.append(copy)
    for copy in a1:
        copy.wait_recv()
    a2 = []
    for d in range(1, chips):
        target = lax.rem(chip + d, chips)
        ma[d - 1] = x_ref[0, target * 2 + core] + ra1[target]
        copy = pltpu.make_async_remote_copy(
            src_ref=ma.at[d - 1], dst_ref=ra2.at[d - 1], send_sem=sa2.at[d - 1],
            recv_sem=qa2.at[d - 1], device_id=_peer(axis, other, target * 2 + core),
            device_id_type=MESH,
        )
        copy.start()
        a2.append(copy)
    for copy in b1:
        copy.wait_recv()
    part = x_ref[1, chip * 2 + 1 - core]
    for d in range(chips - 1):
        part = part + rb1[d, 1]
    mb[...] = part
    b2 = pltpu.make_async_remote_copy(
        src_ref=mb, dst_ref=rb2, send_sem=sb2.at[0], recv_sem=qb2.at[0],
        device_id=sib, device_id_type=MESH,
    )
    b2.start()
    acc_b = x_ref[1, chip * 2 + core]
    for d in range(chips - 1):
        acc_b = acc_b + rb1[d, 0]
    acc_a = x_ref[0, chip * 2 + core] + ra1[chip]
    for d, copy in enumerate(a2):
        copy.wait_recv()
        acc_a = acc_a + ra2[d]
    b2.wait_recv()
    o_ref[:, :width] = acc_a
    o_ref[:, width:] = acc_b + rb2[...]
    for copy in a1 + b1 + a2 + [b2]:
        copy.wait_send()


def _ar_kernel(axis, other_axis, chips, x_ref, o_ref, g_ref, low, *scratch):
    me = lax.axis_index(axis)
    other = lax.axis_index(other_axis)
    chip, core = _row_greet(axis, me, other, chips)
    _mixed_rs_body(axis, other, chips, chip, core, x_ref, o_ref, *scratch[:14])
    low[...] = o_ref[...].astype(low.dtype)
    _ag_body(axis, other, chips, chip, core, low, g_ref, *scratch[14:])


def _all_reduce(x, axis, other_axis, collective_id):
    _, n, rows, half = x.shape
    chips = n // 2
    width = 2 * half
    low = jnp.bfloat16
    return pl.pallas_call(
        functools.partial(_ar_kernel, axis, other_axis, chips),
        out_shape=(
            jax.ShapeDtypeStruct((rows, width), x.dtype),
            jax.ShapeDtypeStruct((chips, 2, rows, width), low),
        ),
        in_specs=[pl.BlockSpec(memory_space=pltpu.VMEM)],
        out_specs=(pl.BlockSpec(memory_space=pltpu.VMEM), pl.BlockSpec(memory_space=pltpu.VMEM)),
        scratch_shapes=[
            pltpu.VMEM((rows, width), low),
            pltpu.VMEM((chips, rows, half), x.dtype),
            pltpu.VMEM((chips - 1, rows, half), x.dtype),
            pltpu.VMEM((chips - 1, rows, half), x.dtype),
            pltpu.VMEM((chips - 1, 2, rows, half), x.dtype),
            pltpu.VMEM((rows, half), x.dtype),
            pltpu.VMEM((rows, half), x.dtype),
            pltpu.SemaphoreType.DMA((chips,)),
            pltpu.SemaphoreType.DMA((chips,)),
            pltpu.SemaphoreType.DMA((chips - 1,)),
            pltpu.SemaphoreType.DMA((chips - 1,)),
            pltpu.SemaphoreType.DMA((chips - 1, 2)),
            pltpu.SemaphoreType.DMA((chips - 1, 2)),
            pltpu.SemaphoreType.DMA((1,)),
            pltpu.SemaphoreType.DMA((1,)),
            pltpu.VMEM((rows, width), low),
            pltpu.VMEM((chips - 1, rows, width), low),
            pltpu.VMEM((chips - 1, rows, width), low),
            pltpu.SemaphoreType.DMA((chips,)),
            pltpu.SemaphoreType.DMA((chips,)),
            pltpu.SemaphoreType.DMA((chips - 1,)),
            pltpu.SemaphoreType.DMA((chips - 1,)),
        ],
        compiler_params=pltpu.CompilerParams(collective_id=collective_id, has_side_effects=True),
    )(x)


def _row_reduce_scatter(x, axis, other_axis, collective_id):
    chips, _, rows, width = x.shape
    return pl.pallas_call(
        functools.partial(_row_rs_kernel, axis, other_axis, chips),
        out_shape=jax.ShapeDtypeStruct((rows, width), x.dtype),
        in_specs=[pl.BlockSpec(memory_space=pltpu.VMEM)],
        out_specs=pl.BlockSpec(memory_space=pltpu.VMEM),
        scratch_shapes=[
            pltpu.VMEM((chips, rows, width), x.dtype),
            pltpu.VMEM((chips - 1, rows, width), x.dtype),
            pltpu.VMEM((chips - 1, rows, width), x.dtype),
            pltpu.SemaphoreType.DMA((chips,)),
            pltpu.SemaphoreType.DMA((chips,)),
            pltpu.SemaphoreType.DMA((chips - 1,)),
            pltpu.SemaphoreType.DMA((chips - 1,)),
        ],
        compiler_params=pltpu.CompilerParams(collective_id=collective_id, has_side_effects=True),
    )(x)


def _row_all_gather(x, axis, other_axis, chips, collective_id):
    rows, width = x.shape
    return pl.pallas_call(
        functools.partial(_row_ag_kernel, axis, other_axis, chips),
        out_shape=jax.ShapeDtypeStruct((chips, 2, rows, width), x.dtype),
        in_specs=[pl.BlockSpec(memory_space=pltpu.VMEM)],
        out_specs=pl.BlockSpec(memory_space=pltpu.VMEM),
        scratch_shapes=[
            pltpu.VMEM((rows, width), x.dtype),
            pltpu.VMEM((chips - 1, rows, width), x.dtype),
            pltpu.VMEM((chips - 1, rows, width), x.dtype),
            pltpu.SemaphoreType.DMA((chips,)),
            pltpu.SemaphoreType.DMA((chips,)),
            pltpu.SemaphoreType.DMA((chips - 1,)),
            pltpu.SemaphoreType.DMA((chips - 1,)),
        ],
        compiler_params=pltpu.CompilerParams(collective_id=collective_id, has_side_effects=True),
    )(x)


def _reduce_scatter(x, axis, other_axis, collective_id):
    n, rows, width = x.shape
    return pl.pallas_call(
        functools.partial(_rs_kernel, axis, other_axis, n),
        out_shape=jax.ShapeDtypeStruct((rows, width), x.dtype),
        in_specs=[pl.BlockSpec(memory_space=pltpu.VMEM)],
        out_specs=pl.BlockSpec(memory_space=pltpu.VMEM),
        scratch_shapes=[
            pltpu.VMEM((n - 1, rows, width), x.dtype),
            pltpu.SemaphoreType.DMA((n - 1,)),
            pltpu.SemaphoreType.DMA((n - 1,)),
        ],
        compiler_params=pltpu.CompilerParams(collective_id=collective_id, has_side_effects=True),
    )(x)


def _all_gather(x, axis, other_axis, n, collective_id):
    rows, width = x.shape
    return pl.pallas_call(
        functools.partial(_ag_kernel, axis, other_axis, n),
        out_shape=jax.ShapeDtypeStruct((n, rows, width), x.dtype),
        in_specs=[pl.BlockSpec(memory_space=pltpu.VMEM)],
        out_specs=pl.BlockSpec(memory_space=pltpu.VMEM),
        scratch_shapes=[
            pltpu.VMEM((n - 1, rows, width), x.dtype),
            pltpu.SemaphoreType.DMA((n - 1,)),
            pltpu.SemaphoreType.DMA((n - 1,)),
        ],
        compiler_params=pltpu.CompilerParams(collective_id=collective_id, has_side_effects=True),
    )(x)


def _mask_lanes(mask_ref, nb, bs, width, row=None, col=None):
    blk = lax.broadcasted_iota(jnp.int32, (1, width), 1) // bs
    keep = jnp.zeros((1, width), jnp.int32)
    for b in range(nb):
        value = mask_ref[row, b] if col is None else mask_ref[b, col]
        keep = jnp.where(blk == b, value, keep)
    return keep != 0


def _sub_blocks(nb):
    return 4 if nb % 4 == 0 else (2 if nb % 2 == 0 else 1)


def _half_blocks(nb):
    return nb // 2


def _sketch_kernel(nb, bs, sub, mask_ref, g_ref, p_ref, o_ref):
    i = pl.program_id(0)
    for h in range(sub):
        keep = _mask_lanes(mask_ref, nb, bs, p_ref.shape[1], row=i * sub + h)
        p = jnp.where(keep, p_ref[...], jnp.zeros_like(p_ref))
        o_ref[:, h * bs:(h + 1) * bs] = lax.dot_general(
            p, g_ref[h * bs:(h + 1) * bs, :], (((1,), (1,)), ((), ())), preferred_element_type=jnp.float32
        )


def _adjoint_kernel(nb, bs, sub, mask_ref, l_ref, g_ref, o_ref):
    j = pl.program_id(0)
    for h in range(sub):
        keep = _mask_lanes(mask_ref, nb, bs, l_ref.shape[1], col=j * sub + h)
        lowered = jnp.where(keep, l_ref[...], jnp.zeros_like(l_ref))
        o_ref[:, h * bs:(h + 1) * bs] = jnp.dot(
            lowered, g_ref[:, h * bs:(h + 1) * bs], preferred_element_type=jnp.float32
        )


def _sketch_partial(mask, green, probes_t):
    rb, cb = mask.shape
    bs = green.shape[0] // rb
    sub = _half_blocks(rb)
    k = probes_t.shape[0]
    return pl.pallas_call(
        functools.partial(_sketch_kernel, cb, bs, sub),
        out_shape=jax.ShapeDtypeStruct((rb // sub, k, bs * sub), jnp.float32),
        grid_spec=pltpu.PrefetchScalarGridSpec(
            num_scalar_prefetch=1,
            grid=(rb // sub,),
            in_specs=[
                pl.BlockSpec((bs * sub, green.shape[1]), lambda i, m: (i, 0)),
                pl.BlockSpec((k, green.shape[1]), lambda i, m: (0, 0)),
            ],
            out_specs=pl.BlockSpec((None, k, bs * sub), lambda i, m: (i, 0, 0)),
        ),
    )(mask, green, probes_t)


def _adjoint_partial(mask, lowered_t, green):
    rb, cb = mask.shape
    bs = green.shape[0] // rb
    sub = _sub_blocks(cb)
    k = lowered_t.shape[0]
    return pl.pallas_call(
        functools.partial(_adjoint_kernel, rb, bs, sub),
        out_shape=jax.ShapeDtypeStruct((k, green.shape[1]), jnp.float32),
        grid_spec=pltpu.PrefetchScalarGridSpec(
            num_scalar_prefetch=1,
            grid=(cb // sub,),
            in_specs=[
                pl.BlockSpec((k, green.shape[0]), lambda j, m: (0, 0)),
                pl.BlockSpec((green.shape[0], bs * sub), lambda j, m: (0, j)),
            ],
            out_specs=pl.BlockSpec((k, bs * sub), lambda j, m: (0, j)),
        ),
    )(mask, lowered_t, green)


def local(green, mask, probes):
    n_row = lax.axis_size("row")
    n_col = lax.axis_size("col")
    probes_t = _row_all_gather(probes.T, "row", "col", n_row // 2, 3)
    k = n_row * probes_t.shape[2]
    probes_t = probes_t.reshape(k, -1)
    partial_t = _sketch_partial(mask, green, probes_t)
    sketch_t, lowered_t = _all_reduce(partial_t.reshape(2, n_col, k // n_col, -1), "col", "row", 0)
    lowered_t = lowered_t.reshape(k, -1)
    term_t = _adjoint_partial(mask, lowered_t, green)
    adjoint_t = _row_reduce_scatter(term_t.reshape(n_row // 2, 2, k // n_row, -1), "row", "col", 2)
    return (sketch_t.T, adjoint_t.T)


def solution(mesh):
    in_specs = (P("row", "col"), P("row", "col"), P("col", "row"))
    out_specs = (P("row", "col"), P("col", "row"))
    return jax.shard_map(local, mesh=mesh, in_specs=in_specs, out_specs=out_specs, check_vma=False)
```

```python
import functools

import jax
import jax.numpy as jnp
from jax import lax
from jax.experimental import pallas as pl
from jax.experimental.pallas import tpu as pltpu
from jax.sharding import PartitionSpec as P

MESH = pl.DeviceIdType.MESH


def _peer(axis, other, p):
    return (other, p) if axis == "col" else (p, other)


def _greet(axis, other, me, n):
    barrier = pltpu.get_barrier_semaphore()
    for d in range(1, n):
        peer = _peer(axis, other, lax.rem(me + d, n))
        pl.semaphore_signal(barrier, 1, device_id=peer, device_id_type=MESH)
    pl.semaphore_wait(barrier, n - 1)


def _rs_kernel(axis, other_axis, n, x_ref, o_ref, recv, send_sem, recv_sem):
    me = lax.axis_index(axis)
    other = lax.axis_index(other_axis)
    _greet(axis, other, me, n)
    copies = []
    for d in range(1, n):
        peer = lax.rem(me + d, n)
        copy = pltpu.make_async_remote_copy(
            src_ref=x_ref.at[peer],
            dst_ref=recv.at[d - 1],
            send_sem=send_sem.at[d - 1],
            recv_sem=recv_sem.at[d - 1],
            device_id=_peer(axis, other, peer),
            device_id_type=MESH,
        )
        copy.start()
        copies.append(copy)
    acc = x_ref[me]
    for d, copy in enumerate(copies):
        copy.wait_recv()
        acc = acc + recv[d]
    for copy in copies:
        copy.wait_send()
    o_ref[...] = acc


def _ag_kernel(axis, other_axis, n, x_ref, o_ref, recv, send_sem, recv_sem):
    me = lax.axis_index(axis)
    other = lax.axis_index(other_axis)
    _greet(axis, other, me, n)
    copies = []
    for d in range(1, n):
        peer = lax.rem(me + d, n)
        copy = pltpu.make_async_remote_copy(
            src_ref=x_ref,
            dst_ref=recv.at[d - 1],
            send_sem=send_sem.at[d - 1],
            recv_sem=recv_sem.at[d - 1],
            device_id=_peer(axis, other, peer),
            device_id_type=MESH,
        )
        copy.start()
        copies.append(copy)
    o_ref[me] = x_ref[...]
    for d, copy in enumerate(copies):
        copy.wait_recv()
        o_ref[lax.rem(me + n - 1 - d, n)] = recv[d]
    for copy in copies:
        copy.wait_send()


def _row_greet(axis, me, other, chips):
    chip, core = me // 2, lax.rem(me, 2)
    barrier = pltpu.get_barrier_semaphore()
    pl.semaphore_signal(barrier, 1, device_id=_peer(axis, other, chip * 2 + 1 - core), device_id_type=MESH)
    for d in range(1, chips):
        peer = lax.rem(chip + d, chips) * 2 + core
        pl.semaphore_signal(barrier, 1, device_id=_peer(axis, other, peer), device_id_type=MESH)
    pl.semaphore_wait(barrier, chips)
    return chip, core


def _row_rs_kernel(axis, other_axis, chips, x_ref, o_ref, recv1, mid, recv2, s1, r1, s2, r2):
    me = lax.axis_index(axis)
    other = lax.axis_index(other_axis)
    chip, core = _row_greet(axis, me, other, chips)
    _rs_body(axis, other, chips, chip, core, x_ref, o_ref, recv1, mid, recv2, s1, r1, s2, r2)


def _rs_body(axis, other, chips, chip, core, x_ref, o_ref, recv1, mid, recv2, s1, r1, s2, r2):
    sib = _peer(axis, other, chip * 2 + 1 - core)
    first = []
    for q in range(chips):
        copy = pltpu.make_async_remote_copy(
            src_ref=x_ref.at[q, 1 - core],
            dst_ref=recv1.at[q],
            send_sem=s1.at[q],
            recv_sem=r1.at[q],
            device_id=sib,
            device_id_type=MESH,
        )
        copy.start()
        first.append(copy)
    for q in range(chips):
        first[q].wait_recv()
    for d in range(1, chips):
        target = lax.rem(chip + d, chips)
        mid[d - 1] = x_ref[target, core] + recv1[target]
    sends = []
    for d in range(1, chips):
        target = lax.rem(chip + d, chips)
        copy = pltpu.make_async_remote_copy(
            src_ref=mid.at[d - 1],
            dst_ref=recv2.at[d - 1],
            send_sem=s2.at[d - 1],
            recv_sem=r2.at[d - 1],
            device_id=_peer(axis, other, target * 2 + core),
            device_id_type=MESH,
        )
        copy.start()
        sends.append(copy)
    acc = x_ref[chip, core] + recv1[chip]
    for d, copy in enumerate(sends):
        copy.wait_recv()
        acc = acc + recv2[d]
    for copy in first + sends:
        copy.wait_send()
    o_ref[...] = acc


def _row_ag_kernel(axis, other_axis, chips, x_ref, o_ref, recv_s, recv_a, recv_f, s1, r1, s2, r2):
    me = lax.axis_index(axis)
    other = lax.axis_index(other_axis)
    chip, core = _row_greet(axis, me, other, chips)
    _ag_body(axis, other, chips, chip, core, x_ref, o_ref, recv_s, recv_a, recv_f, s1, r1, s2, r2)


def _ag_body(axis, other, chips, chip, core, x_ref, o_ref, recv_s, recv_a, recv_f, s1, r1, s2, r2):
    sib = _peer(axis, other, chip * 2 + 1 - core)
    to_sib = pltpu.make_async_remote_copy(
        src_ref=x_ref, dst_ref=recv_s, send_sem=s1.at[0], recv_sem=r1.at[0],
        device_id=sib, device_id_type=MESH,
    )
    to_sib.start()
    first = [to_sib]
    for d in range(1, chips):
        peer = lax.rem(chip + d, chips) * 2 + core
        copy = pltpu.make_async_remote_copy(
            src_ref=x_ref, dst_ref=recv_a.at[d - 1], send_sem=s1.at[d], recv_sem=r1.at[d],
            device_id=_peer(axis, other, peer), device_id_type=MESH,
        )
        copy.start()
        first.append(copy)
    o_ref[chip, core] = x_ref[...]
    forwards = []
    for d in range(1, chips):
        first[d].wait_recv()
        copy = pltpu.make_async_remote_copy(
            src_ref=recv_a.at[d - 1], dst_ref=recv_f.at[d - 1], send_sem=s2.at[d - 1],
            recv_sem=r2.at[d - 1], device_id=sib, device_id_type=MESH,
        )
        copy.start()
        forwards.append(copy)
        o_ref[lax.rem(chip + chips - d, chips), core] = recv_a[d - 1]
    to_sib.wait_recv()
    o_ref[chip, 1 - core] = recv_s[...]
    for d, copy in enumerate(forwards):
        copy.wait_recv()
        o_ref[lax.rem(chip + chips - 1 - d, chips), 1 - core] = recv_f[d]
    for copy in first + forwards:
        copy.wait_send()


def _mixed_rs_body(axis, other, chips, chip, core, x_ref, o_ref, ra1, ma, ra2, rb1, mb, rb2,
                   sa1, qa1, sa2, qa2, sb1, qb1, sb2, qb2):
    sib = _peer(axis, other, chip * 2 + 1 - core)
    width = x_ref.shape[-1]
    a1 = []
    for q in range(chips):
        copy = pltpu.make_async_remote_copy(
            src_ref=x_ref.at[0, q * 2 + 1 - core], dst_ref=ra1.at[q], send_sem=sa1.at[q],
            recv_sem=qa1.at[q], device_id=sib, device_id_type=MESH,
        )
        copy.start()
        a1.append(copy)
    b1 = []
    for d in range(1, chips):
        target = lax.rem(chip + d, chips)
        for half, bit in enumerate((core, 1 - core)):
            copy = pltpu.make_async_remote_copy(
                src_ref=x_ref.at[1, target * 2 + bit], dst_ref=rb1.at[d - 1, half],
                send_sem=sb1.at[d - 1, half], recv_sem=qb1.at[d - 1, half],
                device_id=_peer(axis, other, target * 2 + core), device_id_type=MESH,
            )
            copy.start()
            b1.append(copy)
    for copy in a1:
        copy.wait_recv()
    a2 = []
    for d in range(1, chips):
        target = lax.rem(chip + d, chips)
        ma[d - 1] = x_ref[0, target * 2 + core] + ra1[target]
        copy = pltpu.make_async_remote_copy(
            src_ref=ma.at[d - 1], dst_ref=ra2.at[d - 1], send_sem=sa2.at[d - 1],
            recv_sem=qa2.at[d - 1], device_id=_peer(axis, other, target * 2 + core),
            device_id_type=MESH,
        )
        copy.start()
        a2.append(copy)
    for copy in b1:
        copy.wait_recv()
    part = x_ref[1, chip * 2 + 1 - core]
    for d in range(chips - 1):
        part = part + rb1[d, 1]
    mb[...] = part
    b2 = pltpu.make_async_remote_copy(
        src_ref=mb, dst_ref=rb2, send_sem=sb2.at[0], recv_sem=qb2.at[0],
        device_id=sib, device_id_type=MESH,
    )
    b2.start()
    acc_b = x_ref[1, chip * 2 + core]
    for d in range(chips - 1):
        acc_b = acc_b + rb1[d, 0]
    acc_a = x_ref[0, chip * 2 + core] + ra1[chip]
    for d, copy in enumerate(a2):
        copy.wait_recv()
        acc_a = acc_a + ra2[d]
    b2.wait_recv()
    o_ref[:, :width] = acc_a
    o_ref[:, width:] = acc_b + rb2[...]
    for copy in a1 + b1 + a2 + [b2]:
        copy.wait_send()


def _mixed_ag_body(axis, other, chips, chip, core, low, o_ref, ra, fa, rbs, rb,
                   sa, qa, sf, qf, ss, qs, sb, qb):
    sib = _peer(axis, other, chip * 2 + 1 - core)
    width = low.shape[-1]

    def peer(d):
        return _peer(axis, other, lax.rem(chip + d, chips) * 2 + core)

    a1 = []
    for d in range(1, chips):
        copy = pltpu.make_async_remote_copy(
            src_ref=low.at[0], dst_ref=ra.at[d - 1], send_sem=sa.at[d - 1], recv_sem=qa.at[d - 1],
            device_id=peer(d), device_id_type=MESH,
        )
        copy.start()
        a1.append(copy)
    b1 = pltpu.make_async_remote_copy(
        src_ref=low.at[1], dst_ref=rbs, send_sem=ss.at[0], recv_sem=qs.at[0],
        device_id=sib, device_id_type=MESH,
    )
    b1.start()
    own_a = pltpu.make_async_remote_copy(
        src_ref=low.at[0], dst_ref=fa.at[chips - 1], send_sem=sf.at[chips - 1],
        recv_sem=qf.at[chips - 1], device_id=sib, device_id_type=MESH,
    )
    own_a.start()
    me = chip * 2 + core
    o_ref[me, :, :width] = low[0]
    o_ref[me, :, width:] = low[1]
    b1.wait_recv()
    b2 = []
    for d in range(1, chips):
        for half, src in enumerate((low.at[1], rbs)):
            copy = pltpu.make_async_remote_copy(
                src_ref=src, dst_ref=rb.at[d - 1, half], send_sem=sb.at[d - 1, half],
                recv_sem=qb.at[d - 1, half], device_id=peer(d), device_id_type=MESH,
            )
            copy.start()
            b2.append(copy)
    a2 = []
    for d in range(1, chips):
        a1[d - 1].wait_recv()
        copy = pltpu.make_async_remote_copy(
            src_ref=ra.at[d - 1], dst_ref=fa.at[d - 1], send_sem=sf.at[d - 1], recv_sem=qf.at[d - 1],
            device_id=sib, device_id_type=MESH,
        )
        copy.start()
        a2.append(copy)
    mate = chip * 2 + 1 - core
    o_ref[mate, :, width:] = rbs[...]
    own_a.wait_recv()
    o_ref[mate, :, :width] = fa[chips - 1]
    for copy in a2 + b2:
        copy.wait_recv()
    for d in range(1, chips):
        source = lax.rem(chip + chips - d, chips)
        o_ref[source * 2 + core, :, :width] = ra[d - 1]
        o_ref[source * 2 + core, :, width:] = rb[d - 1, 0]
        o_ref[source * 2 + 1 - core, :, :width] = fa[d - 1]
        o_ref[source * 2 + 1 - core, :, width:] = rb[d - 1, 1]
    for copy in a1 + [b1, own_a] + b2 + a2:
        copy.wait_send()


def _ar_kernel(axis, other_axis, chips, x_ref, o_ref, g_ref, low, *scratch):
    me = lax.axis_index(axis)
    other = lax.axis_index(other_axis)
    chip, core = _row_greet(axis, me, other, chips)
    _mixed_rs_body(axis, other, chips, chip, core, x_ref, o_ref, *scratch[:14])
    half = low.shape[-1]
    low[0] = o_ref[:, :half].astype(low.dtype)
    low[1] = o_ref[:, half:].astype(low.dtype)
    _mixed_ag_body(axis, other, chips, chip, core, low, g_ref, *scratch[14:])


def _all_reduce(x, axis, other_axis, collective_id):
    _, n, rows, half = x.shape
    chips = n // 2
    width = 2 * half
    low = jnp.bfloat16
    return pl.pallas_call(
        functools.partial(_ar_kernel, axis, other_axis, chips),
        out_shape=(
            jax.ShapeDtypeStruct((rows, width), x.dtype),
            jax.ShapeDtypeStruct((n, rows, width), low),
        ),
        in_specs=[pl.BlockSpec(memory_space=pltpu.VMEM)],
        out_specs=(pl.BlockSpec(memory_space=pltpu.VMEM), pl.BlockSpec(memory_space=pltpu.VMEM)),
        scratch_shapes=[
            pltpu.VMEM((2, rows, half), low),
            pltpu.VMEM((chips, rows, half), x.dtype),
            pltpu.VMEM((chips - 1, rows, half), x.dtype),
            pltpu.VMEM((chips - 1, rows, half), x.dtype),
            pltpu.VMEM((chips - 1, 2, rows, half), x.dtype),
            pltpu.VMEM((rows, half), x.dtype),
            pltpu.VMEM((rows, half), x.dtype),
            pltpu.SemaphoreType.DMA((chips,)),
            pltpu.SemaphoreType.DMA((chips,)),
            pltpu.SemaphoreType.DMA((chips - 1,)),
            pltpu.SemaphoreType.DMA((chips - 1,)),
            pltpu.SemaphoreType.DMA((chips - 1, 2)),
            pltpu.SemaphoreType.DMA((chips - 1, 2)),
            pltpu.SemaphoreType.DMA((1,)),
            pltpu.SemaphoreType.DMA((1,)),
            pltpu.VMEM((chips - 1, rows, half), low),
            pltpu.VMEM((chips, rows, half), low),
            pltpu.VMEM((rows, half), low),
            pltpu.VMEM((chips - 1, 2, rows, half), low),
            pltpu.SemaphoreType.DMA((chips - 1,)),
            pltpu.SemaphoreType.DMA((chips - 1,)),
            pltpu.SemaphoreType.DMA((chips,)),
            pltpu.SemaphoreType.DMA((chips,)),
            pltpu.SemaphoreType.DMA((1,)),
            pltpu.SemaphoreType.DMA((1,)),
            pltpu.SemaphoreType.DMA((chips - 1, 2)),
            pltpu.SemaphoreType.DMA((chips - 1, 2)),
        ],
        compiler_params=pltpu.CompilerParams(collective_id=collective_id, has_side_effects=True),
    )(x)


def _row_reduce_scatter(x, axis, other_axis, collective_id):
    chips, _, rows, width = x.shape
    return pl.pallas_call(
        functools.partial(_row_rs_kernel, axis, other_axis, chips),
        out_shape=jax.ShapeDtypeStruct((rows, width), x.dtype),
        in_specs=[pl.BlockSpec(memory_space=pltpu.VMEM)],
        out_specs=pl.BlockSpec(memory_space=pltpu.VMEM),
        scratch_shapes=[
            pltpu.VMEM((chips, rows, width), x.dtype),
            pltpu.VMEM((chips - 1, rows, width), x.dtype),
            pltpu.VMEM((chips - 1, rows, width), x.dtype),
            pltpu.SemaphoreType.DMA((chips,)),
            pltpu.SemaphoreType.DMA((chips,)),
            pltpu.SemaphoreType.DMA((chips - 1,)),
            pltpu.SemaphoreType.DMA((chips - 1,)),
        ],
        compiler_params=pltpu.CompilerParams(collective_id=collective_id, has_side_effects=True),
    )(x)


def _row_all_gather(x, axis, other_axis, chips, collective_id):
    rows, width = x.shape
    return pl.pallas_call(
        functools.partial(_row_ag_kernel, axis, other_axis, chips),
        out_shape=jax.ShapeDtypeStruct((chips, 2, rows, width), x.dtype),
        in_specs=[pl.BlockSpec(memory_space=pltpu.VMEM)],
        out_specs=pl.BlockSpec(memory_space=pltpu.VMEM),
        scratch_shapes=[
            pltpu.VMEM((rows, width), x.dtype),
            pltpu.VMEM((chips - 1, rows, width), x.dtype),
            pltpu.VMEM((chips - 1, rows, width), x.dtype),
            pltpu.SemaphoreType.DMA((chips,)),
            pltpu.SemaphoreType.DMA((chips,)),
            pltpu.SemaphoreType.DMA((chips - 1,)),
            pltpu.SemaphoreType.DMA((chips - 1,)),
        ],
        compiler_params=pltpu.CompilerParams(collective_id=collective_id, has_side_effects=True),
    )(x)


def _reduce_scatter(x, axis, other_axis, collective_id):
    n, rows, width = x.shape
    return pl.pallas_call(
        functools.partial(_rs_kernel, axis, other_axis, n),
        out_shape=jax.ShapeDtypeStruct((rows, width), x.dtype),
        in_specs=[pl.BlockSpec(memory_space=pltpu.VMEM)],
        out_specs=pl.BlockSpec(memory_space=pltpu.VMEM),
        scratch_shapes=[
            pltpu.VMEM((n - 1, rows, width), x.dtype),
            pltpu.SemaphoreType.DMA((n - 1,)),
            pltpu.SemaphoreType.DMA((n - 1,)),
        ],
        compiler_params=pltpu.CompilerParams(collective_id=collective_id, has_side_effects=True),
    )(x)


def _all_gather(x, axis, other_axis, n, collective_id):
    rows, width = x.shape
    return pl.pallas_call(
        functools.partial(_ag_kernel, axis, other_axis, n),
        out_shape=jax.ShapeDtypeStruct((n, rows, width), x.dtype),
        in_specs=[pl.BlockSpec(memory_space=pltpu.VMEM)],
        out_specs=pl.BlockSpec(memory_space=pltpu.VMEM),
        scratch_shapes=[
            pltpu.VMEM((n - 1, rows, width), x.dtype),
            pltpu.SemaphoreType.DMA((n - 1,)),
            pltpu.SemaphoreType.DMA((n - 1,)),
        ],
        compiler_params=pltpu.CompilerParams(collective_id=collective_id, has_side_effects=True),
    )(x)


def _mask_lanes(mask_ref, nb, bs, width, row=None, col=None):
    blk = lax.broadcasted_iota(jnp.int32, (1, width), 1) // bs
    keep = jnp.zeros((1, width), jnp.int32)
    for b in range(nb):
        value = mask_ref[row, b] if col is None else mask_ref[b, col]
        keep = jnp.where(blk == b, value, keep)
    return keep != 0


def _sub_blocks(nb):
    return 4 if nb % 4 == 0 else (2 if nb % 2 == 0 else 1)


def _half_blocks(nb):
    return nb // 2


def _sketch_kernel(nb, bs, sub, mask_ref, g_ref, p_ref, o_ref):
    i = pl.program_id(0)
    for h in range(sub):
        keep = _mask_lanes(mask_ref, nb, bs, p_ref.shape[1], row=i * sub + h)
        p = jnp.where(keep, p_ref[...], jnp.zeros_like(p_ref))
        o_ref[:, h * bs:(h + 1) * bs] = lax.dot_general(
            p, g_ref[h * bs:(h + 1) * bs, :], (((1,), (1,)), ((), ())), preferred_element_type=jnp.float32
        )


def _adjoint_kernel(nb, bs, sub, mask_ref, l_ref, g_ref, o_ref):
    j = pl.program_id(0)
    for h in range(sub):
        keep = _mask_lanes(mask_ref, nb, bs, l_ref.shape[1], col=j * sub + h)
        lowered = jnp.where(keep, l_ref[...], jnp.zeros_like(l_ref))
        o_ref[:, h * bs:(h + 1) * bs] = jnp.dot(
            lowered, g_ref[:, h * bs:(h + 1) * bs], preferred_element_type=jnp.float32
        )


def _sketch_partial(mask, green, probes_t):
    rb, cb = mask.shape
    bs = green.shape[0] // rb
    sub = _half_blocks(rb)
    k = probes_t.shape[0]
    return pl.pallas_call(
        functools.partial(_sketch_kernel, cb, bs, sub),
        out_shape=jax.ShapeDtypeStruct((rb // sub, k, bs * sub), jnp.float32),
        grid_spec=pltpu.PrefetchScalarGridSpec(
            num_scalar_prefetch=1,
            grid=(rb // sub,),
            in_specs=[
                pl.BlockSpec((bs * sub, green.shape[1]), lambda i, m: (i, 0)),
                pl.BlockSpec((k, green.shape[1]), lambda i, m: (0, 0)),
            ],
            out_specs=pl.BlockSpec((None, k, bs * sub), lambda i, m: (i, 0, 0)),
        ),
    )(mask, green, probes_t)


def _adjoint_partial(mask, lowered_t, green):
    rb, cb = mask.shape
    bs = green.shape[0] // rb
    sub = _sub_blocks(cb)
    k = lowered_t.shape[0]
    return pl.pallas_call(
        functools.partial(_adjoint_kernel, rb, bs, sub),
        out_shape=jax.ShapeDtypeStruct((k, green.shape[1]), jnp.float32),
        grid_spec=pltpu.PrefetchScalarGridSpec(
            num_scalar_prefetch=1,
            grid=(cb // sub,),
            in_specs=[
                pl.BlockSpec((k, green.shape[0]), lambda j, m: (0, 0)),
                pl.BlockSpec((green.shape[0], bs * sub), lambda j, m: (0, j)),
            ],
            out_specs=pl.BlockSpec((k, bs * sub), lambda j, m: (0, j)),
        ),
    )(mask, lowered_t, green)


def local(green, mask, probes):
    n_row = lax.axis_size("row")
    n_col = lax.axis_size("col")
    probes_t = _row_all_gather(probes.T, "row", "col", n_row // 2, 3)
    k = n_row * probes_t.shape[2]
    probes_t = probes_t.reshape(k, -1)
    partial_t = _sketch_partial(mask, green, probes_t)
    sketch_t, lowered_t = _all_reduce(partial_t.reshape(2, n_col, k // n_col, -1), "col", "row", 0)
    lowered_t = lowered_t.reshape(k, -1)
    term_t = _adjoint_partial(mask, lowered_t, green)
    adjoint_t = _row_reduce_scatter(term_t.reshape(n_row // 2, 2, k // n_row, -1), "row", "col", 2)
    return (sketch_t.T, adjoint_t.T)


def solution(mesh):
    in_specs = (P("row", "col"), P("row", "col"), P("col", "row"))
    out_specs = (P("row", "col"), P("col", "row"))
    return jax.shard_map(local, mesh=mesh, in_specs=in_specs, out_specs=out_specs, check_vma=False)
```

```python
import functools

import jax
import jax.numpy as jnp
from jax import lax
from jax.experimental import pallas as pl
from jax.experimental.pallas import tpu as pltpu
from jax.sharding import PartitionSpec as P

MESH = pl.DeviceIdType.MESH


def _peer(axis, other, p):
    return (other, p) if axis == "col" else (p, other)


def _greet(axis, other, me, n):
    barrier = pltpu.get_barrier_semaphore()
    for d in range(1, n):
        peer = _peer(axis, other, lax.rem(me + d, n))
        pl.semaphore_signal(barrier, 1, device_id=peer, device_id_type=MESH)
    pl.semaphore_wait(barrier, n - 1)


def _rs_kernel(axis, other_axis, n, x_ref, o_ref, recv, send_sem, recv_sem):
    me = lax.axis_index(axis)
    other = lax.axis_index(other_axis)
    _greet(axis, other, me, n)
    copies = []
    for d in range(1, n):
        peer = lax.rem(me + d, n)
        copy = pltpu.make_async_remote_copy(
            src_ref=x_ref.at[peer],
            dst_ref=recv.at[d - 1],
            send_sem=send_sem.at[d - 1],
            recv_sem=recv_sem.at[d - 1],
            device_id=_peer(axis, other, peer),
            device_id_type=MESH,
        )
        copy.start()
        copies.append(copy)
    acc = x_ref[me]
    for d, copy in enumerate(copies):
        copy.wait_recv()
        acc = acc + recv[d]
    for copy in copies:
        copy.wait_send()
    o_ref[...] = acc


def _ag_kernel(axis, other_axis, n, x_ref, o_ref, recv, send_sem, recv_sem):
    me = lax.axis_index(axis)
    other = lax.axis_index(other_axis)
    _greet(axis, other, me, n)
    copies = []
    for d in range(1, n):
        peer = lax.rem(me + d, n)
        copy = pltpu.make_async_remote_copy(
            src_ref=x_ref,
            dst_ref=recv.at[d - 1],
            send_sem=send_sem.at[d - 1],
            recv_sem=recv_sem.at[d - 1],
            device_id=_peer(axis, other, peer),
            device_id_type=MESH,
        )
        copy.start()
        copies.append(copy)
    o_ref[me] = x_ref[...]
    for d, copy in enumerate(copies):
        copy.wait_recv()
        o_ref[lax.rem(me + n - 1 - d, n)] = recv[d]
    for copy in copies:
        copy.wait_send()


def _row_greet(axis, me, other, chips):
    chip, core = me // 2, lax.rem(me, 2)
    barrier = pltpu.get_barrier_semaphore()
    pl.semaphore_signal(barrier, 1, device_id=_peer(axis, other, chip * 2 + 1 - core), device_id_type=MESH)
    for d in range(1, chips):
        peer = lax.rem(chip + d, chips) * 2 + core
        pl.semaphore_signal(barrier, 1, device_id=_peer(axis, other, peer), device_id_type=MESH)
    pl.semaphore_wait(barrier, chips)
    return chip, core


def _row_rs_kernel(axis, other_axis, chips, x_ref, o_ref, recv1, mid, recv2, s1, r1, s2, r2):
    me = lax.axis_index(axis)
    other = lax.axis_index(other_axis)
    chip, core = _row_greet(axis, me, other, chips)
    _rs_body(axis, other, chips, chip, core, x_ref, o_ref, recv1, mid, recv2, s1, r1, s2, r2)


def _rs_body(axis, other, chips, chip, core, x_ref, o_ref, recv1, mid, recv2, s1, r1, s2, r2):
    sib = _peer(axis, other, chip * 2 + 1 - core)
    first = []
    for d in list(range(1, chips)) + [0]:
        target = lax.rem(chip + d, chips)
        copy = pltpu.make_async_remote_copy(
            src_ref=x_ref.at[target, 1 - core],
            dst_ref=recv1.at[d],
            send_sem=s1.at[d],
            recv_sem=r1.at[d],
            device_id=sib,
            device_id_type=MESH,
        )
        copy.start()
        first.append(copy)
    sends = []
    for d in range(1, chips):
        target = lax.rem(chip + d, chips)
        first[d - 1].wait_recv()
        mid[d - 1] = x_ref[target, core] + recv1[d]
        copy = pltpu.make_async_remote_copy(
            src_ref=mid.at[d - 1],
            dst_ref=recv2.at[d - 1],
            send_sem=s2.at[d - 1],
            recv_sem=r2.at[d - 1],
            device_id=_peer(axis, other, target * 2 + core),
            device_id_type=MESH,
        )
        copy.start()
        sends.append(copy)
    first[chips - 1].wait_recv()
    acc = x_ref[chip, core] + recv1[0]
    for d, copy in enumerate(sends):
        copy.wait_recv()
        acc = acc + recv2[d]
    for copy in first + sends:
        copy.wait_send()
    o_ref[...] = acc


def _row_ag_kernel(axis, other_axis, chips, x_ref, o_ref, recv_s, recv_a, recv_f, s1, r1, s2, r2):
    me = lax.axis_index(axis)
    other = lax.axis_index(other_axis)
    chip, core = _row_greet(axis, me, other, chips)
    _ag_body(axis, other, chips, chip, core, x_ref, o_ref, recv_s, recv_a, recv_f, s1, r1, s2, r2)


def _ag_body(axis, other, chips, chip, core, x_ref, o_ref, recv_s, recv_a, recv_f, s1, r1, s2, r2):
    sib = _peer(axis, other, chip * 2 + 1 - core)
    to_sib = pltpu.make_async_remote_copy(
        src_ref=x_ref, dst_ref=recv_s, send_sem=s1.at[0], recv_sem=r1.at[0],
        device_id=sib, device_id_type=MESH,
    )
    to_sib.start()
    first = [to_sib]
    for d in range(1, chips):
        peer = lax.rem(chip + d, chips) * 2 + core
        copy = pltpu.make_async_remote_copy(
            src_ref=x_ref, dst_ref=recv_a.at[d - 1], send_sem=s1.at[d], recv_sem=r1.at[d],
            device_id=_peer(axis, other, peer), device_id_type=MESH,
        )
        copy.start()
        first.append(copy)
    o_ref[chip, core] = x_ref[...]
    forwards = []
    for d in range(1, chips):
        first[d].wait_recv()
        copy = pltpu.make_async_remote_copy(
            src_ref=recv_a.at[d - 1], dst_ref=recv_f.at[d - 1], send_sem=s2.at[d - 1],
            recv_sem=r2.at[d - 1], device_id=sib, device_id_type=MESH,
        )
        copy.start()
        forwards.append(copy)
        o_ref[lax.rem(chip + chips - d, chips), core] = recv_a[d - 1]
    to_sib.wait_recv()
    o_ref[chip, 1 - core] = recv_s[...]
    for d, copy in enumerate(forwards):
        copy.wait_recv()
        o_ref[lax.rem(chip + chips - 1 - d, chips), 1 - core] = recv_f[d]
    for copy in first + forwards:
        copy.wait_send()


def _mixed_rs_body(axis, other, chips, chip, core, x_ref, o_ref, ra1, ma, ra2, rb1, mb, rb2,
                   sa1, qa1, sa2, qa2, sb1, qb1, sb2, qb2):
    sib = _peer(axis, other, chip * 2 + 1 - core)
    width = x_ref.shape[-1]
    a1 = []
    for d in list(range(1, chips)) + [0]:
        target = lax.rem(chip + d, chips)
        copy = pltpu.make_async_remote_copy(
            src_ref=x_ref.at[0, target * 2 + 1 - core], dst_ref=ra1.at[d], send_sem=sa1.at[d],
            recv_sem=qa1.at[d], device_id=sib, device_id_type=MESH,
        )
        copy.start()
        a1.append(copy)
    b1 = []
    for d in range(1, chips):
        target = lax.rem(chip + d, chips)
        for half, bit in enumerate((core, 1 - core)):
            copy = pltpu.make_async_remote_copy(
                src_ref=x_ref.at[1, target * 2 + bit], dst_ref=rb1.at[d - 1, half],
                send_sem=sb1.at[d - 1, half], recv_sem=qb1.at[d - 1, half],
                device_id=_peer(axis, other, target * 2 + core), device_id_type=MESH,
            )
            copy.start()
            b1.append(copy)
    a2 = []
    for d in range(1, chips):
        target = lax.rem(chip + d, chips)
        a1[d - 1].wait_recv()
        ma[d - 1] = x_ref[0, target * 2 + core] + ra1[d]
        copy = pltpu.make_async_remote_copy(
            src_ref=ma.at[d - 1], dst_ref=ra2.at[d - 1], send_sem=sa2.at[d - 1],
            recv_sem=qa2.at[d - 1], device_id=_peer(axis, other, target * 2 + core),
            device_id_type=MESH,
        )
        copy.start()
        a2.append(copy)
    for copy in b1:
        copy.wait_recv()
    part = x_ref[1, chip * 2 + 1 - core]
    for d in range(chips - 1):
        part = part + rb1[d, 1]
    mb[...] = part
    b2 = pltpu.make_async_remote_copy(
        src_ref=mb, dst_ref=rb2, send_sem=sb2.at[0], recv_sem=qb2.at[0],
        device_id=sib, device_id_type=MESH,
    )
    b2.start()
    acc_b = x_ref[1, chip * 2 + core]
    for d in range(chips - 1):
        acc_b = acc_b + rb1[d, 0]
    a1[chips - 1].wait_recv()
    acc_a = x_ref[0, chip * 2 + core] + ra1[0]
    for d, copy in enumerate(a2):
        copy.wait_recv()
        acc_a = acc_a + ra2[d]
    b2.wait_recv()
    o_ref[:, :width] = acc_a
    o_ref[:, width:] = acc_b + rb2[...]
    for copy in a1 + b1 + a2 + [b2]:
        copy.wait_send()


def _ar_kernel(axis, other_axis, chips, x_ref, o_ref, g_ref, low, *scratch):
    me = lax.axis_index(axis)
    other = lax.axis_index(other_axis)
    chip, core = _row_greet(axis, me, other, chips)
    _mixed_rs_body(axis, other, chips, chip, core, x_ref, o_ref, *scratch[:14])
    low[...] = o_ref[...].astype(low.dtype)
    _ag_body(axis, other, chips, chip, core, low, g_ref, *scratch[14:])


def _all_reduce(x, axis, other_axis, collective_id):
    _, n, rows, half = x.shape
    chips = n // 2
    width = 2 * half
    low = jnp.bfloat16
    return pl.pallas_call(
        functools.partial(_ar_kernel, axis, other_axis, chips),
        out_shape=(
            jax.ShapeDtypeStruct((rows, width), x.dtype),
            jax.ShapeDtypeStruct((chips, 2, rows, width), low),
        ),
        in_specs=[pl.BlockSpec(memory_space=pltpu.VMEM)],
        out_specs=(pl.BlockSpec(memory_space=pltpu.VMEM), pl.BlockSpec(memory_space=pltpu.VMEM)),
        scratch_shapes=[
            pltpu.VMEM((rows, width), low),
            pltpu.VMEM((chips, rows, half), x.dtype),
            pltpu.VMEM((chips - 1, rows, half), x.dtype),
            pltpu.VMEM((chips - 1, rows, half), x.dtype),
            pltpu.VMEM((chips - 1, 2, rows, half), x.dtype),
            pltpu.VMEM((rows, half), x.dtype),
            pltpu.VMEM((rows, half), x.dtype),
            pltpu.SemaphoreType.DMA((chips,)),
            pltpu.SemaphoreType.DMA((chips,)),
            pltpu.SemaphoreType.DMA((chips - 1,)),
            pltpu.SemaphoreType.DMA((chips - 1,)),
            pltpu.SemaphoreType.DMA((chips - 1, 2)),
            pltpu.SemaphoreType.DMA((chips - 1, 2)),
            pltpu.SemaphoreType.DMA((1,)),
            pltpu.SemaphoreType.DMA((1,)),
            pltpu.VMEM((rows, width), low),
            pltpu.VMEM((chips - 1, rows, width), low),
            pltpu.VMEM((chips - 1, rows, width), low),
            pltpu.SemaphoreType.DMA((chips,)),
            pltpu.SemaphoreType.DMA((chips,)),
            pltpu.SemaphoreType.DMA((chips - 1,)),
            pltpu.SemaphoreType.DMA((chips - 1,)),
        ],
        compiler_params=pltpu.CompilerParams(collective_id=collective_id, has_side_effects=True),
    )(x)


def _row_reduce_scatter(x, axis, other_axis, collective_id):
    chips, _, rows, width = x.shape
    return pl.pallas_call(
        functools.partial(_row_rs_kernel, axis, other_axis, chips),
        out_shape=jax.ShapeDtypeStruct((rows, width), x.dtype),
        in_specs=[pl.BlockSpec(memory_space=pltpu.VMEM)],
        out_specs=pl.BlockSpec(memory_space=pltpu.VMEM),
        scratch_shapes=[
            pltpu.VMEM((chips, rows, width), x.dtype),
            pltpu.VMEM((chips - 1, rows, width), x.dtype),
            pltpu.VMEM((chips - 1, rows, width), x.dtype),
            pltpu.SemaphoreType.DMA((chips,)),
            pltpu.SemaphoreType.DMA((chips,)),
            pltpu.SemaphoreType.DMA((chips - 1,)),
            pltpu.SemaphoreType.DMA((chips - 1,)),
        ],
        compiler_params=pltpu.CompilerParams(collective_id=collective_id, has_side_effects=True),
    )(x)


def _row_all_gather(x, axis, other_axis, chips, collective_id):
    rows, width = x.shape
    return pl.pallas_call(
        functools.partial(_row_ag_kernel, axis, other_axis, chips),
        out_shape=jax.ShapeDtypeStruct((chips, 2, rows, width), x.dtype),
        in_specs=[pl.BlockSpec(memory_space=pltpu.VMEM)],
        out_specs=pl.BlockSpec(memory_space=pltpu.VMEM),
        scratch_shapes=[
            pltpu.VMEM((rows, width), x.dtype),
            pltpu.VMEM((chips - 1, rows, width), x.dtype),
            pltpu.VMEM((chips - 1, rows, width), x.dtype),
            pltpu.SemaphoreType.DMA((chips,)),
            pltpu.SemaphoreType.DMA((chips,)),
            pltpu.SemaphoreType.DMA((chips - 1,)),
            pltpu.SemaphoreType.DMA((chips - 1,)),
        ],
        compiler_params=pltpu.CompilerParams(collective_id=collective_id, has_side_effects=True),
    )(x)


def _reduce_scatter(x, axis, other_axis, collective_id):
    n, rows, width = x.shape
    return pl.pallas_call(
        functools.partial(_rs_kernel, axis, other_axis, n),
        out_shape=jax.ShapeDtypeStruct((rows, width), x.dtype),
        in_specs=[pl.BlockSpec(memory_space=pltpu.VMEM)],
        out_specs=pl.BlockSpec(memory_space=pltpu.VMEM),
        scratch_shapes=[
            pltpu.VMEM((n - 1, rows, width), x.dtype),
            pltpu.SemaphoreType.DMA((n - 1,)),
            pltpu.SemaphoreType.DMA((n - 1,)),
        ],
        compiler_params=pltpu.CompilerParams(collective_id=collective_id, has_side_effects=True),
    )(x)


def _all_gather(x, axis, other_axis, n, collective_id):
    rows, width = x.shape
    return pl.pallas_call(
        functools.partial(_ag_kernel, axis, other_axis, n),
        out_shape=jax.ShapeDtypeStruct((n, rows, width), x.dtype),
        in_specs=[pl.BlockSpec(memory_space=pltpu.VMEM)],
        out_specs=pl.BlockSpec(memory_space=pltpu.VMEM),
        scratch_shapes=[
            pltpu.VMEM((n - 1, rows, width), x.dtype),
            pltpu.SemaphoreType.DMA((n - 1,)),
            pltpu.SemaphoreType.DMA((n - 1,)),
        ],
        compiler_params=pltpu.CompilerParams(collective_id=collective_id, has_side_effects=True),
    )(x)


def _mask_lanes(mask_ref, nb, bs, width, row=None, col=None):
    blk = lax.broadcasted_iota(jnp.int32, (1, width), 1) // bs
    keep = jnp.zeros((1, width), jnp.int32)
    for b in range(nb):
        value = mask_ref[row, b] if col is None else mask_ref[b, col]
        keep = jnp.where(blk == b, value, keep)
    return keep != 0


def _sub_blocks(nb):
    return 4 if nb % 4 == 0 else (2 if nb % 2 == 0 else 1)


def _half_blocks(nb):
    return nb // 2


def _sketch_kernel(nb, bs, sub, mask_ref, g_ref, p_ref, o_ref):
    i = pl.program_id(0)
    for h in range(sub):
        keep = _mask_lanes(mask_ref, nb, bs, p_ref.shape[1], row=i * sub + h)
        p = jnp.where(keep, p_ref[...], jnp.zeros_like(p_ref))
        o_ref[:, h * bs:(h + 1) * bs] = lax.dot_general(
            p, g_ref[h * bs:(h + 1) * bs, :], (((1,), (1,)), ((), ())), preferred_element_type=jnp.float32
        )


def _adjoint_kernel(nb, bs, sub, mask_ref, l_ref, g_ref, o_ref):
    j = pl.program_id(0)
    for h in range(sub):
        keep = _mask_lanes(mask_ref, nb, bs, l_ref.shape[1], col=j * sub + h)
        lowered = jnp.where(keep, l_ref[...], jnp.zeros_like(l_ref))
        o_ref[:, h * bs:(h + 1) * bs] = jnp.dot(
            lowered, g_ref[:, h * bs:(h + 1) * bs], preferred_element_type=jnp.float32
        )


def _sketch_partial(mask, green, probes_t):
    rb, cb = mask.shape
    bs = green.shape[0] // rb
    sub = _half_blocks(rb)
    k = probes_t.shape[0]
    return pl.pallas_call(
        functools.partial(_sketch_kernel, cb, bs, sub),
        out_shape=jax.ShapeDtypeStruct((rb // sub, k, bs * sub), jnp.float32),
        grid_spec=pltpu.PrefetchScalarGridSpec(
            num_scalar_prefetch=1,
            grid=(rb // sub,),
            in_specs=[
                pl.BlockSpec((bs * sub, green.shape[1]), lambda i, m: (i, 0)),
                pl.BlockSpec((k, green.shape[1]), lambda i, m: (0, 0)),
            ],
            out_specs=pl.BlockSpec((None, k, bs * sub), lambda i, m: (i, 0, 0)),
        ),
    )(mask, green, probes_t)


def _adjoint_partial(mask, lowered_t, green):
    rb, cb = mask.shape
    bs = green.shape[0] // rb
    sub = _sub_blocks(cb)
    k = lowered_t.shape[0]
    return pl.pallas_call(
        functools.partial(_adjoint_kernel, rb, bs, sub),
        out_shape=jax.ShapeDtypeStruct((k, green.shape[1]), jnp.float32),
        grid_spec=pltpu.PrefetchScalarGridSpec(
            num_scalar_prefetch=1,
            grid=(cb // sub,),
            in_specs=[
                pl.BlockSpec((k, green.shape[0]), lambda j, m: (0, 0)),
                pl.BlockSpec((green.shape[0], bs * sub), lambda j, m: (0, j)),
            ],
            out_specs=pl.BlockSpec((k, bs * sub), lambda j, m: (0, j)),
        ),
    )(mask, lowered_t, green)


def local(green, mask, probes):
    n_row = lax.axis_size("row")
    n_col = lax.axis_size("col")
    probes_t = _row_all_gather(probes.T, "row", "col", n_row // 2, 3)
    k = n_row * probes_t.shape[2]
    probes_t = probes_t.reshape(k, -1)
    partial_t = _sketch_partial(mask, green, probes_t)
    sketch_t, lowered_t = _all_reduce(partial_t.reshape(2, n_col, k // n_col, -1), "col", "row", 0)
    lowered_t = lowered_t.reshape(k, -1)
    term_t = _adjoint_partial(mask, lowered_t, green)
    adjoint_t = _row_reduce_scatter(term_t.reshape(n_row // 2, 2, k // n_row, -1), "row", "col", 2)
    return (sketch_t.T, adjoint_t.T)


def solution(mesh):
    in_specs = (P("row", "col"), P("row", "col"), P("col", "row"))
    out_specs = (P("row", "col"), P("col", "row"))
    return jax.shard_map(local, mesh=mesh, in_specs=in_specs, out_specs=out_specs, check_vma=False)
```

```python
import functools

import jax
import jax.numpy as jnp
from jax import lax
from jax.experimental import pallas as pl
from jax.experimental.pallas import tpu as pltpu
from jax.sharding import PartitionSpec as P

MESH = pl.DeviceIdType.MESH


def _peer(axis, other, p):
    return (other, p) if axis == "col" else (p, other)


def _greet(axis, other, me, n):
    barrier = pltpu.get_barrier_semaphore()
    for d in range(1, n):
        peer = _peer(axis, other, lax.rem(me + d, n))
        pl.semaphore_signal(barrier, 1, device_id=peer, device_id_type=MESH)
    pl.semaphore_wait(barrier, n - 1)


def _rs_kernel(axis, other_axis, n, x_ref, o_ref, recv, send_sem, recv_sem):
    me = lax.axis_index(axis)
    other = lax.axis_index(other_axis)
    _greet(axis, other, me, n)
    copies = []
    for d in range(1, n):
        peer = lax.rem(me + d, n)
        copy = pltpu.make_async_remote_copy(
            src_ref=x_ref.at[peer],
            dst_ref=recv.at[d - 1],
            send_sem=send_sem.at[d - 1],
            recv_sem=recv_sem.at[d - 1],
            device_id=_peer(axis, other, peer),
            device_id_type=MESH,
        )
        copy.start()
        copies.append(copy)
    acc = x_ref[me]
    for d, copy in enumerate(copies):
        copy.wait_recv()
        acc = acc + recv[d]
    for copy in copies:
        copy.wait_send()
    o_ref[...] = acc


def _ag_kernel(axis, other_axis, n, x_ref, o_ref, recv, send_sem, recv_sem):
    me = lax.axis_index(axis)
    other = lax.axis_index(other_axis)
    _greet(axis, other, me, n)
    copies = []
    for d in range(1, n):
        peer = lax.rem(me + d, n)
        copy = pltpu.make_async_remote_copy(
            src_ref=x_ref,
            dst_ref=recv.at[d - 1],
            send_sem=send_sem.at[d - 1],
            recv_sem=recv_sem.at[d - 1],
            device_id=_peer(axis, other, peer),
            device_id_type=MESH,
        )
        copy.start()
        copies.append(copy)
    o_ref[me] = x_ref[...]
    for d, copy in enumerate(copies):
        copy.wait_recv()
        o_ref[lax.rem(me + n - 1 - d, n)] = recv[d]
    for copy in copies:
        copy.wait_send()


def _row_greet(axis, me, other, chips):
    chip, core = me // 2, lax.rem(me, 2)
    barrier = pltpu.get_barrier_semaphore()
    pl.semaphore_signal(barrier, 1, device_id=_peer(axis, other, chip * 2 + 1 - core), device_id_type=MESH)
    for d in range(1, chips):
        peer = lax.rem(chip + d, chips) * 2 + core
        pl.semaphore_signal(barrier, 1, device_id=_peer(axis, other, peer), device_id_type=MESH)
    pl.semaphore_wait(barrier, chips)
    return chip, core


def _row_rs_kernel(axis, other_axis, chips, x_ref, o_ref, recv1, mid, recv2, s1, r1, s2, r2):
    me = lax.axis_index(axis)
    other = lax.axis_index(other_axis)
    chip, core = _row_greet(axis, me, other, chips)
    _rs_body(axis, other, chips, chip, core, x_ref, o_ref, recv1, mid, recv2, s1, r1, s2, r2)


def _rs_body(axis, other, chips, chip, core, x_ref, o_ref, recv1, mid, recv2, s1, r1, s2, r2):
    sib = _peer(axis, other, chip * 2 + 1 - core)
    first = []
    for d in list(range(1, chips)) + [0]:
        target = lax.rem(chip + d, chips)
        copy = pltpu.make_async_remote_copy(
            src_ref=x_ref.at[target, 1 - core],
            dst_ref=recv1.at[d],
            send_sem=s1.at[d],
            recv_sem=r1.at[d],
            device_id=sib,
            device_id_type=MESH,
        )
        copy.start()
        first.append(copy)
    sends = []
    for d in range(1, chips):
        target = lax.rem(chip + d, chips)
        first[d - 1].wait_recv()
        mid[d - 1] = x_ref[target, core] + recv1[d]
        copy = pltpu.make_async_remote_copy(
            src_ref=mid.at[d - 1],
            dst_ref=recv2.at[d - 1],
            send_sem=s2.at[d - 1],
            recv_sem=r2.at[d - 1],
            device_id=_peer(axis, other, target * 2 + core),
            device_id_type=MESH,
        )
        copy.start()
        sends.append(copy)
    first[chips - 1].wait_recv()
    acc = x_ref[chip, core] + recv1[0]
    for d, copy in enumerate(sends):
        copy.wait_recv()
        acc = acc + recv2[d]
    for copy in first + sends:
        copy.wait_send()
    o_ref[...] = acc


def _row_ag_kernel(axis, other_axis, chips, x_ref, o_ref, recv_s, recv_a, recv_f, s1, r1, s2, r2):
    me = lax.axis_index(axis)
    other = lax.axis_index(other_axis)
    chip, core = _row_greet(axis, me, other, chips)
    _ag_body(axis, other, chips, chip, core, x_ref, o_ref, recv_s, recv_a, recv_f, s1, r1, s2, r2)


def _ag_body(axis, other, chips, chip, core, x_ref, o_ref, recv_s, recv_a, recv_f, s1, r1, s2, r2):
    sib = _peer(axis, other, chip * 2 + 1 - core)
    to_sib = pltpu.make_async_remote_copy(
        src_ref=x_ref, dst_ref=recv_s, send_sem=s1.at[0], recv_sem=r1.at[0],
        device_id=sib, device_id_type=MESH,
    )
    to_sib.start()
    first = [to_sib]
    for d in range(1, chips):
        peer = lax.rem(chip + d, chips) * 2 + core
        copy = pltpu.make_async_remote_copy(
            src_ref=x_ref, dst_ref=recv_a.at[d - 1], send_sem=s1.at[d], recv_sem=r1.at[d],
            device_id=_peer(axis, other, peer), device_id_type=MESH,
        )
        copy.start()
        first.append(copy)
    o_ref[chip, core] = x_ref[...]
    forwards = []
    for d in range(1, chips):
        first[d].wait_recv()
        copy = pltpu.make_async_remote_copy(
            src_ref=recv_a.at[d - 1], dst_ref=recv_f.at[d - 1], send_sem=s2.at[d - 1],
            recv_sem=r2.at[d - 1], device_id=sib, device_id_type=MESH,
        )
        copy.start()
        forwards.append(copy)
        o_ref[lax.rem(chip + chips - d, chips), core] = recv_a[d - 1]
    to_sib.wait_recv()
    o_ref[chip, 1 - core] = recv_s[...]
    for d, copy in enumerate(forwards):
        copy.wait_recv()
        o_ref[lax.rem(chip + chips - 1 - d, chips), 1 - core] = recv_f[d]
    for copy in first + forwards:
        copy.wait_send()


def _mixed_rs_body(axis, other, chips, chip, core, x_ref, o_ref, ra1, ma, ra2, rb1, mb, rb2,
                   sa1, qa1, sa2, qa2, sb1, qb1, sb2, qb2):
    sib = _peer(axis, other, chip * 2 + 1 - core)
    width = x_ref.shape[-1]
    a1 = []
    for d in list(range(1, chips)) + [0]:
        target = lax.rem(chip + d, chips)
        copy = pltpu.make_async_remote_copy(
            src_ref=x_ref.at[0, target * 2 + 1 - core], dst_ref=ra1.at[d], send_sem=sa1.at[d],
            recv_sem=qa1.at[d], device_id=sib, device_id_type=MESH,
        )
        copy.start()
        a1.append(copy)
    b1 = []
    for d in range(1, chips):
        target = lax.rem(chip + d, chips)
        for half, bit in enumerate((core, 1 - core)):
            copy = pltpu.make_async_remote_copy(
                src_ref=x_ref.at[1, target * 2 + bit], dst_ref=rb1.at[d - 1, half],
                send_sem=sb1.at[d - 1, half], recv_sem=qb1.at[d - 1, half],
                device_id=_peer(axis, other, target * 2 + core), device_id_type=MESH,
            )
            copy.start()
            b1.append(copy)
    a2 = []
    for d in range(1, chips):
        target = lax.rem(chip + d, chips)
        a1[d - 1].wait_recv()
        ma[d - 1] = x_ref[0, target * 2 + core] + ra1[d]
        copy = pltpu.make_async_remote_copy(
            src_ref=ma.at[d - 1], dst_ref=ra2.at[d - 1], send_sem=sa2.at[d - 1],
            recv_sem=qa2.at[d - 1], device_id=_peer(axis, other, target * 2 + core),
            device_id_type=MESH,
        )
        copy.start()
        a2.append(copy)
    for copy in b1:
        copy.wait_recv()
    part = x_ref[1, chip * 2 + 1 - core]
    for d in range(chips - 1):
        part = part + rb1[d, 1]
    mb[...] = part
    b2 = pltpu.make_async_remote_copy(
        src_ref=mb, dst_ref=rb2, send_sem=sb2.at[0], recv_sem=qb2.at[0],
        device_id=sib, device_id_type=MESH,
    )
    b2.start()
    acc_b = x_ref[1, chip * 2 + core]
    for d in range(chips - 1):
        acc_b = acc_b + rb1[d, 0]
    a1[chips - 1].wait_recv()
    acc_a = x_ref[0, chip * 2 + core] + ra1[0]
    for d, copy in enumerate(a2):
        copy.wait_recv()
        acc_a = acc_a + ra2[d]
    b2.wait_recv()
    o_ref[:, :width] = acc_a
    o_ref[:, width:] = acc_b + rb2[...]
    for copy in a1 + b1 + a2 + [b2]:
        copy.wait_send()


def _ar_kernel(axis, other_axis, chips, rb, cb, bs, mask_ref, x_ref, g_hbm, o_ref, t_ref,
               g_vmem, g_sem, l_all, low, *scratch):
    load = pltpu.make_async_copy(g_hbm, g_vmem, g_sem.at[0])
    load.start()
    me = lax.axis_index(axis)
    other = lax.axis_index(other_axis)
    chip, core = _row_greet(axis, me, other, chips)
    _mixed_rs_body(axis, other, chips, chip, core, x_ref, o_ref, *scratch[:14])
    low[...] = o_ref[...].astype(low.dtype)
    _ag_body(axis, other, chips, chip, core, low, l_all, *scratch[14:])
    k = l_all.shape[0] * l_all.shape[1] * l_all.shape[2]
    lowered = l_all[...].reshape(k, l_all.shape[3])
    load.wait()
    for j in range(cb):
        keep = _mask_lanes(mask_ref, rb, bs, lowered.shape[1], col=j)
        masked = jnp.where(keep, lowered, jnp.zeros_like(lowered))
        t_ref[:, j * bs:(j + 1) * bs] = jnp.dot(
            masked, g_vmem[:, j * bs:(j + 1) * bs], preferred_element_type=jnp.float32
        )


def _all_reduce_adjoint(x, mask, green, axis, other_axis, collective_id):
    _, n, rows, half = x.shape
    chips = n // 2
    width = 2 * half
    low = jnp.bfloat16
    rb, cb = mask.shape
    bs = green.shape[0] // rb
    return pl.pallas_call(
        functools.partial(_ar_kernel, axis, other_axis, chips, rb, cb, bs),
        out_shape=(
            jax.ShapeDtypeStruct((rows, width), x.dtype),
            jax.ShapeDtypeStruct((n * rows, green.shape[1]), jnp.float32),
        ),
        in_specs=[
            pl.BlockSpec(memory_space=pltpu.SMEM),
            pl.BlockSpec(memory_space=pltpu.VMEM),
            pl.BlockSpec(memory_space=pl.ANY),
        ],
        out_specs=(pl.BlockSpec(memory_space=pltpu.VMEM), pl.BlockSpec(memory_space=pltpu.VMEM)),
        scratch_shapes=[
            pltpu.VMEM(green.shape, green.dtype),
            pltpu.SemaphoreType.DMA((1,)),
            pltpu.VMEM((chips, 2, rows, width), low),
            pltpu.VMEM((rows, width), low),
            pltpu.VMEM((chips, rows, half), x.dtype),
            pltpu.VMEM((chips - 1, rows, half), x.dtype),
            pltpu.VMEM((chips - 1, rows, half), x.dtype),
            pltpu.VMEM((chips - 1, 2, rows, half), x.dtype),
            pltpu.VMEM((rows, half), x.dtype),
            pltpu.VMEM((rows, half), x.dtype),
            pltpu.SemaphoreType.DMA((chips,)),
            pltpu.SemaphoreType.DMA((chips,)),
            pltpu.SemaphoreType.DMA((chips - 1,)),
            pltpu.SemaphoreType.DMA((chips - 1,)),
            pltpu.SemaphoreType.DMA((chips - 1, 2)),
            pltpu.SemaphoreType.DMA((chips - 1, 2)),
            pltpu.SemaphoreType.DMA((1,)),
            pltpu.SemaphoreType.DMA((1,)),
            pltpu.VMEM((rows, width), low),
            pltpu.VMEM((chips - 1, rows, width), low),
            pltpu.VMEM((chips - 1, rows, width), low),
            pltpu.SemaphoreType.DMA((chips,)),
            pltpu.SemaphoreType.DMA((chips,)),
            pltpu.SemaphoreType.DMA((chips - 1,)),
            pltpu.SemaphoreType.DMA((chips - 1,)),
        ],
        compiler_params=pltpu.CompilerParams(collective_id=collective_id, has_side_effects=True),
    )(mask, x, green)


def _row_reduce_scatter(x, axis, other_axis, collective_id):
    chips, _, rows, width = x.shape
    return pl.pallas_call(
        functools.partial(_row_rs_kernel, axis, other_axis, chips),
        out_shape=jax.ShapeDtypeStruct((rows, width), x.dtype),
        in_specs=[pl.BlockSpec(memory_space=pltpu.VMEM)],
        out_specs=pl.BlockSpec(memory_space=pltpu.VMEM),
        scratch_shapes=[
            pltpu.VMEM((chips, rows, width), x.dtype),
            pltpu.VMEM((chips - 1, rows, width), x.dtype),
            pltpu.VMEM((chips - 1, rows, width), x.dtype),
            pltpu.SemaphoreType.DMA((chips,)),
            pltpu.SemaphoreType.DMA((chips,)),
            pltpu.SemaphoreType.DMA((chips - 1,)),
            pltpu.SemaphoreType.DMA((chips - 1,)),
        ],
        compiler_params=pltpu.CompilerParams(collective_id=collective_id, has_side_effects=True),
    )(x)


def _row_all_gather(x, axis, other_axis, chips, collective_id):
    rows, width = x.shape
    return pl.pallas_call(
        functools.partial(_row_ag_kernel, axis, other_axis, chips),
        out_shape=jax.ShapeDtypeStruct((chips, 2, rows, width), x.dtype),
        in_specs=[pl.BlockSpec(memory_space=pltpu.VMEM)],
        out_specs=pl.BlockSpec(memory_space=pltpu.VMEM),
        scratch_shapes=[
            pltpu.VMEM((rows, width), x.dtype),
            pltpu.VMEM((chips - 1, rows, width), x.dtype),
            pltpu.VMEM((chips - 1, rows, width), x.dtype),
            pltpu.SemaphoreType.DMA((chips,)),
            pltpu.SemaphoreType.DMA((chips,)),
            pltpu.SemaphoreType.DMA((chips - 1,)),
            pltpu.SemaphoreType.DMA((chips - 1,)),
        ],
        compiler_params=pltpu.CompilerParams(collective_id=collective_id, has_side_effects=True),
    )(x)


def _reduce_scatter(x, axis, other_axis, collective_id):
    n, rows, width = x.shape
    return pl.pallas_call(
        functools.partial(_rs_kernel, axis, other_axis, n),
        out_shape=jax.ShapeDtypeStruct((rows, width), x.dtype),
        in_specs=[pl.BlockSpec(memory_space=pltpu.VMEM)],
        out_specs=pl.BlockSpec(memory_space=pltpu.VMEM),
        scratch_shapes=[
            pltpu.VMEM((n - 1, rows, width), x.dtype),
            pltpu.SemaphoreType.DMA((n - 1,)),
            pltpu.SemaphoreType.DMA((n - 1,)),
        ],
        compiler_params=pltpu.CompilerParams(collective_id=collective_id, has_side_effects=True),
    )(x)


def _all_gather(x, axis, other_axis, n, collective_id):
    rows, width = x.shape
    return pl.pallas_call(
        functools.partial(_ag_kernel, axis, other_axis, n),
        out_shape=jax.ShapeDtypeStruct((n, rows, width), x.dtype),
        in_specs=[pl.BlockSpec(memory_space=pltpu.VMEM)],
        out_specs=pl.BlockSpec(memory_space=pltpu.VMEM),
        scratch_shapes=[
            pltpu.VMEM((n - 1, rows, width), x.dtype),
            pltpu.SemaphoreType.DMA((n - 1,)),
            pltpu.SemaphoreType.DMA((n - 1,)),
        ],
        compiler_params=pltpu.CompilerParams(collective_id=collective_id, has_side_effects=True),
    )(x)


def _mask_lanes(mask_ref, nb, bs, width, row=None, col=None):
    blk = lax.broadcasted_iota(jnp.int32, (1, width), 1) // bs
    keep = jnp.zeros((1, width), jnp.int32)
    for b in range(nb):
        value = mask_ref[row, b] if col is None else mask_ref[b, col]
        keep = jnp.where(blk == b, value, keep)
    return keep != 0


def _sub_blocks(nb):
    return 4 if nb % 4 == 0 else (2 if nb % 2 == 0 else 1)


def _half_blocks(nb):
    return nb // 2


def _sketch_kernel(nb, bs, sub, mask_ref, g_ref, p_ref, o_ref):
    i = pl.program_id(0)
    for h in range(sub):
        keep = _mask_lanes(mask_ref, nb, bs, p_ref.shape[1], row=i * sub + h)
        p = jnp.where(keep, p_ref[...], jnp.zeros_like(p_ref))
        o_ref[:, h * bs:(h + 1) * bs] = lax.dot_general(
            p, g_ref[h * bs:(h + 1) * bs, :], (((1,), (1,)), ((), ())), preferred_element_type=jnp.float32
        )


def _adjoint_kernel(nb, bs, sub, mask_ref, l_ref, g_ref, o_ref):
    j = pl.program_id(0)
    for h in range(sub):
        keep = _mask_lanes(mask_ref, nb, bs, l_ref.shape[1], col=j * sub + h)
        lowered = jnp.where(keep, l_ref[...], jnp.zeros_like(l_ref))
        o_ref[:, h * bs:(h + 1) * bs] = jnp.dot(
            lowered, g_ref[:, h * bs:(h + 1) * bs], preferred_element_type=jnp.float32
        )


def _sketch_partial(mask, green, probes_t):
    rb, cb = mask.shape
    bs = green.shape[0] // rb
    sub = _half_blocks(rb)
    k = probes_t.shape[0]
    return pl.pallas_call(
        functools.partial(_sketch_kernel, cb, bs, sub),
        out_shape=jax.ShapeDtypeStruct((rb // sub, k, bs * sub), jnp.float32),
        grid_spec=pltpu.PrefetchScalarGridSpec(
            num_scalar_prefetch=1,
            grid=(rb // sub,),
            in_specs=[
                pl.BlockSpec((bs * sub, green.shape[1]), lambda i, m: (i, 0)),
                pl.BlockSpec((k, green.shape[1]), lambda i, m: (0, 0)),
            ],
            out_specs=pl.BlockSpec((None, k, bs * sub), lambda i, m: (i, 0, 0)),
        ),
    )(mask, green, probes_t)


def _adjoint_partial(mask, lowered_t, green):
    rb, cb = mask.shape
    bs = green.shape[0] // rb
    sub = _sub_blocks(cb)
    k = lowered_t.shape[0]
    return pl.pallas_call(
        functools.partial(_adjoint_kernel, rb, bs, sub),
        out_shape=jax.ShapeDtypeStruct((k, green.shape[1]), jnp.float32),
        grid_spec=pltpu.PrefetchScalarGridSpec(
            num_scalar_prefetch=1,
            grid=(cb // sub,),
            in_specs=[
                pl.BlockSpec((k, green.shape[0]), lambda j, m: (0, 0)),
                pl.BlockSpec((green.shape[0], bs * sub), lambda j, m: (0, j)),
            ],
            out_specs=pl.BlockSpec((k, bs * sub), lambda j, m: (0, j)),
        ),
    )(mask, lowered_t, green)


def _ag_sketch_kernel(chips, rb, nb, bs, sub, mask_ref, x_ref, g_hbm, o_ref, g_vmem, g_sem, p_all, *scratch):
    load = pltpu.make_async_copy(g_hbm, g_vmem, g_sem.at[0])
    load.start()
    me = lax.axis_index("row")
    other = lax.axis_index("col")
    chip, core = _row_greet("row", me, other, chips)
    _ag_body("row", other, chips, chip, core, x_ref, p_all, *scratch)
    k = p_all.shape[0] * p_all.shape[1] * p_all.shape[2]
    probes_t = p_all[...].reshape(k, p_all.shape[3])
    load.wait()
    for h in range(rb):
        keep = _mask_lanes(mask_ref, nb, bs, probes_t.shape[1], row=h)
        p = jnp.where(keep, probes_t, jnp.zeros_like(probes_t))
        o_ref[h // sub, :, (h % sub) * bs:(h % sub + 1) * bs] = lax.dot_general(
            p, g_vmem[h * bs:(h + 1) * bs, :], (((1,), (1,)), ((), ())), preferred_element_type=jnp.float32
        )


def _ag_sketch(x, mask, green, chips, collective_id):
    rows, width = x.shape
    rb, cb = mask.shape
    bs = green.shape[0] // rb
    sub = _half_blocks(rb)
    k = 2 * chips * rows
    return pl.pallas_call(
        functools.partial(_ag_sketch_kernel, chips, rb, cb, bs, sub),
        out_shape=jax.ShapeDtypeStruct((rb // sub, k, bs * sub), jnp.float32),
        in_specs=[
            pl.BlockSpec(memory_space=pltpu.SMEM),
            pl.BlockSpec(memory_space=pltpu.VMEM),
            pl.BlockSpec(memory_space=pl.ANY),
        ],
        out_specs=pl.BlockSpec(memory_space=pltpu.VMEM),
        scratch_shapes=[
            pltpu.VMEM(green.shape, green.dtype),
            pltpu.SemaphoreType.DMA((1,)),
            pltpu.VMEM((chips, 2, rows, width), x.dtype),
            pltpu.VMEM((rows, width), x.dtype),
            pltpu.VMEM((chips - 1, rows, width), x.dtype),
            pltpu.VMEM((chips - 1, rows, width), x.dtype),
            pltpu.SemaphoreType.DMA((chips,)),
            pltpu.SemaphoreType.DMA((chips,)),
            pltpu.SemaphoreType.DMA((chips - 1,)),
            pltpu.SemaphoreType.DMA((chips - 1,)),
        ],
        compiler_params=pltpu.CompilerParams(collective_id=collective_id, has_side_effects=True),
    )(mask, x, green)


def local(green, mask, probes):
    n_row = lax.axis_size("row")
    n_col = lax.axis_size("col")
    partial_t = _ag_sketch(probes.T, mask, green, n_row // 2, 3)
    k = partial_t.shape[1]
    sketch_t, term_t = _all_reduce_adjoint(
        partial_t.reshape(2, n_col, k // n_col, -1), mask, green, "col", "row", 0
    )
    adjoint_t = _row_reduce_scatter(term_t.reshape(n_row // 2, 2, k // n_row, -1), "row", "col", 2)
    return (sketch_t.T, adjoint_t.T)


def solution(mesh):
    in_specs = (P("row", "col"), P("row", "col"), P("col", "row"))
    out_specs = (P("row", "col"), P("col", "row"))
    return jax.shard_map(local, mesh=mesh, in_specs=in_specs, out_specs=out_specs, check_vma=False)
```

```python
import functools

import jax
import jax.numpy as jnp
from jax import lax
from jax.experimental import pallas as pl
from jax.experimental.pallas import tpu as pltpu
from jax.sharding import PartitionSpec as P

MESH = pl.DeviceIdType.MESH


def _peer(axis, other, p):
    return (other, p) if axis == "col" else (p, other)


def _greet(axis, other, me, n):
    barrier = pltpu.get_barrier_semaphore()
    for d in range(1, n):
        peer = _peer(axis, other, lax.rem(me + d, n))
        pl.semaphore_signal(barrier, 1, device_id=peer, device_id_type=MESH)
    pl.semaphore_wait(barrier, n - 1)


def _rs_kernel(axis, other_axis, n, x_ref, o_ref, recv, send_sem, recv_sem):
    me = lax.axis_index(axis)
    other = lax.axis_index(other_axis)
    _greet(axis, other, me, n)
    copies = []
    for d in range(1, n):
        peer = lax.rem(me + d, n)
        copy = pltpu.make_async_remote_copy(
            src_ref=x_ref.at[peer],
            dst_ref=recv.at[d - 1],
            send_sem=send_sem.at[d - 1],
            recv_sem=recv_sem.at[d - 1],
            device_id=_peer(axis, other, peer),
            device_id_type=MESH,
        )
        copy.start()
        copies.append(copy)
    acc = x_ref[me]
    for d, copy in enumerate(copies):
        copy.wait_recv()
        acc = acc + recv[d]
    for copy in copies:
        copy.wait_send()
    o_ref[...] = acc


def _ag_kernel(axis, other_axis, n, x_ref, o_ref, recv, send_sem, recv_sem):
    me = lax.axis_index(axis)
    other = lax.axis_index(other_axis)
    _greet(axis, other, me, n)
    copies = []
    for d in range(1, n):
        peer = lax.rem(me + d, n)
        copy = pltpu.make_async_remote_copy(
            src_ref=x_ref,
            dst_ref=recv.at[d - 1],
            send_sem=send_sem.at[d - 1],
            recv_sem=recv_sem.at[d - 1],
            device_id=_peer(axis, other, peer),
            device_id_type=MESH,
        )
        copy.start()
        copies.append(copy)
    o_ref[me] = x_ref[...]
    for d, copy in enumerate(copies):
        copy.wait_recv()
        o_ref[lax.rem(me + n - 1 - d, n)] = recv[d]
    for copy in copies:
        copy.wait_send()


def _row_greet(axis, me, other, chips):
    chip, core = me // 2, lax.rem(me, 2)
    barrier = pltpu.get_barrier_semaphore()
    pl.semaphore_signal(barrier, 1, device_id=_peer(axis, other, chip * 2 + 1 - core), device_id_type=MESH)
    for d in range(1, chips):
        peer = lax.rem(chip + d, chips) * 2 + core
        pl.semaphore_signal(barrier, 1, device_id=_peer(axis, other, peer), device_id_type=MESH)
    pl.semaphore_wait(barrier, chips)
    return chip, core


def _row_rs_kernel(axis, other_axis, chips, x_ref, o_ref, recv1, mid, recv2, s1, r1, s2, r2):
    me = lax.axis_index(axis)
    other = lax.axis_index(other_axis)
    chip, core = _row_greet(axis, me, other, chips)
    _rs_body(axis, other, chips, chip, core, x_ref, o_ref, recv1, mid, recv2, s1, r1, s2, r2)


def _rs_body(axis, other, chips, chip, core, x_ref, o_ref, recv1, mid, recv2, s1, r1, s2, r2):
    sib = _peer(axis, other, chip * 2 + 1 - core)
    first = []
    for d in list(range(1, chips)) + [0]:
        target = lax.rem(chip + d, chips)
        copy = pltpu.make_async_remote_copy(
            src_ref=x_ref.at[target, 1 - core],
            dst_ref=recv1.at[d],
            send_sem=s1.at[d],
            recv_sem=r1.at[d],
            device_id=sib,
            device_id_type=MESH,
        )
        copy.start()
        first.append(copy)
    sends = []
    for d in range(1, chips):
        target = lax.rem(chip + d, chips)
        first[d - 1].wait_recv()
        mid[d - 1] = x_ref[target, core] + recv1[d]
        copy = pltpu.make_async_remote_copy(
            src_ref=mid.at[d - 1],
            dst_ref=recv2.at[d - 1],
            send_sem=s2.at[d - 1],
            recv_sem=r2.at[d - 1],
            device_id=_peer(axis, other, target * 2 + core),
            device_id_type=MESH,
        )
        copy.start()
        sends.append(copy)
    first[chips - 1].wait_recv()
    acc = x_ref[chip, core] + recv1[0]
    for d, copy in enumerate(sends):
        copy.wait_recv()
        acc = acc + recv2[d]
    for copy in first + sends:
        copy.wait_send()
    o_ref[...] = acc


def _row_ag_kernel(axis, other_axis, chips, x_ref, o_ref, recv_s, recv_a, recv_f, s1, r1, s2, r2):
    me = lax.axis_index(axis)
    other = lax.axis_index(other_axis)
    chip, core = _row_greet(axis, me, other, chips)
    _ag_body(axis, other, chips, chip, core, x_ref, o_ref, recv_s, recv_a, recv_f, s1, r1, s2, r2)


def _ag_body(axis, other, chips, chip, core, x_ref, o_ref, recv_s, recv_a, recv_f, s1, r1, s2, r2):
    sib = _peer(axis, other, chip * 2 + 1 - core)
    to_sib = pltpu.make_async_remote_copy(
        src_ref=x_ref, dst_ref=recv_s, send_sem=s1.at[0], recv_sem=r1.at[0],
        device_id=sib, device_id_type=MESH,
    )
    to_sib.start()
    first = [to_sib]
    for d in range(1, chips):
        peer = lax.rem(chip + d, chips) * 2 + core
        copy = pltpu.make_async_remote_copy(
            src_ref=x_ref, dst_ref=recv_a.at[d - 1], send_sem=s1.at[d], recv_sem=r1.at[d],
            device_id=_peer(axis, other, peer), device_id_type=MESH,
        )
        copy.start()
        first.append(copy)
    o_ref[chip, core] = x_ref[...]
    forwards = []
    for d in range(1, chips):
        first[d].wait_recv()
        copy = pltpu.make_async_remote_copy(
            src_ref=recv_a.at[d - 1], dst_ref=recv_f.at[d - 1], send_sem=s2.at[d - 1],
            recv_sem=r2.at[d - 1], device_id=sib, device_id_type=MESH,
        )
        copy.start()
        forwards.append(copy)
        o_ref[lax.rem(chip + chips - d, chips), core] = recv_a[d - 1]
    to_sib.wait_recv()
    o_ref[chip, 1 - core] = recv_s[...]
    for d, copy in enumerate(forwards):
        copy.wait_recv()
        o_ref[lax.rem(chip + chips - 1 - d, chips), 1 - core] = recv_f[d]
    for copy in first + forwards:
        copy.wait_send()


def _mixed_rs_body(axis, other, chips, chip, core, x_ref, o_ref, ra1, ma, ra2, rb1, mb, rb2,
                   sa1, qa1, sa2, qa2, sb1, qb1, sb2, qb2):
    sib = _peer(axis, other, chip * 2 + 1 - core)
    width = x_ref.shape[-1]
    a1 = []
    for d in list(range(1, chips)) + [0]:
        target = lax.rem(chip + d, chips)
        copy = pltpu.make_async_remote_copy(
            src_ref=x_ref.at[0, target * 2 + 1 - core], dst_ref=ra1.at[d], send_sem=sa1.at[d],
            recv_sem=qa1.at[d], device_id=sib, device_id_type=MESH,
        )
        copy.start()
        a1.append(copy)
    b1 = []
    for d in range(1, chips):
        target = lax.rem(chip + d, chips)
        for half, bit in enumerate((core, 1 - core)):
            copy = pltpu.make_async_remote_copy(
                src_ref=x_ref.at[1, target * 2 + bit], dst_ref=rb1.at[d - 1, half],
                send_sem=sb1.at[d - 1, half], recv_sem=qb1.at[d - 1, half],
                device_id=_peer(axis, other, target * 2 + core), device_id_type=MESH,
            )
            copy.start()
            b1.append(copy)
    a2 = []
    for d in range(1, chips):
        target = lax.rem(chip + d, chips)
        a1[d - 1].wait_recv()
        ma[d - 1] = x_ref[0, target * 2 + core] + ra1[d]
        copy = pltpu.make_async_remote_copy(
            src_ref=ma.at[d - 1], dst_ref=ra2.at[d - 1], send_sem=sa2.at[d - 1],
            recv_sem=qa2.at[d - 1], device_id=_peer(axis, other, target * 2 + core),
            device_id_type=MESH,
        )
        copy.start()
        a2.append(copy)
    for copy in b1:
        copy.wait_recv()
    part = x_ref[1, chip * 2 + 1 - core]
    for d in range(chips - 1):
        part = part + rb1[d, 1]
    mb[...] = part
    b2 = pltpu.make_async_remote_copy(
        src_ref=mb, dst_ref=rb2, send_sem=sb2.at[0], recv_sem=qb2.at[0],
        device_id=sib, device_id_type=MESH,
    )
    b2.start()
    acc_b = x_ref[1, chip * 2 + core]
    for d in range(chips - 1):
        acc_b = acc_b + rb1[d, 0]
    a1[chips - 1].wait_recv()
    acc_a = x_ref[0, chip * 2 + core] + ra1[0]
    for d, copy in enumerate(a2):
        copy.wait_recv()
        acc_a = acc_a + ra2[d]
    b2.wait_recv()
    o_ref[:, :width] = acc_a
    o_ref[:, width:] = acc_b + rb2[...]
    for copy in a1 + b1 + a2 + [b2]:
        copy.wait_send()


def _ar_kernel(axis, other_axis, chips, row_chips, rb, cb, bs, mask_ref, x_ref, g_hbm, o_ref, a_ref,
               g_vmem, g_sem, l_all, low, t_ref, *scratch):
    row_scratch = scratch[21:]
    load = pltpu.make_async_copy(g_hbm, g_vmem, g_sem.at[0])
    load.start()
    me = lax.axis_index(axis)
    other = lax.axis_index(other_axis)
    chip, core = me // 2, lax.rem(me, 2)
    row_chip, row_core = other // 2, lax.rem(other, 2)
    barrier = pltpu.get_barrier_semaphore()
    for ax, mine, group, bit, count in ((axis, other, chip, core, chips), (other_axis, me, row_chip, row_core, row_chips)):
        pl.semaphore_signal(barrier, 1, device_id=_peer(ax, mine, group * 2 + 1 - bit), device_id_type=MESH)
        for d in range(1, count):
            peer = lax.rem(group + d, count) * 2 + bit
            pl.semaphore_signal(barrier, 1, device_id=_peer(ax, mine, peer), device_id_type=MESH)
    pl.semaphore_wait(barrier, chips + row_chips)
    _mixed_rs_body(axis, other, chips, chip, core, x_ref, o_ref, *scratch[:14])
    low[...] = o_ref[...].astype(low.dtype)
    _ag_body(axis, other, chips, chip, core, low, l_all, *scratch[14:21])
    k = l_all.shape[0] * l_all.shape[1] * l_all.shape[2]
    lowered = l_all[...].reshape(k, l_all.shape[3])
    load.wait()
    for j in range(cb):
        keep = _mask_lanes(mask_ref, rb, bs, lowered.shape[1], col=j)
        masked = jnp.where(keep, lowered, jnp.zeros_like(lowered))
        t_ref[:, :, :, j * bs:(j + 1) * bs] = jnp.dot(
            masked, g_vmem[:, j * bs:(j + 1) * bs], preferred_element_type=jnp.float32
        ).reshape(t_ref.shape[0], 2, t_ref.shape[2], bs)
    _rs_body(other_axis, me, row_chips, row_chip, row_core, t_ref, a_ref, *row_scratch)


def _all_reduce_adjoint(x, mask, green, axis, other_axis, collective_id):
    _, n, rows, half = x.shape
    chips = n // 2
    width = 2 * half
    low = jnp.bfloat16
    rb, cb = mask.shape
    bs = green.shape[0] // rb
    row_chips = lax.axis_size(other_axis) // 2
    k_rows = n * rows // (2 * row_chips)
    cols = green.shape[1]
    return pl.pallas_call(
        functools.partial(_ar_kernel, axis, other_axis, chips, row_chips, rb, cb, bs),
        out_shape=(
            jax.ShapeDtypeStruct((rows, width), x.dtype),
            jax.ShapeDtypeStruct((k_rows, cols), jnp.float32),
        ),
        in_specs=[
            pl.BlockSpec(memory_space=pltpu.SMEM),
            pl.BlockSpec(memory_space=pltpu.VMEM),
            pl.BlockSpec(memory_space=pl.ANY),
        ],
        out_specs=(pl.BlockSpec(memory_space=pltpu.VMEM), pl.BlockSpec(memory_space=pltpu.VMEM)),
        scratch_shapes=[
            pltpu.VMEM(green.shape, green.dtype),
            pltpu.SemaphoreType.DMA((1,)),
            pltpu.VMEM((chips, 2, rows, width), low),
            pltpu.VMEM((rows, width), low),
            pltpu.VMEM((row_chips, 2, k_rows, cols), jnp.float32),
            pltpu.VMEM((chips, rows, half), x.dtype),
            pltpu.VMEM((chips - 1, rows, half), x.dtype),
            pltpu.VMEM((chips - 1, rows, half), x.dtype),
            pltpu.VMEM((chips - 1, 2, rows, half), x.dtype),
            pltpu.VMEM((rows, half), x.dtype),
            pltpu.VMEM((rows, half), x.dtype),
            pltpu.SemaphoreType.DMA((chips,)),
            pltpu.SemaphoreType.DMA((chips,)),
            pltpu.SemaphoreType.DMA((chips - 1,)),
            pltpu.SemaphoreType.DMA((chips - 1,)),
            pltpu.SemaphoreType.DMA((chips - 1, 2)),
            pltpu.SemaphoreType.DMA((chips - 1, 2)),
            pltpu.SemaphoreType.DMA((1,)),
            pltpu.SemaphoreType.DMA((1,)),
            pltpu.VMEM((rows, width), low),
            pltpu.VMEM((chips - 1, rows, width), low),
            pltpu.VMEM((chips - 1, rows, width), low),
            pltpu.SemaphoreType.DMA((chips,)),
            pltpu.SemaphoreType.DMA((chips,)),
            pltpu.SemaphoreType.DMA((chips - 1,)),
            pltpu.SemaphoreType.DMA((chips - 1,)),
            pltpu.VMEM((row_chips, k_rows, cols), jnp.float32),
            pltpu.VMEM((row_chips - 1, k_rows, cols), jnp.float32),
            pltpu.VMEM((row_chips - 1, k_rows, cols), jnp.float32),
            pltpu.SemaphoreType.DMA((row_chips,)),
            pltpu.SemaphoreType.DMA((row_chips,)),
            pltpu.SemaphoreType.DMA((row_chips - 1,)),
            pltpu.SemaphoreType.DMA((row_chips - 1,)),
        ],
        compiler_params=pltpu.CompilerParams(collective_id=collective_id, has_side_effects=True),
    )(mask, x, green)


def _row_reduce_scatter(x, axis, other_axis, collective_id):
    chips, _, rows, width = x.shape
    return pl.pallas_call(
        functools.partial(_row_rs_kernel, axis, other_axis, chips),
        out_shape=jax.ShapeDtypeStruct((rows, width), x.dtype),
        in_specs=[pl.BlockSpec(memory_space=pltpu.VMEM)],
        out_specs=pl.BlockSpec(memory_space=pltpu.VMEM),
        scratch_shapes=[
            pltpu.VMEM((chips, rows, width), x.dtype),
            pltpu.VMEM((chips - 1, rows, width), x.dtype),
            pltpu.VMEM((chips - 1, rows, width), x.dtype),
            pltpu.SemaphoreType.DMA((chips,)),
            pltpu.SemaphoreType.DMA((chips,)),
            pltpu.SemaphoreType.DMA((chips - 1,)),
            pltpu.SemaphoreType.DMA((chips - 1,)),
        ],
        compiler_params=pltpu.CompilerParams(collective_id=collective_id, has_side_effects=True),
    )(x)


def _row_all_gather(x, axis, other_axis, chips, collective_id):
    rows, width = x.shape
    return pl.pallas_call(
        functools.partial(_row_ag_kernel, axis, other_axis, chips),
        out_shape=jax.ShapeDtypeStruct((chips, 2, rows, width), x.dtype),
        in_specs=[pl.BlockSpec(memory_space=pltpu.VMEM)],
        out_specs=pl.BlockSpec(memory_space=pltpu.VMEM),
        scratch_shapes=[
            pltpu.VMEM((rows, width), x.dtype),
            pltpu.VMEM((chips - 1, rows, width), x.dtype),
            pltpu.VMEM((chips - 1, rows, width), x.dtype),
            pltpu.SemaphoreType.DMA((chips,)),
            pltpu.SemaphoreType.DMA((chips,)),
            pltpu.SemaphoreType.DMA((chips - 1,)),
            pltpu.SemaphoreType.DMA((chips - 1,)),
        ],
        compiler_params=pltpu.CompilerParams(collective_id=collective_id, has_side_effects=True),
    )(x)


def _reduce_scatter(x, axis, other_axis, collective_id):
    n, rows, width = x.shape
    return pl.pallas_call(
        functools.partial(_rs_kernel, axis, other_axis, n),
        out_shape=jax.ShapeDtypeStruct((rows, width), x.dtype),
        in_specs=[pl.BlockSpec(memory_space=pltpu.VMEM)],
        out_specs=pl.BlockSpec(memory_space=pltpu.VMEM),
        scratch_shapes=[
            pltpu.VMEM((n - 1, rows, width), x.dtype),
            pltpu.SemaphoreType.DMA((n - 1,)),
            pltpu.SemaphoreType.DMA((n - 1,)),
        ],
        compiler_params=pltpu.CompilerParams(collective_id=collective_id, has_side_effects=True),
    )(x)


def _all_gather(x, axis, other_axis, n, collective_id):
    rows, width = x.shape
    return pl.pallas_call(
        functools.partial(_ag_kernel, axis, other_axis, n),
        out_shape=jax.ShapeDtypeStruct((n, rows, width), x.dtype),
        in_specs=[pl.BlockSpec(memory_space=pltpu.VMEM)],
        out_specs=pl.BlockSpec(memory_space=pltpu.VMEM),
        scratch_shapes=[
            pltpu.VMEM((n - 1, rows, width), x.dtype),
            pltpu.SemaphoreType.DMA((n - 1,)),
            pltpu.SemaphoreType.DMA((n - 1,)),
        ],
        compiler_params=pltpu.CompilerParams(collective_id=collective_id, has_side_effects=True),
    )(x)


def _mask_lanes(mask_ref, nb, bs, width, row=None, col=None):
    blk = lax.broadcasted_iota(jnp.int32, (1, width), 1) // bs
    keep = jnp.zeros((1, width), jnp.int32)
    for b in range(nb):
        value = mask_ref[row, b] if col is None else mask_ref[b, col]
        keep = jnp.where(blk == b, value, keep)
    return keep != 0


def _sub_blocks(nb):
    return 4 if nb % 4 == 0 else (2 if nb % 2 == 0 else 1)


def _half_blocks(nb):
    return nb // 2


def _sketch_kernel(nb, bs, sub, mask_ref, g_ref, p_ref, o_ref):
    i = pl.program_id(0)
    for h in range(sub):
        keep = _mask_lanes(mask_ref, nb, bs, p_ref.shape[1], row=i * sub + h)
        p = jnp.where(keep, p_ref[...], jnp.zeros_like(p_ref))
        o_ref[:, h * bs:(h + 1) * bs] = lax.dot_general(
            p, g_ref[h * bs:(h + 1) * bs, :], (((1,), (1,)), ((), ())), preferred_element_type=jnp.float32
        )


def _adjoint_kernel(nb, bs, sub, mask_ref, l_ref, g_ref, o_ref):
    j = pl.program_id(0)
    for h in range(sub):
        keep = _mask_lanes(mask_ref, nb, bs, l_ref.shape[1], col=j * sub + h)
        lowered = jnp.where(keep, l_ref[...], jnp.zeros_like(l_ref))
        o_ref[:, h * bs:(h + 1) * bs] = jnp.dot(
            lowered, g_ref[:, h * bs:(h + 1) * bs], preferred_element_type=jnp.float32
        )


def _sketch_partial(mask, green, probes_t):
    rb, cb = mask.shape
    bs = green.shape[0] // rb
    sub = _half_blocks(rb)
    k = probes_t.shape[0]
    return pl.pallas_call(
        functools.partial(_sketch_kernel, cb, bs, sub),
        out_shape=jax.ShapeDtypeStruct((rb // sub, k, bs * sub), jnp.float32),
        grid_spec=pltpu.PrefetchScalarGridSpec(
            num_scalar_prefetch=1,
            grid=(rb // sub,),
            in_specs=[
                pl.BlockSpec((bs * sub, green.shape[1]), lambda i, m: (i, 0)),
                pl.BlockSpec((k, green.shape[1]), lambda i, m: (0, 0)),
            ],
            out_specs=pl.BlockSpec((None, k, bs * sub), lambda i, m: (i, 0, 0)),
        ),
    )(mask, green, probes_t)


def _adjoint_partial(mask, lowered_t, green):
    rb, cb = mask.shape
    bs = green.shape[0] // rb
    sub = _sub_blocks(cb)
    k = lowered_t.shape[0]
    return pl.pallas_call(
        functools.partial(_adjoint_kernel, rb, bs, sub),
        out_shape=jax.ShapeDtypeStruct((k, green.shape[1]), jnp.float32),
        grid_spec=pltpu.PrefetchScalarGridSpec(
            num_scalar_prefetch=1,
            grid=(cb // sub,),
            in_specs=[
                pl.BlockSpec((k, green.shape[0]), lambda j, m: (0, 0)),
                pl.BlockSpec((green.shape[0], bs * sub), lambda j, m: (0, j)),
            ],
            out_specs=pl.BlockSpec((k, bs * sub), lambda j, m: (0, j)),
        ),
    )(mask, lowered_t, green)


def _ag_sketch_kernel(chips, rb, nb, bs, sub, mask_ref, x_ref, g_hbm, o_ref, g_vmem, g_sem, p_all, *scratch):
    load = pltpu.make_async_copy(g_hbm, g_vmem, g_sem.at[0])
    load.start()
    me = lax.axis_index("row")
    other = lax.axis_index("col")
    chip, core = _row_greet("row", me, other, chips)
    _ag_body("row", other, chips, chip, core, x_ref, p_all, *scratch)
    k = p_all.shape[0] * p_all.shape[1] * p_all.shape[2]
    probes_t = p_all[...].reshape(k, p_all.shape[3])
    load.wait()
    for h in range(rb):
        keep = _mask_lanes(mask_ref, nb, bs, probes_t.shape[1], row=h)
        p = jnp.where(keep, probes_t, jnp.zeros_like(probes_t))
        o_ref[h // sub, :, (h % sub) * bs:(h % sub + 1) * bs] = lax.dot_general(
            p, g_vmem[h * bs:(h + 1) * bs, :], (((1,), (1,)), ((), ())), preferred_element_type=jnp.float32
        )


def _ag_sketch(x, mask, green, chips, collective_id):
    rows, width = x.shape
    rb, cb = mask.shape
    bs = green.shape[0] // rb
    sub = _half_blocks(rb)
    k = 2 * chips * rows
    return pl.pallas_call(
        functools.partial(_ag_sketch_kernel, chips, rb, cb, bs, sub),
        out_shape=jax.ShapeDtypeStruct((rb // sub, k, bs * sub), jnp.float32),
        in_specs=[
            pl.BlockSpec(memory_space=pltpu.SMEM),
            pl.BlockSpec(memory_space=pltpu.VMEM),
            pl.BlockSpec(memory_space=pl.ANY),
        ],
        out_specs=pl.BlockSpec(memory_space=pltpu.VMEM),
        scratch_shapes=[
            pltpu.VMEM(green.shape, green.dtype),
            pltpu.SemaphoreType.DMA((1,)),
            pltpu.VMEM((chips, 2, rows, width), x.dtype),
            pltpu.VMEM((rows, width), x.dtype),
            pltpu.VMEM((chips - 1, rows, width), x.dtype),
            pltpu.VMEM((chips - 1, rows, width), x.dtype),
            pltpu.SemaphoreType.DMA((chips,)),
            pltpu.SemaphoreType.DMA((chips,)),
            pltpu.SemaphoreType.DMA((chips - 1,)),
            pltpu.SemaphoreType.DMA((chips - 1,)),
        ],
        compiler_params=pltpu.CompilerParams(collective_id=collective_id, has_side_effects=True),
    )(mask, x, green)


def local(green, mask, probes):
    n_row = lax.axis_size("row")
    n_col = lax.axis_size("col")
    partial_t = _ag_sketch(probes.T, mask, green, n_row // 2, 3)
    k = partial_t.shape[1]
    sketch_t, adjoint_t = _all_reduce_adjoint(
        partial_t.reshape(2, n_col, k // n_col, -1), mask, green, "col", "row", 0
    )
    return (sketch_t.T, adjoint_t.T)


def solution(mesh):
    in_specs = (P("row", "col"), P("row", "col"), P("col", "row"))
    out_specs = (P("row", "col"), P("col", "row"))
    return jax.shard_map(local, mesh=mesh, in_specs=in_specs, out_specs=out_specs, check_vma=False)
```

```python
import functools

import jax
import jax.numpy as jnp
from jax import lax
from jax.experimental import pallas as pl
from jax.experimental.pallas import tpu as pltpu
from jax.sharding import PartitionSpec as P

MESH = pl.DeviceIdType.MESH


def _peer(axis, other, p):
    return (other, p) if axis == "col" else (p, other)


def _greet(axis, other, me, n):
    barrier = pltpu.get_barrier_semaphore()
    for d in range(1, n):
        peer = _peer(axis, other, lax.rem(me + d, n))
        pl.semaphore_signal(barrier, 1, device_id=peer, device_id_type=MESH)
    pl.semaphore_wait(barrier, n - 1)


def _rs_kernel(axis, other_axis, n, x_ref, o_ref, recv, send_sem, recv_sem):
    me = lax.axis_index(axis)
    other = lax.axis_index(other_axis)
    _greet(axis, other, me, n)
    copies = []
    for d in range(1, n):
        peer = lax.rem(me + d, n)
        copy = pltpu.make_async_remote_copy(
            src_ref=x_ref.at[peer],
            dst_ref=recv.at[d - 1],
            send_sem=send_sem.at[d - 1],
            recv_sem=recv_sem.at[d - 1],
            device_id=_peer(axis, other, peer),
            device_id_type=MESH,
        )
        copy.start()
        copies.append(copy)
    acc = x_ref[me]
    for d, copy in enumerate(copies):
        copy.wait_recv()
        acc = acc + recv[d]
    for copy in copies:
        copy.wait_send()
    o_ref[...] = acc


def _ag_kernel(axis, other_axis, n, x_ref, o_ref, recv, send_sem, recv_sem):
    me = lax.axis_index(axis)
    other = lax.axis_index(other_axis)
    _greet(axis, other, me, n)
    copies = []
    for d in range(1, n):
        peer = lax.rem(me + d, n)
        copy = pltpu.make_async_remote_copy(
            src_ref=x_ref,
            dst_ref=recv.at[d - 1],
            send_sem=send_sem.at[d - 1],
            recv_sem=recv_sem.at[d - 1],
            device_id=_peer(axis, other, peer),
            device_id_type=MESH,
        )
        copy.start()
        copies.append(copy)
    o_ref[me] = x_ref[...]
    for d, copy in enumerate(copies):
        copy.wait_recv()
        o_ref[lax.rem(me + n - 1 - d, n)] = recv[d]
    for copy in copies:
        copy.wait_send()


def _row_greet(axis, me, other, chips):
    chip, core = me // 2, lax.rem(me, 2)
    barrier = pltpu.get_barrier_semaphore()
    pl.semaphore_signal(barrier, 1, device_id=_peer(axis, other, chip * 2 + 1 - core), device_id_type=MESH)
    for d in range(1, chips):
        peer = lax.rem(chip + d, chips) * 2 + core
        pl.semaphore_signal(barrier, 1, device_id=_peer(axis, other, peer), device_id_type=MESH)
    pl.semaphore_wait(barrier, chips)
    return chip, core


def _row_rs_kernel(axis, other_axis, chips, x_ref, o_ref, recv1, mid, recv2, s1, r1, s2, r2):
    me = lax.axis_index(axis)
    other = lax.axis_index(other_axis)
    chip, core = _row_greet(axis, me, other, chips)
    _rs_body(axis, other, chips, chip, core, x_ref, o_ref, recv1, mid, recv2, s1, r1, s2, r2)


def _rs_body(axis, other, chips, chip, core, x_ref, o_ref, recv1, mid, recv2, s1, r1, s2, r2):
    sib = _peer(axis, other, chip * 2 + 1 - core)
    first = []
    for d in list(range(1, chips)) + [0]:
        target = lax.rem(chip + d, chips)
        copy = pltpu.make_async_remote_copy(
            src_ref=x_ref.at[target, 1 - core],
            dst_ref=recv1.at[d],
            send_sem=s1.at[d],
            recv_sem=r1.at[d],
            device_id=sib,
            device_id_type=MESH,
        )
        copy.start()
        first.append(copy)
    sends = []
    for d in range(1, chips):
        target = lax.rem(chip + d, chips)
        first[d - 1].wait_recv()
        mid[d - 1] = x_ref[target, core] + recv1[d]
        copy = pltpu.make_async_remote_copy(
            src_ref=mid.at[d - 1],
            dst_ref=recv2.at[d - 1],
            send_sem=s2.at[d - 1],
            recv_sem=r2.at[d - 1],
            device_id=_peer(axis, other, target * 2 + core),
            device_id_type=MESH,
        )
        copy.start()
        sends.append(copy)
    first[chips - 1].wait_recv()
    acc = x_ref[chip, core] + recv1[0]
    for d, copy in enumerate(sends):
        copy.wait_recv()
        acc = acc + recv2[d]
    for copy in first + sends:
        copy.wait_send()
    o_ref[...] = acc


def _row_ag_kernel(axis, other_axis, chips, x_ref, o_ref, recv_s, recv_a, recv_f, s1, r1, s2, r2):
    me = lax.axis_index(axis)
    other = lax.axis_index(other_axis)
    chip, core = _row_greet(axis, me, other, chips)
    _ag_body(axis, other, chips, chip, core, x_ref, o_ref, recv_s, recv_a, recv_f, s1, r1, s2, r2)


def _ag_body(axis, other, chips, chip, core, x_ref, o_ref, recv_s, recv_a, recv_f, s1, r1, s2, r2):
    sib = _peer(axis, other, chip * 2 + 1 - core)
    to_sib = pltpu.make_async_remote_copy(
        src_ref=x_ref, dst_ref=recv_s, send_sem=s1.at[0], recv_sem=r1.at[0],
        device_id=sib, device_id_type=MESH,
    )
    to_sib.start()
    first = [to_sib]
    for d in range(1, chips):
        peer = lax.rem(chip + d, chips) * 2 + core
        copy = pltpu.make_async_remote_copy(
            src_ref=x_ref, dst_ref=recv_a.at[d - 1], send_sem=s1.at[d], recv_sem=r1.at[d],
            device_id=_peer(axis, other, peer), device_id_type=MESH,
        )
        copy.start()
        first.append(copy)
    o_ref[chip, core] = x_ref[...]
    forwards = []
    for d in range(1, chips):
        first[d].wait_recv()
        copy = pltpu.make_async_remote_copy(
            src_ref=recv_a.at[d - 1], dst_ref=recv_f.at[d - 1], send_sem=s2.at[d - 1],
            recv_sem=r2.at[d - 1], device_id=sib, device_id_type=MESH,
        )
        copy.start()
        forwards.append(copy)
        o_ref[lax.rem(chip + chips - d, chips), core] = recv_a[d - 1]
    to_sib.wait_recv()
    o_ref[chip, 1 - core] = recv_s[...]
    for d, copy in enumerate(forwards):
        copy.wait_recv()
        o_ref[lax.rem(chip + chips - 1 - d, chips), 1 - core] = recv_f[d]
    for copy in first + forwards:
        copy.wait_send()


def _mixed_rs_body(axis, other, chips, chip, core, x_ref, o_ref, ra1, ma, ra2, rb1, mb, rb2,
                   sa1, qa1, sa2, qa2, sb1, qb1, sb2, qb2):
    sib = _peer(axis, other, chip * 2 + 1 - core)
    width = x_ref.shape[-1]
    a1 = []
    for d in list(range(1, chips)) + [0]:
        target = lax.rem(chip + d, chips)
        copy = pltpu.make_async_remote_copy(
            src_ref=x_ref.at[0, target * 2 + 1 - core], dst_ref=ra1.at[d], send_sem=sa1.at[d],
            recv_sem=qa1.at[d], device_id=sib, device_id_type=MESH,
        )
        copy.start()
        a1.append(copy)
    b1 = []
    for d in range(1, chips):
        target = lax.rem(chip + d, chips)
        for half, bit in enumerate((core, 1 - core)):
            copy = pltpu.make_async_remote_copy(
                src_ref=x_ref.at[1, target * 2 + bit], dst_ref=rb1.at[d - 1, half],
                send_sem=sb1.at[d - 1, half], recv_sem=qb1.at[d - 1, half],
                device_id=_peer(axis, other, target * 2 + core), device_id_type=MESH,
            )
            copy.start()
            b1.append(copy)
    a2 = []
    for d in range(1, chips):
        target = lax.rem(chip + d, chips)
        a1[d - 1].wait_recv()
        ma[d - 1] = x_ref[0, target * 2 + core] + ra1[d]
        copy = pltpu.make_async_remote_copy(
            src_ref=ma.at[d - 1], dst_ref=ra2.at[d - 1], send_sem=sa2.at[d - 1],
            recv_sem=qa2.at[d - 1], device_id=_peer(axis, other, target * 2 + core),
            device_id_type=MESH,
        )
        copy.start()
        a2.append(copy)
    for copy in b1:
        copy.wait_recv()
    part = x_ref[1, chip * 2 + 1 - core]
    for d in range(chips - 1):
        part = part + rb1[d, 1]
    mb[...] = part
    b2 = pltpu.make_async_remote_copy(
        src_ref=mb, dst_ref=rb2, send_sem=sb2.at[0], recv_sem=qb2.at[0],
        device_id=sib, device_id_type=MESH,
    )
    b2.start()
    acc_b = x_ref[1, chip * 2 + core]
    for d in range(chips - 1):
        acc_b = acc_b + rb1[d, 0]
    a1[chips - 1].wait_recv()
    acc_a = x_ref[0, chip * 2 + core] + ra1[0]
    for d, copy in enumerate(a2):
        copy.wait_recv()
        acc_a = acc_a + ra2[d]
    b2.wait_recv()
    o_ref[:, :width] = acc_a
    o_ref[:, width:] = acc_b + rb2[...]
    for copy in a1 + b1 + a2 + [b2]:
        copy.wait_send()


def _ar_kernel(axis, other_axis, chips, row_chips, rb, cb, bs, mask_ref, p_ref, g_hbm, o_ref, a_ref,
               g_vmem, g_sem, l_all, low, t_ref, x_ref, p_all, *scratch):
    row_scratch = scratch[21:28]
    load = pltpu.make_async_copy(g_hbm, g_vmem, g_sem.at[0])
    load.start()
    me = lax.axis_index(axis)
    other = lax.axis_index(other_axis)
    chip, core = me // 2, lax.rem(me, 2)
    row_chip, row_core = other // 2, lax.rem(other, 2)
    barrier = pltpu.get_barrier_semaphore()
    for ax, mine, group, bit, count in ((axis, other, chip, core, chips), (other_axis, me, row_chip, row_core, row_chips)):
        pl.semaphore_signal(barrier, 1, device_id=_peer(ax, mine, group * 2 + 1 - bit), device_id_type=MESH)
        for d in range(1, count):
            peer = lax.rem(group + d, count) * 2 + bit
            pl.semaphore_signal(barrier, 1, device_id=_peer(ax, mine, peer), device_id_type=MESH)
    pl.semaphore_wait(barrier, chips + row_chips)
    _ag_body(other_axis, me, row_chips, row_chip, row_core, p_ref, p_all, *scratch[28:])
    k = p_all.shape[0] * p_all.shape[1] * p_all.shape[2]
    probes_t = p_all[...].reshape(k, p_all.shape[3])
    load.wait()
    sub = x_ref.shape[-1] // bs
    for h in range(rb):
        keep = _mask_lanes(mask_ref, cb, bs, probes_t.shape[1], row=h)
        p = jnp.where(keep, probes_t, jnp.zeros_like(probes_t))
        x_ref[h // sub, :, :, (h % sub) * bs:(h % sub + 1) * bs] = lax.dot_general(
            p, g_vmem[h * bs:(h + 1) * bs, :], (((1,), (1,)), ((), ())), preferred_element_type=jnp.float32
        ).reshape(x_ref.shape[1], x_ref.shape[2], bs)
    _mixed_rs_body(axis, other, chips, chip, core, x_ref, o_ref, *scratch[:14])
    low[...] = o_ref[...].astype(low.dtype)
    _ag_body(axis, other, chips, chip, core, low, l_all, *scratch[14:21])
    k = l_all.shape[0] * l_all.shape[1] * l_all.shape[2]
    lowered = l_all[...].reshape(k, l_all.shape[3])
    for j in range(cb):
        keep = _mask_lanes(mask_ref, rb, bs, lowered.shape[1], col=j)
        masked = jnp.where(keep, lowered, jnp.zeros_like(lowered))
        t_ref[:, :, :, j * bs:(j + 1) * bs] = jnp.dot(
            masked, g_vmem[:, j * bs:(j + 1) * bs], preferred_element_type=jnp.float32
        ).reshape(t_ref.shape[0], 2, t_ref.shape[2], bs)
    _rs_body(other_axis, me, row_chips, row_chip, row_core, t_ref, a_ref, *row_scratch)


def _all_reduce_adjoint(probes_t, mask, green, axis, other_axis, collective_id):
    n = lax.axis_size(axis)
    rows = probes_t.shape[0] * lax.axis_size(other_axis) // n
    half = green.shape[0] // 2
    x = jax.ShapeDtypeStruct((2, n, rows, half), jnp.float32)
    chips = n // 2
    width = 2 * half
    low = jnp.bfloat16
    rb, cb = mask.shape
    bs = green.shape[0] // rb
    row_chips = lax.axis_size(other_axis) // 2
    k_rows = n * rows // (2 * row_chips)
    cols = green.shape[1]
    return pl.pallas_call(
        functools.partial(_ar_kernel, axis, other_axis, chips, row_chips, rb, cb, bs),
        out_shape=(
            jax.ShapeDtypeStruct((rows, width), jnp.float32),
            jax.ShapeDtypeStruct((k_rows, cols), jnp.float32),
        ),
        in_specs=[
            pl.BlockSpec(memory_space=pltpu.SMEM),
            pl.BlockSpec(memory_space=pltpu.VMEM),
            pl.BlockSpec(memory_space=pl.ANY),
        ],
        out_specs=(pl.BlockSpec(memory_space=pltpu.VMEM), pl.BlockSpec(memory_space=pltpu.VMEM)),
        scratch_shapes=[
            pltpu.VMEM(green.shape, green.dtype),
            pltpu.SemaphoreType.DMA((1,)),
            pltpu.VMEM((chips, 2, rows, width), low),
            pltpu.VMEM((rows, width), low),
            pltpu.VMEM((row_chips, 2, k_rows, cols), jnp.float32),
            pltpu.VMEM((2, n, rows, half), jnp.float32),
            pltpu.VMEM((row_chips, 2) + probes_t.shape, probes_t.dtype),
            pltpu.VMEM((chips, rows, half), x.dtype),
            pltpu.VMEM((chips - 1, rows, half), x.dtype),
            pltpu.VMEM((chips - 1, rows, half), x.dtype),
            pltpu.VMEM((chips - 1, 2, rows, half), x.dtype),
            pltpu.VMEM((rows, half), x.dtype),
            pltpu.VMEM((rows, half), x.dtype),
            pltpu.SemaphoreType.DMA((chips,)),
            pltpu.SemaphoreType.DMA((chips,)),
            pltpu.SemaphoreType.DMA((chips - 1,)),
            pltpu.SemaphoreType.DMA((chips - 1,)),
            pltpu.SemaphoreType.DMA((chips - 1, 2)),
            pltpu.SemaphoreType.DMA((chips - 1, 2)),
            pltpu.SemaphoreType.DMA((1,)),
            pltpu.SemaphoreType.DMA((1,)),
            pltpu.VMEM((rows, width), low),
            pltpu.VMEM((chips - 1, rows, width), low),
            pltpu.VMEM((chips - 1, rows, width), low),
            pltpu.SemaphoreType.DMA((chips,)),
            pltpu.SemaphoreType.DMA((chips,)),
            pltpu.SemaphoreType.DMA((chips - 1,)),
            pltpu.SemaphoreType.DMA((chips - 1,)),
            pltpu.VMEM((row_chips, k_rows, cols), jnp.float32),
            pltpu.VMEM((row_chips - 1, k_rows, cols), jnp.float32),
            pltpu.VMEM((row_chips - 1, k_rows, cols), jnp.float32),
            pltpu.SemaphoreType.DMA((row_chips,)),
            pltpu.SemaphoreType.DMA((row_chips,)),
            pltpu.SemaphoreType.DMA((row_chips - 1,)),
            pltpu.SemaphoreType.DMA((row_chips - 1,)),
            pltpu.VMEM(probes_t.shape, probes_t.dtype),
            pltpu.VMEM((row_chips - 1,) + probes_t.shape, probes_t.dtype),
            pltpu.VMEM((row_chips - 1,) + probes_t.shape, probes_t.dtype),
            pltpu.SemaphoreType.DMA((row_chips,)),
            pltpu.SemaphoreType.DMA((row_chips,)),
            pltpu.SemaphoreType.DMA((row_chips - 1,)),
            pltpu.SemaphoreType.DMA((row_chips - 1,)),
        ],
        compiler_params=pltpu.CompilerParams(collective_id=collective_id, has_side_effects=True),
    )(mask, probes_t, green)


def _row_reduce_scatter(x, axis, other_axis, collective_id):
    chips, _, rows, width = x.shape
    return pl.pallas_call(
        functools.partial(_row_rs_kernel, axis, other_axis, chips),
        out_shape=jax.ShapeDtypeStruct((rows, width), x.dtype),
        in_specs=[pl.BlockSpec(memory_space=pltpu.VMEM)],
        out_specs=pl.BlockSpec(memory_space=pltpu.VMEM),
        scratch_shapes=[
            pltpu.VMEM((chips, rows, width), x.dtype),
            pltpu.VMEM((chips - 1, rows, width), x.dtype),
            pltpu.VMEM((chips - 1, rows, width), x.dtype),
            pltpu.SemaphoreType.DMA((chips,)),
            pltpu.SemaphoreType.DMA((chips,)),
            pltpu.SemaphoreType.DMA((chips - 1,)),
            pltpu.SemaphoreType.DMA((chips - 1,)),
        ],
        compiler_params=pltpu.CompilerParams(collective_id=collective_id, has_side_effects=True),
    )(x)


def _row_all_gather(x, axis, other_axis, chips, collective_id):
    rows, width = x.shape
    return pl.pallas_call(
        functools.partial(_row_ag_kernel, axis, other_axis, chips),
        out_shape=jax.ShapeDtypeStruct((chips, 2, rows, width), x.dtype),
        in_specs=[pl.BlockSpec(memory_space=pltpu.VMEM)],
        out_specs=pl.BlockSpec(memory_space=pltpu.VMEM),
        scratch_shapes=[
            pltpu.VMEM((rows, width), x.dtype),
            pltpu.VMEM((chips - 1, rows, width), x.dtype),
            pltpu.VMEM((chips - 1, rows, width), x.dtype),
            pltpu.SemaphoreType.DMA((chips,)),
            pltpu.SemaphoreType.DMA((chips,)),
            pltpu.SemaphoreType.DMA((chips - 1,)),
            pltpu.SemaphoreType.DMA((chips - 1,)),
        ],
        compiler_params=pltpu.CompilerParams(collective_id=collective_id, has_side_effects=True),
    )(x)


def _reduce_scatter(x, axis, other_axis, collective_id):
    n, rows, width = x.shape
    return pl.pallas_call(
        functools.partial(_rs_kernel, axis, other_axis, n),
        out_shape=jax.ShapeDtypeStruct((rows, width), x.dtype),
        in_specs=[pl.BlockSpec(memory_space=pltpu.VMEM)],
        out_specs=pl.BlockSpec(memory_space=pltpu.VMEM),
        scratch_shapes=[
            pltpu.VMEM((n - 1, rows, width), x.dtype),
            pltpu.SemaphoreType.DMA((n - 1,)),
            pltpu.SemaphoreType.DMA((n - 1,)),
        ],
        compiler_params=pltpu.CompilerParams(collective_id=collective_id, has_side_effects=True),
    )(x)


def _all_gather(x, axis, other_axis, n, collective_id):
    rows, width = x.shape
    return pl.pallas_call(
        functools.partial(_ag_kernel, axis, other_axis, n),
        out_shape=jax.ShapeDtypeStruct((n, rows, width), x.dtype),
        in_specs=[pl.BlockSpec(memory_space=pltpu.VMEM)],
        out_specs=pl.BlockSpec(memory_space=pltpu.VMEM),
        scratch_shapes=[
            pltpu.VMEM((n - 1, rows, width), x.dtype),
            pltpu.SemaphoreType.DMA((n - 1,)),
            pltpu.SemaphoreType.DMA((n - 1,)),
        ],
        compiler_params=pltpu.CompilerParams(collective_id=collective_id, has_side_effects=True),
    )(x)


def _mask_lanes(mask_ref, nb, bs, width, row=None, col=None):
    blk = lax.broadcasted_iota(jnp.int32, (1, width), 1) // bs
    keep = jnp.zeros((1, width), jnp.int32)
    for b in range(nb):
        value = mask_ref[row, b] if col is None else mask_ref[b, col]
        keep = jnp.where(blk == b, value, keep)
    return keep != 0


def _sub_blocks(nb):
    return 4 if nb % 4 == 0 else (2 if nb % 2 == 0 else 1)


def _half_blocks(nb):
    return nb // 2


def _sketch_kernel(nb, bs, sub, mask_ref, g_ref, p_ref, o_ref):
    i = pl.program_id(0)
    for h in range(sub):
        keep = _mask_lanes(mask_ref, nb, bs, p_ref.shape[1], row=i * sub + h)
        p = jnp.where(keep, p_ref[...], jnp.zeros_like(p_ref))
        o_ref[:, h * bs:(h + 1) * bs] = lax.dot_general(
            p, g_ref[h * bs:(h + 1) * bs, :], (((1,), (1,)), ((), ())), preferred_element_type=jnp.float32
        )


def _adjoint_kernel(nb, bs, sub, mask_ref, l_ref, g_ref, o_ref):
    j = pl.program_id(0)
    for h in range(sub):
        keep = _mask_lanes(mask_ref, nb, bs, l_ref.shape[1], col=j * sub + h)
        lowered = jnp.where(keep, l_ref[...], jnp.zeros_like(l_ref))
        o_ref[:, h * bs:(h + 1) * bs] = jnp.dot(
            lowered, g_ref[:, h * bs:(h + 1) * bs], preferred_element_type=jnp.float32
        )


def _sketch_partial(mask, green, probes_t):
    rb, cb = mask.shape
    bs = green.shape[0] // rb
    sub = _half_blocks(rb)
    k = probes_t.shape[0]
    return pl.pallas_call(
        functools.partial(_sketch_kernel, cb, bs, sub),
        out_shape=jax.ShapeDtypeStruct((rb // sub, k, bs * sub), jnp.float32),
        grid_spec=pltpu.PrefetchScalarGridSpec(
            num_scalar_prefetch=1,
            grid=(rb // sub,),
            in_specs=[
                pl.BlockSpec((bs * sub, green.shape[1]), lambda i, m: (i, 0)),
                pl.BlockSpec((k, green.shape[1]), lambda i, m: (0, 0)),
            ],
            out_specs=pl.BlockSpec((None, k, bs * sub), lambda i, m: (i, 0, 0)),
        ),
    )(mask, green, probes_t)


def _adjoint_partial(mask, lowered_t, green):
    rb, cb = mask.shape
    bs = green.shape[0] // rb
    sub = _sub_blocks(cb)
    k = lowered_t.shape[0]
    return pl.pallas_call(
        functools.partial(_adjoint_kernel, rb, bs, sub),
        out_shape=jax.ShapeDtypeStruct((k, green.shape[1]), jnp.float32),
        grid_spec=pltpu.PrefetchScalarGridSpec(
            num_scalar_prefetch=1,
            grid=(cb // sub,),
            in_specs=[
                pl.BlockSpec((k, green.shape[0]), lambda j, m: (0, 0)),
                pl.BlockSpec((green.shape[0], bs * sub), lambda j, m: (0, j)),
            ],
            out_specs=pl.BlockSpec((k, bs * sub), lambda j, m: (0, j)),
        ),
    )(mask, lowered_t, green)


def _ag_sketch_kernel(chips, rb, nb, bs, sub, mask_ref, x_ref, g_hbm, o_ref, g_vmem, g_sem, p_all, *scratch):
    load = pltpu.make_async_copy(g_hbm, g_vmem, g_sem.at[0])
    load.start()
    me = lax.axis_index("row")
    other = lax.axis_index("col")
    chip, core = _row_greet("row", me, other, chips)
    _ag_body("row", other, chips, chip, core, x_ref, p_all, *scratch)
    k = p_all.shape[0] * p_all.shape[1] * p_all.shape[2]
    probes_t = p_all[...].reshape(k, p_all.shape[3])
    load.wait()
    for h in range(rb):
        keep = _mask_lanes(mask_ref, nb, bs, probes_t.shape[1], row=h)
        p = jnp.where(keep, probes_t, jnp.zeros_like(probes_t))
        o_ref[h // sub, :, (h % sub) * bs:(h % sub + 1) * bs] = lax.dot_general(
            p, g_vmem[h * bs:(h + 1) * bs, :], (((1,), (1,)), ((), ())), preferred_element_type=jnp.float32
        )


def _ag_sketch(x, mask, green, chips, collective_id):
    rows, width = x.shape
    rb, cb = mask.shape
    bs = green.shape[0] // rb
    sub = _half_blocks(rb)
    k = 2 * chips * rows
    return pl.pallas_call(
        functools.partial(_ag_sketch_kernel, chips, rb, cb, bs, sub),
        out_shape=jax.ShapeDtypeStruct((rb // sub, k, bs * sub), jnp.float32),
        in_specs=[
            pl.BlockSpec(memory_space=pltpu.SMEM),
            pl.BlockSpec(memory_space=pltpu.VMEM),
            pl.BlockSpec(memory_space=pl.ANY),
        ],
        out_specs=pl.BlockSpec(memory_space=pltpu.VMEM),
        scratch_shapes=[
            pltpu.VMEM(green.shape, green.dtype),
            pltpu.SemaphoreType.DMA((1,)),
            pltpu.VMEM((chips, 2, rows, width), x.dtype),
            pltpu.VMEM((rows, width), x.dtype),
            pltpu.VMEM((chips - 1, rows, width), x.dtype),
            pltpu.VMEM((chips - 1, rows, width), x.dtype),
            pltpu.SemaphoreType.DMA((chips,)),
            pltpu.SemaphoreType.DMA((chips,)),
            pltpu.SemaphoreType.DMA((chips - 1,)),
            pltpu.SemaphoreType.DMA((chips - 1,)),
        ],
        compiler_params=pltpu.CompilerParams(collective_id=collective_id, has_side_effects=True),
    )(mask, x, green)


def local(green, mask, probes):
    n_row = lax.axis_size("row")
    n_col = lax.axis_size("col")
    sketch_t, adjoint_t = _all_reduce_adjoint(probes.T, mask, green, "col", "row", 0)
    return (sketch_t.T, adjoint_t.T)


def solution(mesh):
    in_specs = (P("row", "col"), P("row", "col"), P("col", "row"))
    out_specs = (P("row", "col"), P("col", "row"))
    return jax.shard_map(local, mesh=mesh, in_specs=in_specs, out_specs=out_specs, check_vma=False)
```

```python
import functools

import jax
import jax.numpy as jnp
from jax import lax
from jax.experimental import pallas as pl
from jax.experimental.pallas import tpu as pltpu
from jax.sharding import PartitionSpec as P

MESH = pl.DeviceIdType.MESH


def _peer(axis, other, p):
    return (other, p) if axis == "col" else (p, other)


def _greet(axis, other, me, n):
    barrier = pltpu.get_barrier_semaphore()
    for d in range(1, n):
        peer = _peer(axis, other, lax.rem(me + d, n))
        pl.semaphore_signal(barrier, 1, device_id=peer, device_id_type=MESH)
    pl.semaphore_wait(barrier, n - 1)


def _rs_kernel(axis, other_axis, n, x_ref, o_ref, recv, send_sem, recv_sem):
    me = lax.axis_index(axis)
    other = lax.axis_index(other_axis)
    _greet(axis, other, me, n)
    copies = []
    for d in range(1, n):
        peer = lax.rem(me + d, n)
        copy = pltpu.make_async_remote_copy(
            src_ref=x_ref.at[peer],
            dst_ref=recv.at[d - 1],
            send_sem=send_sem.at[d - 1],
            recv_sem=recv_sem.at[d - 1],
            device_id=_peer(axis, other, peer),
            device_id_type=MESH,
        )
        copy.start()
        copies.append(copy)
    acc = x_ref[me]
    for d, copy in enumerate(copies):
        copy.wait_recv()
        acc = acc + recv[d]
    for copy in copies:
        copy.wait_send()
    o_ref[...] = acc


def _ag_kernel(axis, other_axis, n, x_ref, o_ref, recv, send_sem, recv_sem):
    me = lax.axis_index(axis)
    other = lax.axis_index(other_axis)
    _greet(axis, other, me, n)
    copies = []
    for d in range(1, n):
        peer = lax.rem(me + d, n)
        copy = pltpu.make_async_remote_copy(
            src_ref=x_ref,
            dst_ref=recv.at[d - 1],
            send_sem=send_sem.at[d - 1],
            recv_sem=recv_sem.at[d - 1],
            device_id=_peer(axis, other, peer),
            device_id_type=MESH,
        )
        copy.start()
        copies.append(copy)
    o_ref[me] = x_ref[...]
    for d, copy in enumerate(copies):
        copy.wait_recv()
        o_ref[lax.rem(me + n - 1 - d, n)] = recv[d]
    for copy in copies:
        copy.wait_send()


def _row_greet(axis, me, other, chips):
    chip, core = me // 2, lax.rem(me, 2)
    barrier = pltpu.get_barrier_semaphore()
    pl.semaphore_signal(barrier, 1, device_id=_peer(axis, other, chip * 2 + 1 - core), device_id_type=MESH)
    for d in range(1, chips):
        peer = lax.rem(chip + d, chips) * 2 + core
        pl.semaphore_signal(barrier, 1, device_id=_peer(axis, other, peer), device_id_type=MESH)
    pl.semaphore_wait(barrier, chips)
    return chip, core


def _row_rs_kernel(axis, other_axis, chips, x_ref, o_ref, recv1, mid, recv2, s1, r1, s2, r2):
    me = lax.axis_index(axis)
    other = lax.axis_index(other_axis)
    chip, core = _row_greet(axis, me, other, chips)
    _rs_body(axis, other, chips, chip, core, x_ref, o_ref, recv1, mid, recv2, s1, r1, s2, r2)


def _rs_body(axis, other, chips, chip, core, x_ref, o_ref, recv1, mid, recv2, s1, r1, s2, r2):
    sib = _peer(axis, other, chip * 2 + 1 - core)
    first = []
    for d in list(range(1, chips)) + [0]:
        target = lax.rem(chip + d, chips)
        copy = pltpu.make_async_remote_copy(
            src_ref=x_ref.at[target, 1 - core],
            dst_ref=recv1.at[d],
            send_sem=s1.at[d],
            recv_sem=r1.at[d],
            device_id=sib,
            device_id_type=MESH,
        )
        copy.start()
        first.append(copy)
    sends = []
    for d in range(1, chips):
        target = lax.rem(chip + d, chips)
        first[d - 1].wait_recv()
        mid[d - 1] = x_ref[target, core] + recv1[d]
        copy = pltpu.make_async_remote_copy(
            src_ref=mid.at[d - 1],
            dst_ref=recv2.at[d - 1],
            send_sem=s2.at[d - 1],
            recv_sem=r2.at[d - 1],
            device_id=_peer(axis, other, target * 2 + core),
            device_id_type=MESH,
        )
        copy.start()
        sends.append(copy)
    first[chips - 1].wait_recv()
    acc = x_ref[chip, core] + recv1[0]
    for d, copy in enumerate(sends):
        copy.wait_recv()
        acc = acc + recv2[d]
    for copy in first + sends:
        copy.wait_send()
    o_ref[...] = acc


def _row_ag_kernel(axis, other_axis, chips, x_ref, o_ref, recv_s, recv_a, recv_f, s1, r1, s2, r2):
    me = lax.axis_index(axis)
    other = lax.axis_index(other_axis)
    chip, core = _row_greet(axis, me, other, chips)
    _ag_body(axis, other, chips, chip, core, x_ref, o_ref, recv_s, recv_a, recv_f, s1, r1, s2, r2)


def _ag_body(axis, other, chips, chip, core, x_ref, o_ref, recv_s, recv_a, recv_f, s1, r1, s2, r2):
    sib = _peer(axis, other, chip * 2 + 1 - core)
    to_sib = pltpu.make_async_remote_copy(
        src_ref=x_ref, dst_ref=recv_s, send_sem=s1.at[0], recv_sem=r1.at[0],
        device_id=sib, device_id_type=MESH,
    )
    to_sib.start()
    first = [to_sib]
    for d in range(1, chips):
        peer = lax.rem(chip + d, chips) * 2 + core
        copy = pltpu.make_async_remote_copy(
            src_ref=x_ref, dst_ref=recv_a.at[d - 1], send_sem=s1.at[d], recv_sem=r1.at[d],
            device_id=_peer(axis, other, peer), device_id_type=MESH,
        )
        copy.start()
        first.append(copy)
    o_ref[chip, core] = x_ref[...]
    forwards = []
    for d in range(1, chips):
        first[d].wait_recv()
        copy = pltpu.make_async_remote_copy(
            src_ref=recv_a.at[d - 1], dst_ref=recv_f.at[d - 1], send_sem=s2.at[d - 1],
            recv_sem=r2.at[d - 1], device_id=sib, device_id_type=MESH,
        )
        copy.start()
        forwards.append(copy)
        o_ref[lax.rem(chip + chips - d, chips), core] = recv_a[d - 1]
    to_sib.wait_recv()
    o_ref[chip, 1 - core] = recv_s[...]
    for d, copy in enumerate(forwards):
        copy.wait_recv()
        o_ref[lax.rem(chip + chips - 1 - d, chips), 1 - core] = recv_f[d]
    for copy in first + forwards:
        copy.wait_send()


def _mixed_rs_body(axis, other, chips, chip, core, x_ref, o_ref, ra1, ma, ra2, rb1, mb, rb2,
                   sa1, qa1, sa2, qa2, sb1, qb1, sb2, qb2, between=None):
    sib = _peer(axis, other, chip * 2 + 1 - core)
    width = x_ref.shape[-1]
    a1 = []
    for d in list(range(1, chips)) + [0]:
        target = lax.rem(chip + d, chips)
        copy = pltpu.make_async_remote_copy(
            src_ref=x_ref.at[0, target * 2 + 1 - core], dst_ref=ra1.at[d], send_sem=sa1.at[d],
            recv_sem=qa1.at[d], device_id=sib, device_id_type=MESH,
        )
        copy.start()
        a1.append(copy)
    if between is not None:
        between()
    b1 = []
    for d in range(1, chips):
        target = lax.rem(chip + d, chips)
        for half, bit in enumerate((core, 1 - core)):
            copy = pltpu.make_async_remote_copy(
                src_ref=x_ref.at[1, target * 2 + bit], dst_ref=rb1.at[d - 1, half],
                send_sem=sb1.at[d - 1, half], recv_sem=qb1.at[d - 1, half],
                device_id=_peer(axis, other, target * 2 + core), device_id_type=MESH,
            )
            copy.start()
            b1.append(copy)
    a2 = []
    for d in range(1, chips):
        target = lax.rem(chip + d, chips)
        a1[d - 1].wait_recv()
        ma[d - 1] = x_ref[0, target * 2 + core] + ra1[d]
        copy = pltpu.make_async_remote_copy(
            src_ref=ma.at[d - 1], dst_ref=ra2.at[d - 1], send_sem=sa2.at[d - 1],
            recv_sem=qa2.at[d - 1], device_id=_peer(axis, other, target * 2 + core),
            device_id_type=MESH,
        )
        copy.start()
        a2.append(copy)
    for copy in b1:
        copy.wait_recv()
    part = x_ref[1, chip * 2 + 1 - core]
    for d in range(chips - 1):
        part = part + rb1[d, 1]
    mb[...] = part
    b2 = pltpu.make_async_remote_copy(
        src_ref=mb, dst_ref=rb2, send_sem=sb2.at[0], recv_sem=qb2.at[0],
        device_id=sib, device_id_type=MESH,
    )
    b2.start()
    acc_b = x_ref[1, chip * 2 + core]
    for d in range(chips - 1):
        acc_b = acc_b + rb1[d, 0]
    a1[chips - 1].wait_recv()
    acc_a = x_ref[0, chip * 2 + core] + ra1[0]
    for d, copy in enumerate(a2):
        copy.wait_recv()
        acc_a = acc_a + ra2[d]
    b2.wait_recv()
    o_ref[:, :width] = acc_a
    o_ref[:, width:] = acc_b + rb2[...]
    for copy in a1 + b1 + a2 + [b2]:
        copy.wait_send()


def _ar_kernel(axis, other_axis, chips, row_chips, rb, cb, bs, mask_ref, p_ref, g_hbm, o_ref, a_ref,
               g_vmem, g_sem, l_all, low, t_ref, x_ref, p_all, *scratch):
    row_scratch = scratch[21:28]
    load = pltpu.make_async_copy(g_hbm, g_vmem, g_sem.at[0])
    load.start()
    me = lax.axis_index(axis)
    other = lax.axis_index(other_axis)
    chip, core = me // 2, lax.rem(me, 2)
    row_chip, row_core = other // 2, lax.rem(other, 2)
    barrier = pltpu.get_barrier_semaphore()
    for ax, mine, group, bit, count in ((axis, other, chip, core, chips), (other_axis, me, row_chip, row_core, row_chips)):
        pl.semaphore_signal(barrier, 1, device_id=_peer(ax, mine, group * 2 + 1 - bit), device_id_type=MESH)
        for d in range(1, count):
            peer = lax.rem(group + d, count) * 2 + bit
            pl.semaphore_signal(barrier, 1, device_id=_peer(ax, mine, peer), device_id_type=MESH)
    pl.semaphore_wait(barrier, chips + row_chips)
    _ag_body(other_axis, me, row_chips, row_chip, row_core, p_ref, p_all, *scratch[28:])
    k = p_all.shape[0] * p_all.shape[1] * p_all.shape[2]
    probes_t = p_all[...].reshape(k, p_all.shape[3])
    load.wait()
    sub = x_ref.shape[-1] // bs

    def sketch(step):
        for h in range(step * sub, (step + 1) * sub):
            keep = _mask_lanes(mask_ref, cb, bs, probes_t.shape[1], row=h)
            p = jnp.where(keep, probes_t, jnp.zeros_like(probes_t))
            x_ref[step, :, :, (h % sub) * bs:(h % sub + 1) * bs] = lax.dot_general(
                p, g_vmem[h * bs:(h + 1) * bs, :], (((1,), (1,)), ((), ())), preferred_element_type=jnp.float32
            ).reshape(x_ref.shape[1], x_ref.shape[2], bs)

    sketch(0)
    _mixed_rs_body(axis, other, chips, chip, core, x_ref, o_ref, *scratch[:14], between=lambda: sketch(1))
    low[...] = o_ref[...].astype(low.dtype)
    _ag_body(axis, other, chips, chip, core, low, l_all, *scratch[14:21])
    k = l_all.shape[0] * l_all.shape[1] * l_all.shape[2]
    lowered = l_all[...].reshape(k, l_all.shape[3])
    for j in range(cb):
        keep = _mask_lanes(mask_ref, rb, bs, lowered.shape[1], col=j)
        masked = jnp.where(keep, lowered, jnp.zeros_like(lowered))
        t_ref[:, :, :, j * bs:(j + 1) * bs] = jnp.dot(
            masked, g_vmem[:, j * bs:(j + 1) * bs], preferred_element_type=jnp.float32
        ).reshape(t_ref.shape[0], 2, t_ref.shape[2], bs)
    _rs_body(other_axis, me, row_chips, row_chip, row_core, t_ref, a_ref, *row_scratch)


def _all_reduce_adjoint(probes_t, mask, green, axis, other_axis, collective_id):
    n = lax.axis_size(axis)
    rows = probes_t.shape[0] * lax.axis_size(other_axis) // n
    half = green.shape[0] // 2
    x = jax.ShapeDtypeStruct((2, n, rows, half), jnp.float32)
    chips = n // 2
    width = 2 * half
    low = jnp.bfloat16
    rb, cb = mask.shape
    bs = green.shape[0] // rb
    row_chips = lax.axis_size(other_axis) // 2
    k_rows = n * rows // (2 * row_chips)
    cols = green.shape[1]
    return pl.pallas_call(
        functools.partial(_ar_kernel, axis, other_axis, chips, row_chips, rb, cb, bs),
        out_shape=(
            jax.ShapeDtypeStruct((rows, width), jnp.float32),
            jax.ShapeDtypeStruct((k_rows, cols), jnp.float32),
        ),
        in_specs=[
            pl.BlockSpec(memory_space=pltpu.SMEM),
            pl.BlockSpec(memory_space=pltpu.VMEM),
            pl.BlockSpec(memory_space=pl.ANY),
        ],
        out_specs=(pl.BlockSpec(memory_space=pltpu.VMEM), pl.BlockSpec(memory_space=pltpu.VMEM)),
        scratch_shapes=[
            pltpu.VMEM(green.shape, green.dtype),
            pltpu.SemaphoreType.DMA((1,)),
            pltpu.VMEM((chips, 2, rows, width), low),
            pltpu.VMEM((rows, width), low),
            pltpu.VMEM((row_chips, 2, k_rows, cols), jnp.float32),
            pltpu.VMEM((2, n, rows, half), jnp.float32),
            pltpu.VMEM((row_chips, 2) + probes_t.shape, probes_t.dtype),
            pltpu.VMEM((chips, rows, half), x.dtype),
            pltpu.VMEM((chips - 1, rows, half), x.dtype),
            pltpu.VMEM((chips - 1, rows, half), x.dtype),
            pltpu.VMEM((chips - 1, 2, rows, half), x.dtype),
            pltpu.VMEM((rows, half), x.dtype),
            pltpu.VMEM((rows, half), x.dtype),
            pltpu.SemaphoreType.DMA((chips,)),
            pltpu.SemaphoreType.DMA((chips,)),
            pltpu.SemaphoreType.DMA((chips - 1,)),
            pltpu.SemaphoreType.DMA((chips - 1,)),
            pltpu.SemaphoreType.DMA((chips - 1, 2)),
            pltpu.SemaphoreType.DMA((chips - 1, 2)),
            pltpu.SemaphoreType.DMA((1,)),
            pltpu.SemaphoreType.DMA((1,)),
            pltpu.VMEM((rows, width), low),
            pltpu.VMEM((chips - 1, rows, width), low),
            pltpu.VMEM((chips - 1, rows, width), low),
            pltpu.SemaphoreType.DMA((chips,)),
            pltpu.SemaphoreType.DMA((chips,)),
            pltpu.SemaphoreType.DMA((chips - 1,)),
            pltpu.SemaphoreType.DMA((chips - 1,)),
            pltpu.VMEM((row_chips, k_rows, cols), jnp.float32),
            pltpu.VMEM((row_chips - 1, k_rows, cols), jnp.float32),
            pltpu.VMEM((row_chips - 1, k_rows, cols), jnp.float32),
            pltpu.SemaphoreType.DMA((row_chips,)),
            pltpu.SemaphoreType.DMA((row_chips,)),
            pltpu.SemaphoreType.DMA((row_chips - 1,)),
            pltpu.SemaphoreType.DMA((row_chips - 1,)),
            pltpu.VMEM(probes_t.shape, probes_t.dtype),
            pltpu.VMEM((row_chips - 1,) + probes_t.shape, probes_t.dtype),
            pltpu.VMEM((row_chips - 1,) + probes_t.shape, probes_t.dtype),
            pltpu.SemaphoreType.DMA((row_chips,)),
            pltpu.SemaphoreType.DMA((row_chips,)),
            pltpu.SemaphoreType.DMA((row_chips - 1,)),
            pltpu.SemaphoreType.DMA((row_chips - 1,)),
        ],
        compiler_params=pltpu.CompilerParams(collective_id=collective_id, has_side_effects=True),
    )(mask, probes_t, green)


def _row_reduce_scatter(x, axis, other_axis, collective_id):
    chips, _, rows, width = x.shape
    return pl.pallas_call(
        functools.partial(_row_rs_kernel, axis, other_axis, chips),
        out_shape=jax.ShapeDtypeStruct((rows, width), x.dtype),
        in_specs=[pl.BlockSpec(memory_space=pltpu.VMEM)],
        out_specs=pl.BlockSpec(memory_space=pltpu.VMEM),
        scratch_shapes=[
            pltpu.VMEM((chips, rows, width), x.dtype),
            pltpu.VMEM((chips - 1, rows, width), x.dtype),
            pltpu.VMEM((chips - 1, rows, width), x.dtype),
            pltpu.SemaphoreType.DMA((chips,)),
            pltpu.SemaphoreType.DMA((chips,)),
            pltpu.SemaphoreType.DMA((chips - 1,)),
            pltpu.SemaphoreType.DMA((chips - 1,)),
        ],
        compiler_params=pltpu.CompilerParams(collective_id=collective_id, has_side_effects=True),
    )(x)


def _row_all_gather(x, axis, other_axis, chips, collective_id):
    rows, width = x.shape
    return pl.pallas_call(
        functools.partial(_row_ag_kernel, axis, other_axis, chips),
        out_shape=jax.ShapeDtypeStruct((chips, 2, rows, width), x.dtype),
        in_specs=[pl.BlockSpec(memory_space=pltpu.VMEM)],
        out_specs=pl.BlockSpec(memory_space=pltpu.VMEM),
        scratch_shapes=[
            pltpu.VMEM((rows, width), x.dtype),
            pltpu.VMEM((chips - 1, rows, width), x.dtype),
            pltpu.VMEM((chips - 1, rows, width), x.dtype),
            pltpu.SemaphoreType.DMA((chips,)),
            pltpu.SemaphoreType.DMA((chips,)),
            pltpu.SemaphoreType.DMA((chips - 1,)),
            pltpu.SemaphoreType.DMA((chips - 1,)),
        ],
        compiler_params=pltpu.CompilerParams(collective_id=collective_id, has_side_effects=True),
    )(x)


def _reduce_scatter(x, axis, other_axis, collective_id):
    n, rows, width = x.shape
    return pl.pallas_call(
        functools.partial(_rs_kernel, axis, other_axis, n),
        out_shape=jax.ShapeDtypeStruct((rows, width), x.dtype),
        in_specs=[pl.BlockSpec(memory_space=pltpu.VMEM)],
        out_specs=pl.BlockSpec(memory_space=pltpu.VMEM),
        scratch_shapes=[
            pltpu.VMEM((n - 1, rows, width), x.dtype),
            pltpu.SemaphoreType.DMA((n - 1,)),
            pltpu.SemaphoreType.DMA((n - 1,)),
        ],
        compiler_params=pltpu.CompilerParams(collective_id=collective_id, has_side_effects=True),
    )(x)


def _all_gather(x, axis, other_axis, n, collective_id):
    rows, width = x.shape
    return pl.pallas_call(
        functools.partial(_ag_kernel, axis, other_axis, n),
        out_shape=jax.ShapeDtypeStruct((n, rows, width), x.dtype),
        in_specs=[pl.BlockSpec(memory_space=pltpu.VMEM)],
        out_specs=pl.BlockSpec(memory_space=pltpu.VMEM),
        scratch_shapes=[
            pltpu.VMEM((n - 1, rows, width), x.dtype),
            pltpu.SemaphoreType.DMA((n - 1,)),
            pltpu.SemaphoreType.DMA((n - 1,)),
        ],
        compiler_params=pltpu.CompilerParams(collective_id=collective_id, has_side_effects=True),
    )(x)


def _mask_lanes(mask_ref, nb, bs, width, row=None, col=None):
    blk = lax.broadcasted_iota(jnp.int32, (1, width), 1) // bs
    keep = jnp.zeros((1, width), jnp.int32)
    for b in range(nb):
        value = mask_ref[row, b] if col is None else mask_ref[b, col]
        keep = jnp.where(blk == b, value, keep)
    return keep != 0


def _sub_blocks(nb):
    return 4 if nb % 4 == 0 else (2 if nb % 2 == 0 else 1)


def _half_blocks(nb):
    return nb // 2


def _sketch_kernel(nb, bs, sub, mask_ref, g_ref, p_ref, o_ref):
    i = pl.program_id(0)
    for h in range(sub):
        keep = _mask_lanes(mask_ref, nb, bs, p_ref.shape[1], row=i * sub + h)
        p = jnp.where(keep, p_ref[...], jnp.zeros_like(p_ref))
        o_ref[:, h * bs:(h + 1) * bs] = lax.dot_general(
            p, g_ref[h * bs:(h + 1) * bs, :], (((1,), (1,)), ((), ())), preferred_element_type=jnp.float32
        )


def _adjoint_kernel(nb, bs, sub, mask_ref, l_ref, g_ref, o_ref):
    j = pl.program_id(0)
    for h in range(sub):
        keep = _mask_lanes(mask_ref, nb, bs, l_ref.shape[1], col=j * sub + h)
        lowered = jnp.where(keep, l_ref[...], jnp.zeros_like(l_ref))
        o_ref[:, h * bs:(h + 1) * bs] = jnp.dot(
            lowered, g_ref[:, h * bs:(h + 1) * bs], preferred_element_type=jnp.float32
        )


def _sketch_partial(mask, green, probes_t):
    rb, cb = mask.shape
    bs = green.shape[0] // rb
    sub = _half_blocks(rb)
    k = probes_t.shape[0]
    return pl.pallas_call(
        functools.partial(_sketch_kernel, cb, bs, sub),
        out_shape=jax.ShapeDtypeStruct((rb // sub, k, bs * sub), jnp.float32),
        grid_spec=pltpu.PrefetchScalarGridSpec(
            num_scalar_prefetch=1,
            grid=(rb // sub,),
            in_specs=[
                pl.BlockSpec((bs * sub, green.shape[1]), lambda i, m: (i, 0)),
                pl.BlockSpec((k, green.shape[1]), lambda i, m: (0, 0)),
            ],
            out_specs=pl.BlockSpec((None, k, bs * sub), lambda i, m: (i, 0, 0)),
        ),
    )(mask, green, probes_t)


def _adjoint_partial(mask, lowered_t, green):
    rb, cb = mask.shape
    bs = green.shape[0] // rb
    sub = _sub_blocks(cb)
    k = lowered_t.shape[0]
    return pl.pallas_call(
        functools.partial(_adjoint_kernel, rb, bs, sub),
        out_shape=jax.ShapeDtypeStruct((k, green.shape[1]), jnp.float32),
        grid_spec=pltpu.PrefetchScalarGridSpec(
            num_scalar_prefetch=1,
            grid=(cb // sub,),
            in_specs=[
                pl.BlockSpec((k, green.shape[0]), lambda j, m: (0, 0)),
                pl.BlockSpec((green.shape[0], bs * sub), lambda j, m: (0, j)),
            ],
            out_specs=pl.BlockSpec((k, bs * sub), lambda j, m: (0, j)),
        ),
    )(mask, lowered_t, green)


def _ag_sketch_kernel(chips, rb, nb, bs, sub, mask_ref, x_ref, g_hbm, o_ref, g_vmem, g_sem, p_all, *scratch):
    load = pltpu.make_async_copy(g_hbm, g_vmem, g_sem.at[0])
    load.start()
    me = lax.axis_index("row")
    other = lax.axis_index("col")
    chip, core = _row_greet("row", me, other, chips)
    _ag_body("row", other, chips, chip, core, x_ref, p_all, *scratch)
    k = p_all.shape[0] * p_all.shape[1] * p_all.shape[2]
    probes_t = p_all[...].reshape(k, p_all.shape[3])
    load.wait()
    for h in range(rb):
        keep = _mask_lanes(mask_ref, nb, bs, probes_t.shape[1], row=h)
        p = jnp.where(keep, probes_t, jnp.zeros_like(probes_t))
        o_ref[h // sub, :, (h % sub) * bs:(h % sub + 1) * bs] = lax.dot_general(
            p, g_vmem[h * bs:(h + 1) * bs, :], (((1,), (1,)), ((), ())), preferred_element_type=jnp.float32
        )


def _ag_sketch(x, mask, green, chips, collective_id):
    rows, width = x.shape
    rb, cb = mask.shape
    bs = green.shape[0] // rb
    sub = _half_blocks(rb)
    k = 2 * chips * rows
    return pl.pallas_call(
        functools.partial(_ag_sketch_kernel, chips, rb, cb, bs, sub),
        out_shape=jax.ShapeDtypeStruct((rb // sub, k, bs * sub), jnp.float32),
        in_specs=[
            pl.BlockSpec(memory_space=pltpu.SMEM),
            pl.BlockSpec(memory_space=pltpu.VMEM),
            pl.BlockSpec(memory_space=pl.ANY),
        ],
        out_specs=pl.BlockSpec(memory_space=pltpu.VMEM),
        scratch_shapes=[
            pltpu.VMEM(green.shape, green.dtype),
            pltpu.SemaphoreType.DMA((1,)),
            pltpu.VMEM((chips, 2, rows, width), x.dtype),
            pltpu.VMEM((rows, width), x.dtype),
            pltpu.VMEM((chips - 1, rows, width), x.dtype),
            pltpu.VMEM((chips - 1, rows, width), x.dtype),
            pltpu.SemaphoreType.DMA((chips,)),
            pltpu.SemaphoreType.DMA((chips,)),
            pltpu.SemaphoreType.DMA((chips - 1,)),
            pltpu.SemaphoreType.DMA((chips - 1,)),
        ],
        compiler_params=pltpu.CompilerParams(collective_id=collective_id, has_side_effects=True),
    )(mask, x, green)


def local(green, mask, probes):
    n_row = lax.axis_size("row")
    n_col = lax.axis_size("col")
    sketch_t, adjoint_t = _all_reduce_adjoint(probes.T, mask, green, "col", "row", 0)
    return (sketch_t.T, adjoint_t.T)


def solution(mesh):
    in_specs = (P("row", "col"), P("row", "col"), P("col", "row"))
    out_specs = (P("row", "col"), P("col", "row"))
    return jax.shard_map(local, mesh=mesh, in_specs=in_specs, out_specs=out_specs, check_vma=False)
```

```python
import functools

import jax
import jax.numpy as jnp
from jax import lax
from jax.experimental import pallas as pl
from jax.experimental.pallas import tpu as pltpu
from jax.sharding import PartitionSpec as P

MESH = pl.DeviceIdType.MESH


def _peer(axis, other, p):
    return (other, p) if axis == "col" else (p, other)


def _greet(axis, other, me, n):
    barrier = pltpu.get_barrier_semaphore()
    for d in range(1, n):
        peer = _peer(axis, other, lax.rem(me + d, n))
        pl.semaphore_signal(barrier, 1, device_id=peer, device_id_type=MESH)
    pl.semaphore_wait(barrier, n - 1)


def _rs_kernel(axis, other_axis, n, x_ref, o_ref, recv, send_sem, recv_sem):
    me = lax.axis_index(axis)
    other = lax.axis_index(other_axis)
    _greet(axis, other, me, n)
    copies = []
    for d in range(1, n):
        peer = lax.rem(me + d, n)
        copy = pltpu.make_async_remote_copy(
            src_ref=x_ref.at[peer],
            dst_ref=recv.at[d - 1],
            send_sem=send_sem.at[d - 1],
            recv_sem=recv_sem.at[d - 1],
            device_id=_peer(axis, other, peer),
            device_id_type=MESH,
        )
        copy.start()
        copies.append(copy)
    acc = x_ref[me]
    for d, copy in enumerate(copies):
        copy.wait_recv()
        acc = acc + recv[d]
    for copy in copies:
        copy.wait_send()
    o_ref[...] = acc


def _ag_kernel(axis, other_axis, n, x_ref, o_ref, recv, send_sem, recv_sem):
    me = lax.axis_index(axis)
    other = lax.axis_index(other_axis)
    _greet(axis, other, me, n)
    copies = []
    for d in range(1, n):
        peer = lax.rem(me + d, n)
        copy = pltpu.make_async_remote_copy(
            src_ref=x_ref,
            dst_ref=recv.at[d - 1],
            send_sem=send_sem.at[d - 1],
            recv_sem=recv_sem.at[d - 1],
            device_id=_peer(axis, other, peer),
            device_id_type=MESH,
        )
        copy.start()
        copies.append(copy)
    o_ref[me] = x_ref[...]
    for d, copy in enumerate(copies):
        copy.wait_recv()
        o_ref[lax.rem(me + n - 1 - d, n)] = recv[d]
    for copy in copies:
        copy.wait_send()


def _row_greet(axis, me, other, chips):
    chip, core = me // 2, lax.rem(me, 2)
    barrier = pltpu.get_barrier_semaphore()
    pl.semaphore_signal(barrier, 1, device_id=_peer(axis, other, chip * 2 + 1 - core), device_id_type=MESH)
    for d in range(1, chips):
        peer = lax.rem(chip + d, chips) * 2 + core
        pl.semaphore_signal(barrier, 1, device_id=_peer(axis, other, peer), device_id_type=MESH)
    pl.semaphore_wait(barrier, chips)
    return chip, core


def _row_rs_kernel(axis, other_axis, chips, x_ref, o_ref, recv1, mid, recv2, s1, r1, s2, r2):
    me = lax.axis_index(axis)
    other = lax.axis_index(other_axis)
    chip, core = _row_greet(axis, me, other, chips)
    _rs_body(axis, other, chips, chip, core, x_ref, o_ref, recv1, mid, recv2, s1, r1, s2, r2)


def _rs_body(axis, other, chips, chip, core, x_ref, o_ref, recv1, mid, recv2, s1, r1, s2, r2, between=None):
    sib = _peer(axis, other, chip * 2 + 1 - core)
    first = []
    for d in list(range(1, chips)) + [0]:
        target = lax.rem(chip + d, chips)
        copy = pltpu.make_async_remote_copy(
            src_ref=x_ref.at[target, 1 - core],
            dst_ref=recv1.at[d],
            send_sem=s1.at[d],
            recv_sem=r1.at[d],
            device_id=sib,
            device_id_type=MESH,
        )
        copy.start()
        first.append(copy)
    if between is not None:
        between()
    sends = []
    for d in range(1, chips):
        target = lax.rem(chip + d, chips)
        first[d - 1].wait_recv()
        mid[d - 1] = x_ref[target, core] + recv1[d]
        copy = pltpu.make_async_remote_copy(
            src_ref=mid.at[d - 1],
            dst_ref=recv2.at[d - 1],
            send_sem=s2.at[d - 1],
            recv_sem=r2.at[d - 1],
            device_id=_peer(axis, other, target * 2 + core),
            device_id_type=MESH,
        )
        copy.start()
        sends.append(copy)
    first[chips - 1].wait_recv()
    acc = x_ref[chip, core] + recv1[0]
    for d, copy in enumerate(sends):
        copy.wait_recv()
        acc = acc + recv2[d]
    for copy in first + sends:
        copy.wait_send()
    o_ref[...] = acc


def _row_ag_kernel(axis, other_axis, chips, x_ref, o_ref, recv_s, recv_a, recv_f, s1, r1, s2, r2):
    me = lax.axis_index(axis)
    other = lax.axis_index(other_axis)
    chip, core = _row_greet(axis, me, other, chips)
    _ag_body(axis, other, chips, chip, core, x_ref, o_ref, recv_s, recv_a, recv_f, s1, r1, s2, r2)


def _ag_body(axis, other, chips, chip, core, x_ref, o_ref, recv_s, recv_a, recv_f, s1, r1, s2, r2):
    sib = _peer(axis, other, chip * 2 + 1 - core)
    to_sib = pltpu.make_async_remote_copy(
        src_ref=x_ref, dst_ref=recv_s, send_sem=s1.at[0], recv_sem=r1.at[0],
        device_id=sib, device_id_type=MESH,
    )
    to_sib.start()
    first = [to_sib]
    for d in range(1, chips):
        peer = lax.rem(chip + d, chips) * 2 + core
        copy = pltpu.make_async_remote_copy(
            src_ref=x_ref, dst_ref=recv_a.at[d - 1], send_sem=s1.at[d], recv_sem=r1.at[d],
            device_id=_peer(axis, other, peer), device_id_type=MESH,
        )
        copy.start()
        first.append(copy)
    o_ref[chip, core] = x_ref[...]
    forwards = []
    for d in range(1, chips):
        first[d].wait_recv()
        copy = pltpu.make_async_remote_copy(
            src_ref=recv_a.at[d - 1], dst_ref=recv_f.at[d - 1], send_sem=s2.at[d - 1],
            recv_sem=r2.at[d - 1], device_id=sib, device_id_type=MESH,
        )
        copy.start()
        forwards.append(copy)
        o_ref[lax.rem(chip + chips - d, chips), core] = recv_a[d - 1]
    to_sib.wait_recv()
    o_ref[chip, 1 - core] = recv_s[...]
    for d, copy in enumerate(forwards):
        copy.wait_recv()
        o_ref[lax.rem(chip + chips - 1 - d, chips), 1 - core] = recv_f[d]
    for copy in first + forwards:
        copy.wait_send()


def _mixed_rs_body(axis, other, chips, chip, core, x_ref, o_ref, ra1, ma, ra2, rb1, mb, rb2,
                   sa1, qa1, sa2, qa2, sb1, qb1, sb2, qb2, between=None):
    sib = _peer(axis, other, chip * 2 + 1 - core)
    width = x_ref.shape[-1]
    a1 = []
    for d in list(range(1, chips)) + [0]:
        target = lax.rem(chip + d, chips)
        copy = pltpu.make_async_remote_copy(
            src_ref=x_ref.at[0, target * 2 + 1 - core], dst_ref=ra1.at[d], send_sem=sa1.at[d],
            recv_sem=qa1.at[d], device_id=sib, device_id_type=MESH,
        )
        copy.start()
        a1.append(copy)
    if between is not None:
        between()
    b1 = []
    for d in range(1, chips):
        target = lax.rem(chip + d, chips)
        for half, bit in enumerate((core, 1 - core)):
            copy = pltpu.make_async_remote_copy(
                src_ref=x_ref.at[1, target * 2 + bit], dst_ref=rb1.at[d - 1, half],
                send_sem=sb1.at[d - 1, half], recv_sem=qb1.at[d - 1, half],
                device_id=_peer(axis, other, target * 2 + core), device_id_type=MESH,
            )
            copy.start()
            b1.append(copy)
    a2 = []
    for d in range(1, chips):
        target = lax.rem(chip + d, chips)
        a1[d - 1].wait_recv()
        ma[d - 1] = x_ref[0, target * 2 + core] + ra1[d]
        copy = pltpu.make_async_remote_copy(
            src_ref=ma.at[d - 1], dst_ref=ra2.at[d - 1], send_sem=sa2.at[d - 1],
            recv_sem=qa2.at[d - 1], device_id=_peer(axis, other, target * 2 + core),
            device_id_type=MESH,
        )
        copy.start()
        a2.append(copy)
    for copy in b1:
        copy.wait_recv()
    part = x_ref[1, chip * 2 + 1 - core]
    for d in range(chips - 1):
        part = part + rb1[d, 1]
    mb[...] = part
    b2 = pltpu.make_async_remote_copy(
        src_ref=mb, dst_ref=rb2, send_sem=sb2.at[0], recv_sem=qb2.at[0],
        device_id=sib, device_id_type=MESH,
    )
    b2.start()
    acc_b = x_ref[1, chip * 2 + core]
    for d in range(chips - 1):
        acc_b = acc_b + rb1[d, 0]
    a1[chips - 1].wait_recv()
    acc_a = x_ref[0, chip * 2 + core] + ra1[0]
    for d, copy in enumerate(a2):
        copy.wait_recv()
        acc_a = acc_a + ra2[d]
    b2.wait_recv()
    o_ref[:, :width] = acc_a
    o_ref[:, width:] = acc_b + rb2[...]
    for copy in a1 + b1 + a2 + [b2]:
        copy.wait_send()


def _ar_kernel(axis, other_axis, chips, row_chips, rb, cb, bs, mask_ref, p_ref, g_hbm, o_ref, a_ref,
               g_vmem, g_sem, l_all, low, t_ref, x_ref, p_all, *scratch):
    row_scratch = scratch[21:28]
    load = pltpu.make_async_copy(g_hbm, g_vmem, g_sem.at[0])
    load.start()
    me = lax.axis_index(axis)
    other = lax.axis_index(other_axis)
    chip, core = me // 2, lax.rem(me, 2)
    row_chip, row_core = other // 2, lax.rem(other, 2)
    barrier = pltpu.get_barrier_semaphore()
    for ax, mine, group, bit, count in ((axis, other, chip, core, chips), (other_axis, me, row_chip, row_core, row_chips)):
        pl.semaphore_signal(barrier, 1, device_id=_peer(ax, mine, group * 2 + 1 - bit), device_id_type=MESH)
        for d in range(1, count):
            peer = lax.rem(group + d, count) * 2 + bit
            pl.semaphore_signal(barrier, 1, device_id=_peer(ax, mine, peer), device_id_type=MESH)
    pl.semaphore_wait(barrier, chips + row_chips)
    _ag_body(other_axis, me, row_chips, row_chip, row_core, p_ref, p_all, *scratch[28:])
    k = p_all.shape[0] * p_all.shape[1] * p_all.shape[2]
    probes_t = p_all[...].reshape(k, p_all.shape[3])
    load.wait()
    sub = x_ref.shape[-1] // bs

    def sketch(step):
        for h in range(step * sub, (step + 1) * sub):
            keep = _mask_lanes(mask_ref, cb, bs, probes_t.shape[1], row=h)
            p = jnp.where(keep, probes_t, jnp.zeros_like(probes_t))
            x_ref[step, :, :, (h % sub) * bs:(h % sub + 1) * bs] = lax.dot_general(
                p, g_vmem[h * bs:(h + 1) * bs, :], (((1,), (1,)), ((), ())), preferred_element_type=jnp.float32
            ).reshape(x_ref.shape[1], x_ref.shape[2], bs)

    sketch(0)
    _mixed_rs_body(axis, other, chips, chip, core, x_ref, o_ref, *scratch[:14], between=lambda: sketch(1))
    low[...] = o_ref[...].astype(low.dtype)
    _ag_body(axis, other, chips, chip, core, low, l_all, *scratch[14:21])
    def adjoint(bit):
        k = l_all.shape[0] * l_all.shape[1] * l_all.shape[2]
        full = l_all[...].reshape(t_ref.shape[0], 2, k // (2 * t_ref.shape[0]), l_all.shape[3])
        lowered = jnp.where(bit == 0, full[:, 0], full[:, 1]).reshape(k // 2, l_all.shape[3])
        for j in range(cb):
            keep = _mask_lanes(mask_ref, rb, bs, lowered.shape[1], col=j)
            masked = jnp.where(keep, lowered, jnp.zeros_like(lowered))
            t_ref[:, bit, :, j * bs:(j + 1) * bs] = jnp.dot(
                masked, g_vmem[:, j * bs:(j + 1) * bs], preferred_element_type=jnp.float32
            ).reshape(t_ref.shape[0], t_ref.shape[2], bs)

    adjoint(1 - row_core)
    _rs_body(other_axis, me, row_chips, row_chip, row_core, t_ref, a_ref, *row_scratch,
             between=lambda: adjoint(row_core))


def _all_reduce_adjoint(probes_t, mask, green, axis, other_axis, collective_id):
    n = lax.axis_size(axis)
    rows = probes_t.shape[0] * lax.axis_size(other_axis) // n
    half = green.shape[0] // 2
    x = jax.ShapeDtypeStruct((2, n, rows, half), jnp.float32)
    chips = n // 2
    width = 2 * half
    low = jnp.bfloat16
    rb, cb = mask.shape
    bs = green.shape[0] // rb
    row_chips = lax.axis_size(other_axis) // 2
    k_rows = n * rows // (2 * row_chips)
    cols = green.shape[1]
    return pl.pallas_call(
        functools.partial(_ar_kernel, axis, other_axis, chips, row_chips, rb, cb, bs),
        out_shape=(
            jax.ShapeDtypeStruct((rows, width), jnp.float32),
            jax.ShapeDtypeStruct((k_rows, cols), jnp.float32),
        ),
        in_specs=[
            pl.BlockSpec(memory_space=pltpu.SMEM),
            pl.BlockSpec(memory_space=pltpu.VMEM),
            pl.BlockSpec(memory_space=pl.ANY),
        ],
        out_specs=(pl.BlockSpec(memory_space=pltpu.VMEM), pl.BlockSpec(memory_space=pltpu.VMEM)),
        scratch_shapes=[
            pltpu.VMEM(green.shape, green.dtype),
            pltpu.SemaphoreType.DMA((1,)),
            pltpu.VMEM((chips, 2, rows, width), low),
            pltpu.VMEM((rows, width), low),
            pltpu.VMEM((row_chips, 2, k_rows, cols), jnp.float32),
            pltpu.VMEM((2, n, rows, half), jnp.float32),
            pltpu.VMEM((row_chips, 2) + probes_t.shape, probes_t.dtype),
            pltpu.VMEM((chips, rows, half), x.dtype),
            pltpu.VMEM((chips - 1, rows, half), x.dtype),
            pltpu.VMEM((chips - 1, rows, half), x.dtype),
            pltpu.VMEM((chips - 1, 2, rows, half), x.dtype),
            pltpu.VMEM((rows, half), x.dtype),
            pltpu.VMEM((rows, half), x.dtype),
            pltpu.SemaphoreType.DMA((chips,)),
            pltpu.SemaphoreType.DMA((chips,)),
            pltpu.SemaphoreType.DMA((chips - 1,)),
            pltpu.SemaphoreType.DMA((chips - 1,)),
            pltpu.SemaphoreType.DMA((chips - 1, 2)),
            pltpu.SemaphoreType.DMA((chips - 1, 2)),
            pltpu.SemaphoreType.DMA((1,)),
            pltpu.SemaphoreType.DMA((1,)),
            pltpu.VMEM((rows, width), low),
            pltpu.VMEM((chips - 1, rows, width), low),
            pltpu.VMEM((chips - 1, rows, width), low),
            pltpu.SemaphoreType.DMA((chips,)),
            pltpu.SemaphoreType.DMA((chips,)),
            pltpu.SemaphoreType.DMA((chips - 1,)),
            pltpu.SemaphoreType.DMA((chips - 1,)),
            pltpu.VMEM((row_chips, k_rows, cols), jnp.float32),
            pltpu.VMEM((row_chips - 1, k_rows, cols), jnp.float32),
            pltpu.VMEM((row_chips - 1, k_rows, cols), jnp.float32),
            pltpu.SemaphoreType.DMA((row_chips,)),
            pltpu.SemaphoreType.DMA((row_chips,)),
            pltpu.SemaphoreType.DMA((row_chips - 1,)),
            pltpu.SemaphoreType.DMA((row_chips - 1,)),
            pltpu.VMEM(probes_t.shape, probes_t.dtype),
            pltpu.VMEM((row_chips - 1,) + probes_t.shape, probes_t.dtype),
            pltpu.VMEM((row_chips - 1,) + probes_t.shape, probes_t.dtype),
            pltpu.SemaphoreType.DMA((row_chips,)),
            pltpu.SemaphoreType.DMA((row_chips,)),
            pltpu.SemaphoreType.DMA((row_chips - 1,)),
            pltpu.SemaphoreType.DMA((row_chips - 1,)),
        ],
        compiler_params=pltpu.CompilerParams(collective_id=collective_id, has_side_effects=True),
    )(mask, probes_t, green)


def _row_reduce_scatter(x, axis, other_axis, collective_id):
    chips, _, rows, width = x.shape
    return pl.pallas_call(
        functools.partial(_row_rs_kernel, axis, other_axis, chips),
        out_shape=jax.ShapeDtypeStruct((rows, width), x.dtype),
        in_specs=[pl.BlockSpec(memory_space=pltpu.VMEM)],
        out_specs=pl.BlockSpec(memory_space=pltpu.VMEM),
        scratch_shapes=[
            pltpu.VMEM((chips, rows, width), x.dtype),
            pltpu.VMEM((chips - 1, rows, width), x.dtype),
            pltpu.VMEM((chips - 1, rows, width), x.dtype),
            pltpu.SemaphoreType.DMA((chips,)),
            pltpu.SemaphoreType.DMA((chips,)),
            pltpu.SemaphoreType.DMA((chips - 1,)),
            pltpu.SemaphoreType.DMA((chips - 1,)),
        ],
        compiler_params=pltpu.CompilerParams(collective_id=collective_id, has_side_effects=True),
    )(x)


def _row_all_gather(x, axis, other_axis, chips, collective_id):
    rows, width = x.shape
    return pl.pallas_call(
        functools.partial(_row_ag_kernel, axis, other_axis, chips),
        out_shape=jax.ShapeDtypeStruct((chips, 2, rows, width), x.dtype),
        in_specs=[pl.BlockSpec(memory_space=pltpu.VMEM)],
        out_specs=pl.BlockSpec(memory_space=pltpu.VMEM),
        scratch_shapes=[
            pltpu.VMEM((rows, width), x.dtype),
            pltpu.VMEM((chips - 1, rows, width), x.dtype),
            pltpu.VMEM((chips - 1, rows, width), x.dtype),
            pltpu.SemaphoreType.DMA((chips,)),
            pltpu.SemaphoreType.DMA((chips,)),
            pltpu.SemaphoreType.DMA((chips - 1,)),
            pltpu.SemaphoreType.DMA((chips - 1,)),
        ],
        compiler_params=pltpu.CompilerParams(collective_id=collective_id, has_side_effects=True),
    )(x)


def _reduce_scatter(x, axis, other_axis, collective_id):
    n, rows, width = x.shape
    return pl.pallas_call(
        functools.partial(_rs_kernel, axis, other_axis, n),
        out_shape=jax.ShapeDtypeStruct((rows, width), x.dtype),
        in_specs=[pl.BlockSpec(memory_space=pltpu.VMEM)],
        out_specs=pl.BlockSpec(memory_space=pltpu.VMEM),
        scratch_shapes=[
            pltpu.VMEM((n - 1, rows, width), x.dtype),
            pltpu.SemaphoreType.DMA((n - 1,)),
            pltpu.SemaphoreType.DMA((n - 1,)),
        ],
        compiler_params=pltpu.CompilerParams(collective_id=collective_id, has_side_effects=True),
    )(x)


def _all_gather(x, axis, other_axis, n, collective_id):
    rows, width = x.shape
    return pl.pallas_call(
        functools.partial(_ag_kernel, axis, other_axis, n),
        out_shape=jax.ShapeDtypeStruct((n, rows, width), x.dtype),
        in_specs=[pl.BlockSpec(memory_space=pltpu.VMEM)],
        out_specs=pl.BlockSpec(memory_space=pltpu.VMEM),
        scratch_shapes=[
            pltpu.VMEM((n - 1, rows, width), x.dtype),
            pltpu.SemaphoreType.DMA((n - 1,)),
            pltpu.SemaphoreType.DMA((n - 1,)),
        ],
        compiler_params=pltpu.CompilerParams(collective_id=collective_id, has_side_effects=True),
    )(x)


def _mask_lanes(mask_ref, nb, bs, width, row=None, col=None):
    blk = lax.broadcasted_iota(jnp.int32, (1, width), 1) // bs
    keep = jnp.zeros((1, width), jnp.int32)
    for b in range(nb):
        value = mask_ref[row, b] if col is None else mask_ref[b, col]
        keep = jnp.where(blk == b, value, keep)
    return keep != 0


def _sub_blocks(nb):
    return 4 if nb % 4 == 0 else (2 if nb % 2 == 0 else 1)


def _half_blocks(nb):
    return nb // 2


def _sketch_kernel(nb, bs, sub, mask_ref, g_ref, p_ref, o_ref):
    i = pl.program_id(0)
    for h in range(sub):
        keep = _mask_lanes(mask_ref, nb, bs, p_ref.shape[1], row=i * sub + h)
        p = jnp.where(keep, p_ref[...], jnp.zeros_like(p_ref))
        o_ref[:, h * bs:(h + 1) * bs] = lax.dot_general(
            p, g_ref[h * bs:(h + 1) * bs, :], (((1,), (1,)), ((), ())), preferred_element_type=jnp.float32
        )


def _adjoint_kernel(nb, bs, sub, mask_ref, l_ref, g_ref, o_ref):
    j = pl.program_id(0)
    for h in range(sub):
        keep = _mask_lanes(mask_ref, nb, bs, l_ref.shape[1], col=j * sub + h)
        lowered = jnp.where(keep, l_ref[...], jnp.zeros_like(l_ref))
        o_ref[:, h * bs:(h + 1) * bs] = jnp.dot(
            lowered, g_ref[:, h * bs:(h + 1) * bs], preferred_element_type=jnp.float32
        )


def _sketch_partial(mask, green, probes_t):
    rb, cb = mask.shape
    bs = green.shape[0] // rb
    sub = _half_blocks(rb)
    k = probes_t.shape[0]
    return pl.pallas_call(
        functools.partial(_sketch_kernel, cb, bs, sub),
        out_shape=jax.ShapeDtypeStruct((rb // sub, k, bs * sub), jnp.float32),
        grid_spec=pltpu.PrefetchScalarGridSpec(
            num_scalar_prefetch=1,
            grid=(rb // sub,),
            in_specs=[
                pl.BlockSpec((bs * sub, green.shape[1]), lambda i, m: (i, 0)),
                pl.BlockSpec((k, green.shape[1]), lambda i, m: (0, 0)),
            ],
            out_specs=pl.BlockSpec((None, k, bs * sub), lambda i, m: (i, 0, 0)),
        ),
    )(mask, green, probes_t)


def _adjoint_partial(mask, lowered_t, green):
    rb, cb = mask.shape
    bs = green.shape[0] // rb
    sub = _sub_blocks(cb)
    k = lowered_t.shape[0]
    return pl.pallas_call(
        functools.partial(_adjoint_kernel, rb, bs, sub),
        out_shape=jax.ShapeDtypeStruct((k, green.shape[1]), jnp.float32),
        grid_spec=pltpu.PrefetchScalarGridSpec(
            num_scalar_prefetch=1,
            grid=(cb // sub,),
            in_specs=[
                pl.BlockSpec((k, green.shape[0]), lambda j, m: (0, 0)),
                pl.BlockSpec((green.shape[0], bs * sub), lambda j, m: (0, j)),
            ],
            out_specs=pl.BlockSpec((k, bs * sub), lambda j, m: (0, j)),
        ),
    )(mask, lowered_t, green)


def _ag_sketch_kernel(chips, rb, nb, bs, sub, mask_ref, x_ref, g_hbm, o_ref, g_vmem, g_sem, p_all, *scratch):
    load = pltpu.make_async_copy(g_hbm, g_vmem, g_sem.at[0])
    load.start()
    me = lax.axis_index("row")
    other = lax.axis_index("col")
    chip, core = _row_greet("row", me, other, chips)
    _ag_body("row", other, chips, chip, core, x_ref, p_all, *scratch)
    k = p_all.shape[0] * p_all.shape[1] * p_all.shape[2]
    probes_t = p_all[...].reshape(k, p_all.shape[3])
    load.wait()
    for h in range(rb):
        keep = _mask_lanes(mask_ref, nb, bs, probes_t.shape[1], row=h)
        p = jnp.where(keep, probes_t, jnp.zeros_like(probes_t))
        o_ref[h // sub, :, (h % sub) * bs:(h % sub + 1) * bs] = lax.dot_general(
            p, g_vmem[h * bs:(h + 1) * bs, :], (((1,), (1,)), ((), ())), preferred_element_type=jnp.float32
        )


def _ag_sketch(x, mask, green, chips, collective_id):
    rows, width = x.shape
    rb, cb = mask.shape
    bs = green.shape[0] // rb
    sub = _half_blocks(rb)
    k = 2 * chips * rows
    return pl.pallas_call(
        functools.partial(_ag_sketch_kernel, chips, rb, cb, bs, sub),
        out_shape=jax.ShapeDtypeStruct((rb // sub, k, bs * sub), jnp.float32),
        in_specs=[
            pl.BlockSpec(memory_space=pltpu.SMEM),
            pl.BlockSpec(memory_space=pltpu.VMEM),
            pl.BlockSpec(memory_space=pl.ANY),
        ],
        out_specs=pl.BlockSpec(memory_space=pltpu.VMEM),
        scratch_shapes=[
            pltpu.VMEM(green.shape, green.dtype),
            pltpu.SemaphoreType.DMA((1,)),
            pltpu.VMEM((chips, 2, rows, width), x.dtype),
            pltpu.VMEM((rows, width), x.dtype),
            pltpu.VMEM((chips - 1, rows, width), x.dtype),
            pltpu.VMEM((chips - 1, rows, width), x.dtype),
            pltpu.SemaphoreType.DMA((chips,)),
            pltpu.SemaphoreType.DMA((chips,)),
            pltpu.SemaphoreType.DMA((chips - 1,)),
            pltpu.SemaphoreType.DMA((chips - 1,)),
        ],
        compiler_params=pltpu.CompilerParams(collective_id=collective_id, has_side_effects=True),
    )(mask, x, green)


def local(green, mask, probes):
    n_row = lax.axis_size("row")
    n_col = lax.axis_size("col")
    sketch_t, adjoint_t = _all_reduce_adjoint(probes.T, mask, green, "col", "row", 0)
    return (sketch_t.T, adjoint_t.T)


def solution(mesh):
    in_specs = (P("row", "col"), P("row", "col"), P("col", "row"))
    out_specs = (P("row", "col"), P("col", "row"))
    return jax.shard_map(local, mesh=mesh, in_specs=in_specs, out_specs=out_specs, check_vma=False)
```

```python
import functools

import jax
import jax.numpy as jnp
from jax import lax
from jax.experimental import pallas as pl
from jax.experimental.pallas import tpu as pltpu
from jax.sharding import PartitionSpec as P

MESH = pl.DeviceIdType.MESH


def _peer(axis, other, p):
    return (other, p) if axis == "col" else (p, other)


def _greet(axis, other, me, n):
    barrier = pltpu.get_barrier_semaphore()
    for d in range(1, n):
        peer = _peer(axis, other, lax.rem(me + d, n))
        pl.semaphore_signal(barrier, 1, device_id=peer, device_id_type=MESH)
    pl.semaphore_wait(barrier, n - 1)


def _rs_kernel(axis, other_axis, n, x_ref, o_ref, recv, send_sem, recv_sem):
    me = lax.axis_index(axis)
    other = lax.axis_index(other_axis)
    _greet(axis, other, me, n)
    copies = []
    for d in range(1, n):
        peer = lax.rem(me + d, n)
        copy = pltpu.make_async_remote_copy(
            src_ref=x_ref.at[peer],
            dst_ref=recv.at[d - 1],
            send_sem=send_sem.at[d - 1],
            recv_sem=recv_sem.at[d - 1],
            device_id=_peer(axis, other, peer),
            device_id_type=MESH,
        )
        copy.start()
        copies.append(copy)
    acc = x_ref[me]
    for d, copy in enumerate(copies):
        copy.wait_recv()
        acc = acc + recv[d]
    for copy in copies:
        copy.wait_send()
    o_ref[...] = acc


def _ag_kernel(axis, other_axis, n, x_ref, o_ref, recv, send_sem, recv_sem):
    me = lax.axis_index(axis)
    other = lax.axis_index(other_axis)
    _greet(axis, other, me, n)
    copies = []
    for d in range(1, n):
        peer = lax.rem(me + d, n)
        copy = pltpu.make_async_remote_copy(
            src_ref=x_ref,
            dst_ref=recv.at[d - 1],
            send_sem=send_sem.at[d - 1],
            recv_sem=recv_sem.at[d - 1],
            device_id=_peer(axis, other, peer),
            device_id_type=MESH,
        )
        copy.start()
        copies.append(copy)
    o_ref[me] = x_ref[...]
    for d, copy in enumerate(copies):
        copy.wait_recv()
        o_ref[lax.rem(me + n - 1 - d, n)] = recv[d]
    for copy in copies:
        copy.wait_send()


def _row_greet(axis, me, other, chips):
    chip, core = me // 2, lax.rem(me, 2)
    barrier = pltpu.get_barrier_semaphore()
    pl.semaphore_signal(barrier, 1, device_id=_peer(axis, other, chip * 2 + 1 - core), device_id_type=MESH)
    for d in range(1, chips):
        peer = lax.rem(chip + d, chips) * 2 + core
        pl.semaphore_signal(barrier, 1, device_id=_peer(axis, other, peer), device_id_type=MESH)
    pl.semaphore_wait(barrier, chips)
    return chip, core


def _row_rs_kernel(axis, other_axis, chips, x_ref, o_ref, recv1, mid, recv2, s1, r1, s2, r2):
    me = lax.axis_index(axis)
    other = lax.axis_index(other_axis)
    chip, core = _row_greet(axis, me, other, chips)
    _rs_body(axis, other, chips, chip, core, x_ref, o_ref, recv1, mid, recv2, s1, r1, s2, r2)


def _rs_body(axis, other, chips, chip, core, x_ref, o_ref, recv1, mid, recv2, s1, r1, s2, r2):
    sib = _peer(axis, other, chip * 2 + 1 - core)
    first = []
    for d in list(range(1, chips)) + [0]:
        target = lax.rem(chip + d, chips)
        copy = pltpu.make_async_remote_copy(
            src_ref=x_ref.at[target, 1 - core],
            dst_ref=recv1.at[d],
            send_sem=s1.at[d],
            recv_sem=r1.at[d],
            device_id=sib,
            device_id_type=MESH,
        )
        copy.start()
        first.append(copy)
    sends = []
    for d in range(1, chips):
        target = lax.rem(chip + d, chips)
        first[d - 1].wait_recv()
        mid[d - 1] = x_ref[target, core] + recv1[d]
        copy = pltpu.make_async_remote_copy(
            src_ref=mid.at[d - 1],
            dst_ref=recv2.at[d - 1],
            send_sem=s2.at[d - 1],
            recv_sem=r2.at[d - 1],
            device_id=_peer(axis, other, target * 2 + core),
            device_id_type=MESH,
        )
        copy.start()
        sends.append(copy)
    first[chips - 1].wait_recv()
    acc = x_ref[chip, core] + recv1[0]
    for d, copy in enumerate(sends):
        copy.wait_recv()
        acc = acc + recv2[d]
    for copy in first + sends:
        copy.wait_send()
    o_ref[...] = acc


def _row_ag_kernel(axis, other_axis, chips, x_ref, o_ref, recv_s, recv_a, recv_f, s1, r1, s2, r2):
    me = lax.axis_index(axis)
    other = lax.axis_index(other_axis)
    chip, core = _row_greet(axis, me, other, chips)
    _ag_body(axis, other, chips, chip, core, x_ref, o_ref, recv_s, recv_a, recv_f, s1, r1, s2, r2)


def _ag_body(axis, other, chips, chip, core, x_ref, o_ref, recv_s, recv_a, recv_f, s1, r1, s2, r2):
    sib = _peer(axis, other, chip * 2 + 1 - core)
    to_sib = pltpu.make_async_remote_copy(
        src_ref=x_ref, dst_ref=recv_s, send_sem=s1.at[0], recv_sem=r1.at[0],
        device_id=sib, device_id_type=MESH,
    )
    to_sib.start()
    first = [to_sib]
    for d in range(1, chips):
        peer = lax.rem(chip + d, chips) * 2 + core
        copy = pltpu.make_async_remote_copy(
            src_ref=x_ref, dst_ref=recv_a.at[d - 1], send_sem=s1.at[d], recv_sem=r1.at[d],
            device_id=_peer(axis, other, peer), device_id_type=MESH,
        )
        copy.start()
        first.append(copy)
    o_ref[chip, core] = x_ref[...]
    forwards = []
    for d in range(1, chips):
        first[d].wait_recv()
        copy = pltpu.make_async_remote_copy(
            src_ref=recv_a.at[d - 1], dst_ref=recv_f.at[d - 1], send_sem=s2.at[d - 1],
            recv_sem=r2.at[d - 1], device_id=sib, device_id_type=MESH,
        )
        copy.start()
        forwards.append(copy)
        o_ref[lax.rem(chip + chips - d, chips), core] = recv_a[d - 1]
    to_sib.wait_recv()
    o_ref[chip, 1 - core] = recv_s[...]
    for d, copy in enumerate(forwards):
        copy.wait_recv()
        o_ref[lax.rem(chip + chips - 1 - d, chips), 1 - core] = recv_f[d]
    for copy in first + forwards:
        copy.wait_send()


def _mixed_rs_body(axis, other, chips, chip, core, x_ref, o_ref, ra1, ma, ra2, rb1, mb, rb2,
                   sa1, qa1, sa2, qa2, sb1, qb1, sb2, qb2, between=None):
    sib = _peer(axis, other, chip * 2 + 1 - core)
    width = x_ref.shape[-1]
    b1 = []
    for d in range(1, chips):
        target = lax.rem(chip + d, chips)
        for half, bit in enumerate((core, 1 - core)):
            copy = pltpu.make_async_remote_copy(
                src_ref=x_ref.at[1, target * 2 + bit], dst_ref=rb1.at[d - 1, half],
                send_sem=sb1.at[d - 1, half], recv_sem=qb1.at[d - 1, half],
                device_id=_peer(axis, other, target * 2 + core), device_id_type=MESH,
            )
            copy.start()
            b1.append(copy)
    if between is not None:
        between()
    a1 = []
    for d in list(range(1, chips)) + [0]:
        target = lax.rem(chip + d, chips)
        copy = pltpu.make_async_remote_copy(
            src_ref=x_ref.at[0, target * 2 + 1 - core], dst_ref=ra1.at[d], send_sem=sa1.at[d],
            recv_sem=qa1.at[d], device_id=sib, device_id_type=MESH,
        )
        copy.start()
        a1.append(copy)
    a2 = []
    for d in range(1, chips):
        target = lax.rem(chip + d, chips)
        a1[d - 1].wait_recv()
        ma[d - 1] = x_ref[0, target * 2 + core] + ra1[d]
        copy = pltpu.make_async_remote_copy(
            src_ref=ma.at[d - 1], dst_ref=ra2.at[d - 1], send_sem=sa2.at[d - 1],
            recv_sem=qa2.at[d - 1], device_id=_peer(axis, other, target * 2 + core),
            device_id_type=MESH,
        )
        copy.start()
        a2.append(copy)
    for copy in b1:
        copy.wait_recv()
    part = x_ref[1, chip * 2 + 1 - core]
    for d in range(chips - 1):
        part = part + rb1[d, 1]
    mb[...] = part
    b2 = pltpu.make_async_remote_copy(
        src_ref=mb, dst_ref=rb2, send_sem=sb2.at[0], recv_sem=qb2.at[0],
        device_id=sib, device_id_type=MESH,
    )
    b2.start()
    acc_b = x_ref[1, chip * 2 + core]
    for d in range(chips - 1):
        acc_b = acc_b + rb1[d, 0]
    a1[chips - 1].wait_recv()
    acc_a = x_ref[0, chip * 2 + core] + ra1[0]
    for d, copy in enumerate(a2):
        copy.wait_recv()
        acc_a = acc_a + ra2[d]
    b2.wait_recv()
    o_ref[:, :width] = acc_a
    o_ref[:, width:] = acc_b + rb2[...]
    for copy in a1 + b1 + a2 + [b2]:
        copy.wait_send()


def _ar_kernel(axis, other_axis, chips, row_chips, rb, cb, bs, mask_ref, p_ref, g_hbm, o_ref, a_ref,
               g_vmem, g_sem, l_all, low, t_ref, x_ref, p_all, *scratch):
    row_scratch = scratch[21:28]
    load = pltpu.make_async_copy(g_hbm, g_vmem, g_sem.at[0])
    load.start()
    me = lax.axis_index(axis)
    other = lax.axis_index(other_axis)
    chip, core = me // 2, lax.rem(me, 2)
    row_chip, row_core = other // 2, lax.rem(other, 2)
    barrier = pltpu.get_barrier_semaphore()
    for ax, mine, group, bit, count in ((axis, other, chip, core, chips), (other_axis, me, row_chip, row_core, row_chips)):
        pl.semaphore_signal(barrier, 1, device_id=_peer(ax, mine, group * 2 + 1 - bit), device_id_type=MESH)
        for d in range(1, count):
            peer = lax.rem(group + d, count) * 2 + bit
            pl.semaphore_signal(barrier, 1, device_id=_peer(ax, mine, peer), device_id_type=MESH)
    pl.semaphore_wait(barrier, chips + row_chips)
    _ag_body(other_axis, me, row_chips, row_chip, row_core, p_ref, p_all, *scratch[28:])
    k = p_all.shape[0] * p_all.shape[1] * p_all.shape[2]
    probes_t = p_all[...].reshape(k, p_all.shape[3])
    load.wait()
    sub = x_ref.shape[-1] // bs

    def sketch(step):
        for h in range(step * sub, (step + 1) * sub):
            keep = _mask_lanes(mask_ref, cb, bs, probes_t.shape[1], row=h)
            p = jnp.where(keep, probes_t, jnp.zeros_like(probes_t))
            x_ref[step, :, :, (h % sub) * bs:(h % sub + 1) * bs] = lax.dot_general(
                p, g_vmem[h * bs:(h + 1) * bs, :], (((1,), (1,)), ((), ())), preferred_element_type=jnp.float32
            ).reshape(x_ref.shape[1], x_ref.shape[2], bs)

    sketch(1)
    _mixed_rs_body(axis, other, chips, chip, core, x_ref, o_ref, *scratch[:14], between=lambda: sketch(0))
    low[...] = o_ref[...].astype(low.dtype)
    _ag_body(axis, other, chips, chip, core, low, l_all, *scratch[14:21])
    k = l_all.shape[0] * l_all.shape[1] * l_all.shape[2]
    lowered = l_all[...].reshape(k, l_all.shape[3])
    for j in range(cb):
        keep = _mask_lanes(mask_ref, rb, bs, lowered.shape[1], col=j)
        masked = jnp.where(keep, lowered, jnp.zeros_like(lowered))
        t_ref[:, :, :, j * bs:(j + 1) * bs] = jnp.dot(
            masked, g_vmem[:, j * bs:(j + 1) * bs], preferred_element_type=jnp.float32
        ).reshape(t_ref.shape[0], 2, t_ref.shape[2], bs)
    _rs_body(other_axis, me, row_chips, row_chip, row_core, t_ref, a_ref, *row_scratch)


def _all_reduce_adjoint(probes_t, mask, green, axis, other_axis, collective_id):
    n = lax.axis_size(axis)
    rows = probes_t.shape[0] * lax.axis_size(other_axis) // n
    half = green.shape[0] // 2
    x = jax.ShapeDtypeStruct((2, n, rows, half), jnp.float32)
    chips = n // 2
    width = 2 * half
    low = jnp.bfloat16
    rb, cb = mask.shape
    bs = green.shape[0] // rb
    row_chips = lax.axis_size(other_axis) // 2
    k_rows = n * rows // (2 * row_chips)
    cols = green.shape[1]
    return pl.pallas_call(
        functools.partial(_ar_kernel, axis, other_axis, chips, row_chips, rb, cb, bs),
        out_shape=(
            jax.ShapeDtypeStruct((rows, width), jnp.float32),
            jax.ShapeDtypeStruct((k_rows, cols), jnp.float32),
        ),
        in_specs=[
            pl.BlockSpec(memory_space=pltpu.SMEM),
            pl.BlockSpec(memory_space=pltpu.VMEM),
            pl.BlockSpec(memory_space=pl.ANY),
        ],
        out_specs=(pl.BlockSpec(memory_space=pltpu.VMEM), pl.BlockSpec(memory_space=pltpu.VMEM)),
        scratch_shapes=[
            pltpu.VMEM(green.shape, green.dtype),
            pltpu.SemaphoreType.DMA((1,)),
            pltpu.VMEM((chips, 2, rows, width), low),
            pltpu.VMEM((rows, width), low),
            pltpu.VMEM((row_chips, 2, k_rows, cols), jnp.float32),
            pltpu.VMEM((2, n, rows, half), jnp.float32),
            pltpu.VMEM((row_chips, 2) + probes_t.shape, probes_t.dtype),
            pltpu.VMEM((chips, rows, half), x.dtype),
            pltpu.VMEM((chips - 1, rows, half), x.dtype),
            pltpu.VMEM((chips - 1, rows, half), x.dtype),
            pltpu.VMEM((chips - 1, 2, rows, half), x.dtype),
            pltpu.VMEM((rows, half), x.dtype),
            pltpu.VMEM((rows, half), x.dtype),
            pltpu.SemaphoreType.DMA((chips,)),
            pltpu.SemaphoreType.DMA((chips,)),
            pltpu.SemaphoreType.DMA((chips - 1,)),
            pltpu.SemaphoreType.DMA((chips - 1,)),
            pltpu.SemaphoreType.DMA((chips - 1, 2)),
            pltpu.SemaphoreType.DMA((chips - 1, 2)),
            pltpu.SemaphoreType.DMA((1,)),
            pltpu.SemaphoreType.DMA((1,)),
            pltpu.VMEM((rows, width), low),
            pltpu.VMEM((chips - 1, rows, width), low),
            pltpu.VMEM((chips - 1, rows, width), low),
            pltpu.SemaphoreType.DMA((chips,)),
            pltpu.SemaphoreType.DMA((chips,)),
            pltpu.SemaphoreType.DMA((chips - 1,)),
            pltpu.SemaphoreType.DMA((chips - 1,)),
            pltpu.VMEM((row_chips, k_rows, cols), jnp.float32),
            pltpu.VMEM((row_chips - 1, k_rows, cols), jnp.float32),
            pltpu.VMEM((row_chips - 1, k_rows, cols), jnp.float32),
            pltpu.SemaphoreType.DMA((row_chips,)),
            pltpu.SemaphoreType.DMA((row_chips,)),
            pltpu.SemaphoreType.DMA((row_chips - 1,)),
            pltpu.SemaphoreType.DMA((row_chips - 1,)),
            pltpu.VMEM(probes_t.shape, probes_t.dtype),
            pltpu.VMEM((row_chips - 1,) + probes_t.shape, probes_t.dtype),
            pltpu.VMEM((row_chips - 1,) + probes_t.shape, probes_t.dtype),
            pltpu.SemaphoreType.DMA((row_chips,)),
            pltpu.SemaphoreType.DMA((row_chips,)),
            pltpu.SemaphoreType.DMA((row_chips - 1,)),
            pltpu.SemaphoreType.DMA((row_chips - 1,)),
        ],
        compiler_params=pltpu.CompilerParams(collective_id=collective_id, has_side_effects=True),
    )(mask, probes_t, green)


def _row_reduce_scatter(x, axis, other_axis, collective_id):
    chips, _, rows, width = x.shape
    return pl.pallas_call(
        functools.partial(_row_rs_kernel, axis, other_axis, chips),
        out_shape=jax.ShapeDtypeStruct((rows, width), x.dtype),
        in_specs=[pl.BlockSpec(memory_space=pltpu.VMEM)],
        out_specs=pl.BlockSpec(memory_space=pltpu.VMEM),
        scratch_shapes=[
            pltpu.VMEM((chips, rows, width), x.dtype),
            pltpu.VMEM((chips - 1, rows, width), x.dtype),
            pltpu.VMEM((chips - 1, rows, width), x.dtype),
            pltpu.SemaphoreType.DMA((chips,)),
            pltpu.SemaphoreType.DMA((chips,)),
            pltpu.SemaphoreType.DMA((chips - 1,)),
            pltpu.SemaphoreType.DMA((chips - 1,)),
        ],
        compiler_params=pltpu.CompilerParams(collective_id=collective_id, has_side_effects=True),
    )(x)


def _row_all_gather(x, axis, other_axis, chips, collective_id):
    rows, width = x.shape
    return pl.pallas_call(
        functools.partial(_row_ag_kernel, axis, other_axis, chips),
        out_shape=jax.ShapeDtypeStruct((chips, 2, rows, width), x.dtype),
        in_specs=[pl.BlockSpec(memory_space=pltpu.VMEM)],
        out_specs=pl.BlockSpec(memory_space=pltpu.VMEM),
        scratch_shapes=[
            pltpu.VMEM((rows, width), x.dtype),
            pltpu.VMEM((chips - 1, rows, width), x.dtype),
            pltpu.VMEM((chips - 1, rows, width), x.dtype),
            pltpu.SemaphoreType.DMA((chips,)),
            pltpu.SemaphoreType.DMA((chips,)),
            pltpu.SemaphoreType.DMA((chips - 1,)),
            pltpu.SemaphoreType.DMA((chips - 1,)),
        ],
        compiler_params=pltpu.CompilerParams(collective_id=collective_id, has_side_effects=True),
    )(x)


def _reduce_scatter(x, axis, other_axis, collective_id):
    n, rows, width = x.shape
    return pl.pallas_call(
        functools.partial(_rs_kernel, axis, other_axis, n),
        out_shape=jax.ShapeDtypeStruct((rows, width), x.dtype),
        in_specs=[pl.BlockSpec(memory_space=pltpu.VMEM)],
        out_specs=pl.BlockSpec(memory_space=pltpu.VMEM),
        scratch_shapes=[
            pltpu.VMEM((n - 1, rows, width), x.dtype),
            pltpu.SemaphoreType.DMA((n - 1,)),
            pltpu.SemaphoreType.DMA((n - 1,)),
        ],
        compiler_params=pltpu.CompilerParams(collective_id=collective_id, has_side_effects=True),
    )(x)


def _all_gather(x, axis, other_axis, n, collective_id):
    rows, width = x.shape
    return pl.pallas_call(
        functools.partial(_ag_kernel, axis, other_axis, n),
        out_shape=jax.ShapeDtypeStruct((n, rows, width), x.dtype),
        in_specs=[pl.BlockSpec(memory_space=pltpu.VMEM)],
        out_specs=pl.BlockSpec(memory_space=pltpu.VMEM),
        scratch_shapes=[
            pltpu.VMEM((n - 1, rows, width), x.dtype),
            pltpu.SemaphoreType.DMA((n - 1,)),
            pltpu.SemaphoreType.DMA((n - 1,)),
        ],
        compiler_params=pltpu.CompilerParams(collective_id=collective_id, has_side_effects=True),
    )(x)


def _mask_lanes(mask_ref, nb, bs, width, row=None, col=None):
    blk = lax.broadcasted_iota(jnp.int32, (1, width), 1) // bs
    keep = jnp.zeros((1, width), jnp.int32)
    for b in range(nb):
        value = mask_ref[row, b] if col is None else mask_ref[b, col]
        keep = jnp.where(blk == b, value, keep)
    return keep != 0


def _sub_blocks(nb):
    return 4 if nb % 4 == 0 else (2 if nb % 2 == 0 else 1)


def _half_blocks(nb):
    return nb // 2


def _sketch_kernel(nb, bs, sub, mask_ref, g_ref, p_ref, o_ref):
    i = pl.program_id(0)
    for h in range(sub):
        keep = _mask_lanes(mask_ref, nb, bs, p_ref.shape[1], row=i * sub + h)
        p = jnp.where(keep, p_ref[...], jnp.zeros_like(p_ref))
        o_ref[:, h * bs:(h + 1) * bs] = lax.dot_general(
            p, g_ref[h * bs:(h + 1) * bs, :], (((1,), (1,)), ((), ())), preferred_element_type=jnp.float32
        )


def _adjoint_kernel(nb, bs, sub, mask_ref, l_ref, g_ref, o_ref):
    j = pl.program_id(0)
    for h in range(sub):
        keep = _mask_lanes(mask_ref, nb, bs, l_ref.shape[1], col=j * sub + h)
        lowered = jnp.where(keep, l_ref[...], jnp.zeros_like(l_ref))
        o_ref[:, h * bs:(h + 1) * bs] = jnp.dot(
            lowered, g_ref[:, h * bs:(h + 1) * bs], preferred_element_type=jnp.float32
        )


def _sketch_partial(mask, green, probes_t):
    rb, cb = mask.shape
    bs = green.shape[0] // rb
    sub = _half_blocks(rb)
    k = probes_t.shape[0]
    return pl.pallas_call(
        functools.partial(_sketch_kernel, cb, bs, sub),
        out_shape=jax.ShapeDtypeStruct((rb // sub, k, bs * sub), jnp.float32),
        grid_spec=pltpu.PrefetchScalarGridSpec(
            num_scalar_prefetch=1,
            grid=(rb // sub,),
            in_specs=[
                pl.BlockSpec((bs * sub, green.shape[1]), lambda i, m: (i, 0)),
                pl.BlockSpec((k, green.shape[1]), lambda i, m: (0, 0)),
            ],
            out_specs=pl.BlockSpec((None, k, bs * sub), lambda i, m: (i, 0, 0)),
        ),
    )(mask, green, probes_t)


def _adjoint_partial(mask, lowered_t, green):
    rb, cb = mask.shape
    bs = green.shape[0] // rb
    sub = _sub_blocks(cb)
    k = lowered_t.shape[0]
    return pl.pallas_call(
        functools.partial(_adjoint_kernel, rb, bs, sub),
        out_shape=jax.ShapeDtypeStruct((k, green.shape[1]), jnp.float32),
        grid_spec=pltpu.PrefetchScalarGridSpec(
            num_scalar_prefetch=1,
            grid=(cb // sub,),
            in_specs=[
                pl.BlockSpec((k, green.shape[0]), lambda j, m: (0, 0)),
                pl.BlockSpec((green.shape[0], bs * sub), lambda j, m: (0, j)),
            ],
            out_specs=pl.BlockSpec((k, bs * sub), lambda j, m: (0, j)),
        ),
    )(mask, lowered_t, green)


def _ag_sketch_kernel(chips, rb, nb, bs, sub, mask_ref, x_ref, g_hbm, o_ref, g_vmem, g_sem, p_all, *scratch):
    load = pltpu.make_async_copy(g_hbm, g_vmem, g_sem.at[0])
    load.start()
    me = lax.axis_index("row")
    other = lax.axis_index("col")
    chip, core = _row_greet("row", me, other, chips)
    _ag_body("row", other, chips, chip, core, x_ref, p_all, *scratch)
    k = p_all.shape[0] * p_all.shape[1] * p_all.shape[2]
    probes_t = p_all[...].reshape(k, p_all.shape[3])
    load.wait()
    for h in range(rb):
        keep = _mask_lanes(mask_ref, nb, bs, probes_t.shape[1], row=h)
        p = jnp.where(keep, probes_t, jnp.zeros_like(probes_t))
        o_ref[h // sub, :, (h % sub) * bs:(h % sub + 1) * bs] = lax.dot_general(
            p, g_vmem[h * bs:(h + 1) * bs, :], (((1,), (1,)), ((), ())), preferred_element_type=jnp.float32
        )


def _ag_sketch(x, mask, green, chips, collective_id):
    rows, width = x.shape
    rb, cb = mask.shape
    bs = green.shape[0] // rb
    sub = _half_blocks(rb)
    k = 2 * chips * rows
    return pl.pallas_call(
        functools.partial(_ag_sketch_kernel, chips, rb, cb, bs, sub),
        out_shape=jax.ShapeDtypeStruct((rb // sub, k, bs * sub), jnp.float32),
        in_specs=[
            pl.BlockSpec(memory_space=pltpu.SMEM),
            pl.BlockSpec(memory_space=pltpu.VMEM),
            pl.BlockSpec(memory_space=pl.ANY),
        ],
        out_specs=pl.BlockSpec(memory_space=pltpu.VMEM),
        scratch_shapes=[
            pltpu.VMEM(green.shape, green.dtype),
            pltpu.SemaphoreType.DMA((1,)),
            pltpu.VMEM((chips, 2, rows, width), x.dtype),
            pltpu.VMEM((rows, width), x.dtype),
            pltpu.VMEM((chips - 1, rows, width), x.dtype),
            pltpu.VMEM((chips - 1, rows, width), x.dtype),
            pltpu.SemaphoreType.DMA((chips,)),
            pltpu.SemaphoreType.DMA((chips,)),
            pltpu.SemaphoreType.DMA((chips - 1,)),
            pltpu.SemaphoreType.DMA((chips - 1,)),
        ],
        compiler_params=pltpu.CompilerParams(collective_id=collective_id, has_side_effects=True),
    )(mask, x, green)


def local(green, mask, probes):
    n_row = lax.axis_size("row")
    n_col = lax.axis_size("col")
    sketch_t, adjoint_t = _all_reduce_adjoint(probes.T, mask, green, "col", "row", 0)
    return (sketch_t.T, adjoint_t.T)


def solution(mesh):
    in_specs = (P("row", "col"), P("row", "col"), P("col", "row"))
    out_specs = (P("row", "col"), P("col", "row"))
    return jax.shard_map(local, mesh=mesh, in_specs=in_specs, out_specs=out_specs, check_vma=False)
```
